32 devices in a mesh: blk: 4 (over y, x), row: 8 (over z, core).
Axes of the slice: x: 2, y: 2, z: 4, core: 2. Of those that a mesh axis runs over, the one named last changes fastest.
Arguments:
- inputs: float32 [16384, 512], P('row', 'blk'), may hold values from -30 to 30
- seq_lengths: int32 [8, 3], P('row'), may hold values from 1 to 1024, 2048 in all within a row
- poles: float32 [2, 2, 384], P(None, None, 'blk'), may hold values from -4 to 4, as said below
- log_step: float32 [2, 384], P(None, 'blk'), may hold values from -6.9 to -2.3
- in_matrix: float32 [2, 2, 384, 512], P(None, None, 'blk'), may hold values from -0.25 to 0.25
- out_matrix: float32 [2, 2, 384, 512], P(None, None, 'blk'), may hold values from -0.21875 to 0.21875
- feedthrough: float32 [2, 512], P(None, 'blk'), may hold values from -4 to 4
- norm_gain: float32 [2, 512], P(None, 'blk'), may hold values from 0.5 to 1.5
- norm_bias: float32 [2, 512], P(None, 'blk'), may hold values from -3 to 3
- cotangent: float32 [16384, 512], P('row', 'blk'), may hold values from -6 to 6
Outputs:
- outputs: float32 [16384, 512], P('row', 'blk')
- grad_inputs: float32 [16384, 512], P('row', 'blk')
- grad_poles: float32 [2, 2, 384], P(None, None, 'blk')
- grad_log_step: float32 [2, 384], P(None, 'blk')
- grad_in_matrix: float32 [2, 2, 384, 512], P(None, None, 'blk')
- grad_out_matrix: float32 [2, 2, 384, 512], P(None, None, 'blk')
- grad_feedthrough: float32 [2, 512], P(None, 'blk')
- grad_norm_gain: float32 [2, 512], P(None, 'blk')
- grad_norm_bias: float32 [2, 512], P(None, 'blk')
The draws below stay inside these ranges and needn't reach their ends.
Inputs may be any that keep to these rules, and one draw needn't show every extreme that they name: `seq_lengths`: each packed row holds 3 sequences whose lengths sum to 2048; the longest of each row has exactly 1024 tokens. `poles`: the real parts are negative.
All inputs are finite; a program needn't handle non-finite values.
Results may differ from the reference program's by a relative error of at most 0.0003.
Values sent between devices are 32-bit elements; how exact they have to be, the bound alone decides.
A program may use at most 128 MiB of HBM per device.

```python
import math
import jax
import jax.numpy as jnp
import numpy as np
from jax import lax

H = 512
P_SIZE = 384
LAYERS = 2
SEQS = 3
ROW_LEN = 2048
PACKS = 8
TOKENS = 16384
LONGEST = 1024


def draw_inputs(key, part):
    subkeys = jax.random.split(key, 3)
    row_count = TOKENS // ROW_LEN
    row_fraction = (jnp.arange(TOKENS) // ROW_LEN).astype(jnp.float32) / max(row_count - 1, 1)
    offset = jax.random.uniform(subkeys[0], (H,), jnp.float32, -1.0, 1.0)
    spread = jnp.exp(jax.random.uniform(subkeys[1], (H,), jnp.float32, math.log(0.5), math.log(2.0)))
    noise_values = jnp.clip(jax.random.normal(subkeys[2], (TOKENS, H), jnp.float32), -4.0, 4.0)
    row_scale = jnp.exp(math.log(3.0) * row_fraction)
    return (offset[None, :] + noise_values) * spread[None, :] * row_scale[:, None]


def draw_poles(key, part):
    subkeys = jax.random.split(key, 2)
    real_part = -jax.random.uniform(subkeys[0], (LAYERS, 1, P_SIZE), jnp.float32, 0.25, 0.75)
    imag_part = jax.random.uniform(subkeys[1], (LAYERS, 1, P_SIZE), jnp.float32, -4.0, 4.0)
    return jnp.concatenate([real_part, imag_part], axis=1)


def levels(own_key, dims, shards, least, high):
    def one(position, blocks):
        heights = jax.random.uniform(jax.random.fold_in(jax.random.fold_in(own_key, 6), position), (blocks,), jnp.float32, least / len(shards), high / len(shards))
        return jnp.repeat(jnp.exp(heights), dims[position] // blocks).reshape((-1,) + (1,) * (len(dims) - position - 1))

    loudness = one(*shards[0])
    for cut in shards[1:]:
        loudness = loudness * one(*cut)
    return loudness


def length_profile(amount, total, limit, lean):
    loads = [(1 << 20) // math.isqrt(rank ** lean) + 1 for rank in range(2, amount + 1)]
    spare, given = total - limit - (amount - 1), [1] * (amount - 1)
    while spare > 0:
        candidates = [i for i in range(amount - 1) if given[i] < limit]
        whole, remaining = sum([loads[i] for i in candidates]), spare
        for i in candidates:
            more = min(limit - given[i], max(1, remaining * loads[i] // whole), spare)
            given[i] = given[i] + more
            spare = spare - more
    return np.array([limit] + given)


def ragged(rng, number_of, total, limit, skew):
    if number_of == 2:
        one = jax.random.randint(rng, (), max(1, total - limit), min(limit, total - 1) + 1)
        return jnp.stack([one, total - one])
    lengths = jnp.asarray(length_profile(number_of, total, limit, skew), jnp.int32)
    couples = (number_of - 1) // 2
    donor, sink = lengths[1:1 + 2 * couples:2], lengths[2:2 + 2 * couples:2]
    slack = jnp.minimum(donor - 1, limit - sink)
    shifted = jax.random.randint(jax.random.fold_in(rng, 1), (couples,), 0, 1 << 20) % (slack + 1)
    lengths = lengths.at[1:1 + 2 * couples:2].set(donor - shifted).at[2:2 + 2 * couples:2].set(sink + shifted)
    return lengths[jax.random.permutation(jax.random.fold_in(rng, 2), number_of)]


def scatter_about(key, extent, width, bound, cuts=(), kind=jnp.bfloat16):
    loudness = levels(key, extent, cuts, -0.22, 0.18) if cuts else 1.0
    array = jax.random.normal(key, extent, jnp.float32) * width * loudness
    return jnp.minimum(jnp.maximum(array, -bound), bound).astype(kind)


def setup_inputs(seed: int = 0) -> dict:
    seeds = jax.random.split(jax.random.key(seed), 11)
    inputs = draw_inputs(jax.random.fold_in(seeds[10], 71), 0)
    seq_lengths = jax.vmap(lambda own: ragged(own, SEQS, ROW_LEN, LONGEST, 2))(jax.random.split(seeds[1], PACKS)).reshape((PACKS, SEQS)).astype(jnp.int32)
    poles = draw_poles(jax.random.fold_in(seeds[10], 71), 0)
    log_step = jnp.clip(-6.9 + 4.6000001430511475 * jax.random.uniform(seeds[3], (LAYERS, P_SIZE), jnp.float32) ** levels(seeds[3], (LAYERS, P_SIZE), ((1, 4),), -0.2, 0.2), -6.9, -2.3)
    in_matrix = scatter_about(seeds[4], (LAYERS, 2, P_SIZE, H), H ** -0.5, 0.25, ((2, 4),), jnp.float32)
    out_matrix = scatter_about(seeds[5], (LAYERS, 2, P_SIZE, H), (2 * P_SIZE) ** -0.5, 0.21875, ((2, 4),), jnp.float32)
    feedthrough = scatter_about(seeds[6], (LAYERS, H), 1.0, 4.0, ((1, 4),), jnp.float32)
    norm_gain = jnp.clip(1.0 + 0.1 * jax.random.normal(seeds[7], (LAYERS, H), jnp.float32), 0.5, 1.5)
    norm_bias = scatter_about(seeds[8], (LAYERS, H), 0.5, 3.0, ((1, 4),), jnp.float32)
    cotangent = scatter_about(seeds[9], (TOKENS, H), 1.0, 6.0, ((0, 8), (1, 4)), jnp.float32)
    return dict(inputs=inputs, seq_lengths=seq_lengths, poles=poles, log_step=log_step, in_matrix=in_matrix, out_matrix=out_matrix, feedthrough=feedthrough, norm_gain=norm_gain, norm_bias=norm_bias, cotangent=cotangent)


EPSILON = 1e-05
PRECISE = lax.Precision.HIGHEST

@jax.custom_vjp
def low(v):
    return lax.optimization_barrier(v.astype(jnp.bfloat16)).astype(jnp.float32)

@jax.custom_vjp
def low_back(v):
    return v

def low_keep(v):
    return (low(v), None)

def low_pass(kept, grad):
    return (grad,)

def back_keep(v):
    return (v, None)

def back_low(kept, grad):
    return (low(grad),)
low.defvjp(low_keep, low_pass)
low_back.defvjp(back_keep, back_low)

def discretize(pole_parts, log_steps, in_parts):
    step_sizes = jnp.exp(log_steps)
    decay_real = pole_parts[0] * step_sizes
    turn_imag = pole_parts[1] * step_sizes
    magnitude = jnp.exp(decay_real)
    lbar_real = magnitude * jnp.cos(turn_imag)
    lbar_imag = magnitude * jnp.sin(turn_imag)
    modulus = pole_parts[0] * pole_parts[0] + pole_parts[1] * pole_parts[1]
    factor_real = ((lbar_real - 1.0) * pole_parts[0] + lbar_imag * pole_parts[1]) / modulus
    factor_imag = (lbar_imag * pole_parts[0] - (lbar_real - 1.0) * pole_parts[1]) / modulus
    drive_real = factor_real[:, None] * in_parts[0] - factor_imag[:, None] * in_parts[1]
    drive_imag = factor_real[:, None] * in_parts[1] + factor_imag[:, None] * in_parts[0]
    return (lbar_real, lbar_imag, jnp.concatenate([drive_real, drive_imag], axis=0))

def compose(earlier, later):
    return (later[0] * earlier[0] - later[1] * earlier[1], later[0] * earlier[1] + later[1] * earlier[0], later[0] * earlier[2] - later[1] * earlier[3] + later[2], later[0] * earlier[3] + later[1] * earlier[2] + later[3])

def linear_scan(keep_flags, coef_real, coef_imag, drive_real, drive_imag, backward):
    gates_real = keep_flags[:, None] * coef_real[None, :]
    gates_imag = keep_flags[:, None] * coef_imag[None, :]
    result = lax.associative_scan(compose, (gates_real, gates_imag, drive_real, drive_imag), reverse=backward, axis=0)
    return (result[2], result[3])

def boundary_flags(seq_lengths, row_tokens):
    seq_ends = jnp.cumsum(seq_lengths, axis=1).astype(jnp.int32)
    begins = (seq_ends - seq_lengths).astype(jnp.int32)
    positions = jnp.arange(row_tokens, dtype=jnp.int32)
    matches = positions[None, :, None] == begins[:, None, :]
    return jnp.any(matches, axis=2).astype(jnp.float32)

def residual_layer(hidden, pole_parts, log_steps, in_parts, out_parts, feed_gain, norm_scale, norm_shift, keep_flags, backward, row_count):
    feature_mean = lax.optimization_barrier(jnp.mean(hidden, axis=0))
    feature_square = lax.optimization_barrier(jnp.mean(hidden * hidden, axis=0))
    inv_scale = lax.rsqrt(feature_square - feature_mean * feature_mean + EPSILON)
    normed = norm_scale * ((hidden - feature_mean) * inv_scale) + norm_shift
    lbar_real, lbar_imag, drive_matrix = discretize(pole_parts, log_steps, in_parts)
    state_count = lbar_real.shape[0]
    mixing = jnp.concatenate([2.0 * out_parts[0], -2.0 * out_parts[1]], axis=0)

    def one_row(row_args):
        normed_row, keep_row = row_args
        drive_terms = jnp.dot(normed_row, drive_matrix.T, precision=PRECISE, preferred_element_type=jnp.float32)
        state_real, state_imag = linear_scan(keep_row, lbar_real, lbar_imag, drive_terms[:, :state_count], drive_terms[:, state_count:], backward)
        states = jnp.concatenate([state_real, state_imag], axis=1)
        return jnp.dot(states, mixing, precision=PRECISE, preferred_element_type=jnp.float32)
    feature_count = hidden.shape[1]
    mixed_out = lax.map(jax.checkpoint(one_row), (normed.reshape(row_count, -1, feature_count), keep_flags))
    mixed_out = mixed_out.reshape(-1, feature_count) + feed_gain * normed
    return hidden + jax.nn.gelu(mixed_out, approximate=False) * jax.nn.sigmoid(mixed_out)

def reference(inputs, seq_lengths, poles, log_step, in_matrix, out_matrix, feedthrough, norm_gain, norm_bias, cotangent):
    row_count = seq_lengths.shape[0]
    row_tokens = inputs.shape[0] // row_count
    start_flags = boundary_flags(seq_lengths, row_tokens)
    keep_here = 1.0 - start_flags
    keep_next = jnp.concatenate([keep_here[:, 1:], jnp.zeros((row_count, 1), jnp.float32)], axis=1)

    def forward(inputs, poles, log_step, in_matrix, out_matrix, feedthrough, norm_gain, norm_bias):
        first_out = residual_layer(inputs, poles[0], log_step[0], in_matrix[0], out_matrix[0], feedthrough[0], norm_gain[0], norm_bias[0], keep_here, False, row_count)
        return residual_layer(first_out, poles[1], log_step[1], in_matrix[1], out_matrix[1], feedthrough[1], norm_gain[1], norm_bias[1], keep_next, True, row_count)
    outputs, pullback = jax.vjp(forward, inputs, poles, log_step, in_matrix, out_matrix, feedthrough, norm_gain, norm_bias)
    gradients = pullback(cotangent)
    return (outputs, gradients[0], gradients[1], gradients[2], gradients[3], gradients[4], gradients[5], gradients[6], gradients[7])
```

```python
import functools

import jax
import jax.numpy as jnp
from jax import lax
from jax.experimental import pallas as pl
from jax.experimental.pallas import tpu as pltpu
from jax.sharding import PartitionSpec as P


EPSILON = 1e-05
LANES = 128
SUBS = 8
MESH = pl.DeviceIdType.MESH
F32 = jnp.float32
BF16 = jnp.bfloat16
MATRICES = ((0, "in"), (0, "out"), (1, "in"), (1, "out"))
DIMS = {
    "nt": (((1,), (1,)), ((), ())),
    "nn": (((1,), (0,)), ((), ())),
    "tn": (((0,), (0,)), ((), ())),
}


def halves(values):
    high = values.astype(BF16)
    return high, (values - high.astype(F32)).astype(BF16)


def product(left, right, form):
    def one(a, b):
        return lax.dot_general(a, b, DIMS[form], preferred_element_type=F32)

    return one(left[0], right[0]) + (one(left[0], right[1]) + one(left[1], right[0]))


def cmul(ar, ai, br, bi):
    return ar * br - ai * bi, ar * bi + ai * br


def kernel(
    sizes,
    x_hbm,
    seq_ref,
    poles_ref,
    step_ref,
    in_hbm,
    out_mat_hbm,
    feed_ref,
    gain_ref,
    bias_ref,
    cot_hbm,
    out_hbm,
    gx_hbm,
    gpoles_ref,
    gstep_ref,
    gin_hbm,
    gout_hbm,
    gfeed_ref,
    ggain_ref,
    gbias_ref,
    xloc,
    small_src,
    small_all,
    wf,
    wh,
    wl,
    par,
    ktab,
    hid,
    cotb,
    zn,
    zh,
    zl,
    raw,
    xs,
    ybuf,
    actp,
    dyf,
    dyh,
    dyl,
    seed,
    gadj,
    dz,
    dh,
    gl,
    gsib,
    gblk,
    psum,
    gz,
    fin,
    s0_own,
    s0_sib,
    s0_z,
    s0_b,
    st_own,
    st_sib,
    st_src,
    st_buf,
    st_tot,
    cy_src,
    cy_buf,
    q_own,
    q_sib,
    q_blk,
    q_z,
    loc_s,
    sm_s,
    sm_r,
    aa_s,
    aa_r,
    w_s,
    w_r,
    wc_s,
    wc_r,
    s0c,
    s0z_s,
    s0z_r,
    s0b_s,
    s0b_r,
    stc_s,
    stc_r,
    stx_s,
    stx_r,
    cy_s,
    cy_r,
    gc_s,
    gc_r,
    gb_s,
    gb_r,
    gz_s,
    gz_r,
    ga_s,
    ga_r,
    g2_s,
    g2_r,
    qc,
    qb_s,
    qb_r,
    qz_s,
    qz_r,
):
    nb, nz, seqs, tokens, feats, states, token_count = sizes
    nch = nb * nz
    tc, fb, sb = tokens // nb, feats // nb, states // nb
    steps = tc // SUBS
    ng = states // LANES
    fl = feats // LANES
    b = lax.axis_index("blk")
    r = lax.axis_index("row")
    core = r % 2
    z = r // 2
    chip = b * nz + z
    sibling = (b, z * 2 + 1 - core)
    blk_peers = [((b + k) % nb) for k in range(1, nb)]
    z_peers = [((z + k) % nz) for k in range(1, nz)] if nz <= 8 else None

    def blk_dev(p):
        return (p, r)

    def z_dev(p):
        return (b, p * 2 + core)

    def remote(src, dst, ss, rs, dev):
        return pltpu.make_async_remote_copy(
            src, dst, ss, rs, device_id=dev, device_id_type=MESH
        )

    def over_z(body):
        if nz <= 8:
            for k in range(1, nz):
                body((z + k) % nz)
        else:

            def step(k, carry):
                body((z + k) % nz)
                return carry

            lax.fori_loop(1, nz, step, 0)

    def over_chips(body):
        def peer(k):
            q = (chip + k) % nch
            body(q, (q // nz, (q % nz) * 2 + core))

        if nch <= 16:
            for k in range(1, nch):
                peer(k)
        else:

            def step(k, carry):
                peer(k)
                return carry

            lax.fori_loop(1, nch, step, 0)

    def rows_of(i, size):
        return pl.ds(pl.multiple_of(i * size, size), size)

    my_cols = rows_of(b, fb)

    def local_copy(i, src, dst):
        return pltpu.make_async_copy(src, dst, loc_s.at[i])

    mats = [in_hbm if kind == "in" else out_mat_hbm for _, kind in MATRICES]
    locals_ = {
        "x": local_copy(0, x_hbm, xloc),
        "h": local_copy(1, x_hbm.at[rows_of(b, tc), :], hid.at[0, :, my_cols]),
        "c": local_copy(2, cot_hbm.at[rows_of(b, tc), :], cotb.at[:, my_cols]),
    }
    my_rows = pl.ds(pl.multiple_of(core * states + b * sb, 8), sb)
    for m, (layer, _) in enumerate(MATRICES):
        locals_[m] = local_copy(3 + m, mats[m].at[layer, core], wf.at[m, my_rows, :])
    for copy in locals_.values():
        copy.start()

    barrier = pltpu.get_barrier_semaphore()
    pl.semaphore_signal(barrier, 1, device_id=sibling, device_id_type=MESH)
    over_chips(
        lambda q, dev: pl.semaphore_signal(barrier, 1, device_id=dev, device_id_type=MESH)
    )

    small_src[...] = jnp.zeros_like(small_src)
    for layer in range(2):
        small_src[2 * layer : 2 * layer + 2, 0:sb] = poles_ref[layer]
    small_src[4:6, 0:sb] = step_ref[...]
    small_src[6:8, :] = feed_ref[...]
    small_src[8:10, :] = gain_ref[...]
    small_src[10:12, :] = bias_ref[...]
    small_all[b] = small_src[...]
    pl.semaphore_wait(barrier, nch)

    sends = []

    def send(copy):
        copy.start()
        sends.append(copy)

    for p in blk_peers:
        send(remote(small_src, small_all.at[b], sm_s.at[p], sm_r.at[b], blk_dev(p)))

    def send_matrix(m):
        layer = MATRICES[m][0]
        for p in blk_peers:
            send(
                remote(
                    mats[m].at[layer, core],
                    wf.at[m, my_rows, :],
                    w_s.at[m, p],
                    w_r.at[m, b],
                    blk_dev(p),
                )
            )

    def send_in(i, src, dst):
        for p in blk_peers:
            send(
                remote(
                    src.at[rows_of(p, tc), :],
                    dst.at[:, my_cols],
                    aa_s.at[i, p],
                    aa_r.at[i, b],
                    blk_dev(p),
                )
            )

    def wait_in(i, dst):
        for p in blk_peers:
            piece = dst.at[:, rows_of(p, fb)]
            remote(piece, piece, aa_s.at[i, p], aa_r.at[i, p], blk_dev(p)).wait_recv()

    def send_out(i, src, dst):
        own = pltpu.make_async_copy(
            src.at[:, my_cols], dst.at[rows_of(b, tc), :], loc_s.at[5 + i]
        )
        own.start()
        for p in blk_peers:
            send(
                remote(
                    src.at[:, rows_of(p, fb)],
                    dst.at[rows_of(b, tc), :],
                    aa_s.at[i, p],
                    aa_r.at[i, b],
                    blk_dev(p),
                )
            )
        return own

    def wait_out(i, dst):
        for p in blk_peers:
            piece = dst.at[rows_of(p, tc), :]
            remote(piece, piece, aa_s.at[i, p], aa_r.at[i, p], blk_dev(p)).wait_recv()

    def core_rows(part):
        return pl.ds(pl.multiple_of(part * states, 8), states)

    def forward_matrix(m):
        locals_[m].wait()
        for p in blk_peers:
            piece = wf.at[m, pl.ds(pl.multiple_of(core * states + p * sb, 8), sb), :]
            remote(piece, piece, w_s.at[m, p], w_r.at[m, p], blk_dev(p)).wait_recv()
        piece = wf.at[m, core_rows(core), :]
        send(remote(piece, piece, wc_s.at[m], wc_r.at[m], sibling))

    def split_matrix(m):
        piece = wf.at[m, core_rows(1 - core), :]
        remote(piece, piece, wc_s.at[m], wc_r.at[m], sibling).wait_recv()
        scaled = MATRICES[m][1] == "out"
        for part in range(2):

            def body(i, carry, part=part):
                rows = pl.ds(pl.multiple_of(part * states + i * 64, 64), 64)
                values = wf[m, rows, :]
                if scaled:
                    values = values * (2.0 - 4.0 * part)
                wh[m, rows, :], wl[m, rows, :] = halves(values)
                return carry

            lax.fori_loop(0, states // 64, body, 0)

    send_matrix(0)
    locals_["x"].wait()

    def add_rows(i, carry):
        total, square = carry
        values = xloc[rows_of(i, 64), :].reshape(8, SUBS, LANES * (fb // LANES))
        return total + jnp.sum(values, axis=0), square + jnp.sum(values * values, axis=0)

    zero_tile = jnp.zeros((SUBS, fb), F32)
    total, square = lax.fori_loop(0, tokens // 64, add_rows, (zero_tile, zero_tile))
    s0_own[...] = jnp.zeros_like(s0_own)
    s0_own[0:1, :] = jnp.sum(total, axis=0, keepdims=True)
    s0_own[1:2, :] = jnp.sum(square, axis=0, keepdims=True)
    copy = remote(s0_own, s0_sib, s0c.at[0], s0c.at[1], sibling)
    copy.start()
    copy.wait_recv()
    s0_z[z] = s0_own[...] + s0_sib[...]
    sends.append(copy)
    over_z(
        lambda p: remote(
            s0_z.at[z], s0_z.at[z], s0z_s.at[p], s0z_r.at[z], z_dev(p)
        ).start()
    )
    over_z(
        lambda p: remote(
            s0_z.at[p], s0_z.at[p], s0z_s.at[p], s0z_r.at[p], z_dev(p)
        ).wait()
    )
    s0_b[b] = jnp.sum(s0_z[...], axis=0)
    for p in blk_peers:
        send(remote(s0_b.at[b], s0_b.at[b], s0b_s.at[p], s0b_r.at[b], blk_dev(p)))
    send_in(0, x_hbm, hid.at[0])
    send_matrix(1)

    for p in blk_peers:
        remote(
            small_all.at[p], small_all.at[p], sm_s.at[p], sm_r.at[p], blk_dev(p)
        ).wait_recv()
    state_rows = jnp.concatenate([small_all[p][0:8, 0:sb] for p in range(nb)], axis=1)

    def feature_row(row):
        return jnp.concatenate([small_all[p][row : row + 1, :] for p in range(nb)], axis=1)

    def discretize(real, imag, log_step):
        step = jnp.exp(log_step)
        magnitude = jnp.exp(real * step)
        lr = magnitude * jnp.cos(imag * step)
        li = magnitude * jnp.sin(imag * step)
        modulus = real * real + imag * imag
        fr = ((lr - 1.0) * real + li * imag) / modulus
        fi = (li * real - (lr - 1.0) * imag) / modulus
        return step, lr, li, fr, fi, modulus

    for layer in range(2):
        _, lr, li, fr, fi, _ = discretize(
            state_rows[2 * layer : 2 * layer + 1, :],
            state_rows[2 * layer + 1 : 2 * layer + 2, :],
            state_rows[4 + layer : 5 + layer, :],
        )
        power = [(lr, li)]
        size = 1
        while size < tc:
            power.append(cmul(*power[-1], *power[-1]))
            size *= 2
        at_steps = power[steps.bit_length() - 1]
        for row, value in enumerate((lr, li, fr, fi, *at_steps, *power[-1])):
            par[layer, row : row + 1, :] = value

    def wide(layer, row, group):
        part = par[layer, row : row + 1, group * LANES : (group + 1) * LANES]
        return jnp.broadcast_to(part, (SUBS, LANES))

    starts = [jnp.int32(0)]
    for i in range(seqs - 1):
        starts.append(starts[-1] + seq_ref[0, i])
    begins = starts
    ends = starts[1:] + [jnp.int32(tokens)]

    def none_in(low, size, marks, shift):
        hit = None
        for mark in marks:
            at = mark - shift - low
            inside = jnp.logical_and(at >= 0, at < size)
            hit = inside if hit is None else jnp.logical_or(hit, inside)
        return jnp.where(hit, 0.0, 1.0).astype(F32)

    sub_index = lax.broadcasted_iota(jnp.int32, (SUBS, LANES), 0)
    base = b * tc
    marks = ((begins, 0), (ends, 1))

    def fill_flags(k, carry):
        for way in range(2):
            ktab[way, k] = none_in(base + sub_index * steps + k, 1, *marks[way])
        return carry

    lax.fori_loop(0, steps, fill_flags, 0)
    whole_sub = [none_in(base + sub_index * steps, steps, *marks[way]) for way in range(2)]
    whole_chunk = [[none_in(p * tc, tc, *marks[way]) for p in range(nb)] for way in range(2)]

    def load(ref, g, k):
        return ref[g, pl.ds(k, SUBS, stride=steps), :]

    def recur(carry, keep, lam, pushes):
        gated = [c * keep for c in carry]
        new = []
        for g in range(ng):
            vr, vi = cmul(lam[0][g], lam[1][g], gated[g], gated[ng + g])
            new.append((vr + pushes[g], vi + pushes[ng + g]))
        return gated, [v[0] for v in new] + [v[1] for v in new]

    def scan_local(src, lam, way, reverse):
        def body(i, carry):
            k = steps - 1 - i if reverse else i
            pushes = [load(src, g, k) for g in range(2 * ng)]
            return tuple(recur(carry, ktab[way, k], lam, pushes)[1])

        zero = jnp.zeros((SUBS, LANES), F32)
        return lax.fori_loop(0, steps, body, (zero,) * (2 * ng), unroll=4)

    def prefix(last, power, way, reverse):
        out = []
        for g in range(ng):
            sr, si = last[g], last[ng + g]
            ar, ai = power[0][g] * whole_sub[way], power[1][g] * whole_sub[way]
            for d in (1, 2, 4):
                shift = SUBS - d if reverse else d
                ok = sub_index < SUBS - d if reverse else sub_index >= d
                tr, ti = cmul(ar, ai, pltpu.roll(sr, shift, 0), pltpu.roll(si, shift, 0))
                br, bi = cmul(ar, ai, pltpu.roll(ar, shift, 0), pltpu.roll(ai, shift, 0))
                sr, si = jnp.where(ok, sr + tr, sr), jnp.where(ok, si + ti, si)
                ar, ai = jnp.where(ok, br, ar), jnp.where(ok, bi, ai)
            out.append((sr, si, ar, ai))
        return out

    def send_carry(e, pre, reverse):
        row = 0 if reverse else SUBS - 1
        for g in range(ng):
            cols = slice(g * LANES, (g + 1) * LANES)
            for part in range(2):
                cy_src[e, part : part + 1, cols] = pre[g][part][row : row + 1, :]
                cy_buf[e, b, part : part + 1, cols] = pre[g][part][row : row + 1, :]
        for p in blk_peers:
            send(
                remote(cy_src.at[e], cy_buf.at[e, b], cy_s.at[e, p], cy_r.at[e, b], blk_dev(p))
            )

    def take_carry(e, pre, layer, way, reverse, sign):
        for p in blk_peers:
            piece = cy_buf.at[e, p]
            remote(cy_src.at[e], piece, cy_s.at[e, p], cy_r.at[e, p], blk_dev(p)).wait_recv()
        ar, ai = par[layer, 6:7, :], sign * par[layer, 7:8, :]
        zero = jnp.zeros((1, states), F32)
        cr, ci, er, ei = zero, zero, zero, zero
        for p in reversed(range(nb)) if reverse else range(nb):
            er, ei = jnp.where(b == p, cr, er), jnp.where(b == p, ci, ei)
            tr, ti = cmul(ar, ai, cr, ci)
            keep = whole_chunk[way][p]
            cr = cy_buf[e, p, 0:1, :] + keep * tr
            ci = cy_buf[e, p, 1:2, :] + keep * ti
        shift = SUBS - 1 if reverse else 1
        first = sub_index == (SUBS - 1 if reverse else 0)
        carry_r, carry_i = [], []
        for g in range(ng):
            cols = slice(g * LANES, (g + 1) * LANES)
            wr = jnp.broadcast_to(er[:, cols], (SUBS, LANES))
            wi = jnp.broadcast_to(ei[:, cols], (SUBS, LANES))
            sr, si, dr, di = (pltpu.roll(v, shift, 0) for v in pre[g])
            tr, ti = cmul(dr, di, wr, wi)
            carry_r.append(jnp.where(first, wr, sr + tr))
            carry_i.append(jnp.where(first, wi, si + ti))
        return tuple(carry_r + carry_i)

    def forward_states(layer, carry, way, reverse, lam):
        scale = [[wide(layer, 2 + part, g) for g in range(ng)] for part in range(2)]
        src, dst = raw.at[layer], xs.at[layer]

        def body(i, carry):
            k = steps - 1 - i if reverse else i
            pushes = [load(src, g, k) for g in range(2 * ng)]
            _, new = recur(carry, ktab[way, k], lam, pushes)
            for g in range(ng):
                vr, vi = cmul(scale[0][g], scale[1][g], new[g], new[ng + g])
                dst[g, pl.ds(k, SUBS, stride=steps), :] = vr
                dst[ng + g, pl.ds(k, SUBS, stride=steps), :] = vi
            return tuple(new)

        lax.fori_loop(0, steps, body, carry, unroll=2)

    def adjoint_states(layer, carry, way, reverse, lam):
        scale = [[wide(layer, 2 + part, g) for g in range(ng)] for part in range(2)]
        zero = jnp.zeros((SUBS, LANES), F32)

        def body(i, loop):
            carry, sums = loop
            k = steps - 1 - i if reverse else i
            at = pl.ds(k, SUBS, stride=steps)
            pushes = [load(seed, g, k) for g in range(2 * ng)]
            gated, new = recur(carry, ktab[way, k], lam, pushes)
            sums = list(sums)
            for g in range(ng):
                xr, xi = xs[layer, g, at, :], xs[layer, ng + g, at, :]
                ur, ui = raw[layer, g, at, :], raw[layer, ng + g, at, :]
                pr, pi = gated[g], gated[ng + g]
                vr, vi = new[g], new[ng + g]
                sums[g] += pr * xr + pi * xi
                sums[ng + g] += pi * xr - pr * xi
                sums[2 * ng + g] += vr * ur + vi * ui
                sums[3 * ng + g] += vi * ur - vr * ui
                gadj[g, at, :] = scale[0][g] * vr + scale[1][g] * vi
                gadj[ng + g, at, :] = scale[0][g] * vi - scale[1][g] * vr
            return tuple(new), tuple(sums)

        return lax.fori_loop(0, steps, body, (carry, (zero,) * (4 * ng)))[1]

    tile = 256 if tc % 256 == 0 else tc

    def to_groups(left, m, dst):
        def body(i, carry):
            rows = rows_of(i, tile)
            value = product(
                (left[0][rows, :], left[1][rows, :]), (wh[m], wl[m]), "nt"
            )
            for g in range(2 * ng):
                dst[g, rows, :] = value[:, g * LANES : (g + 1) * LANES]
            return carry

        lax.fori_loop(0, tc // tile, body, 0)

    def from_groups(src, m, dst):
        def body(i, carry):
            rows = rows_of(i, tile)
            left = jnp.concatenate([src[g, rows, :] for g in range(2 * ng)], axis=1)
            dst[rows, :] = product(halves(left), (wh[m], wl[m]), "nn")
            return carry

        lax.fori_loop(0, tc // tile, body, 0)

    def weight_grad(src, right, m, scaled):
        def body(pair, carry):
            left = jnp.concatenate([src[2 * pair], src[2 * pair + 1]], axis=1)
            value = product(halves(left), (right[0][...], right[1][...]), "tn")
            for half in range(2):
                g = 2 * pair + half
                part = value[half * LANES : (half + 1) * LANES, :]
                if scaled:
                    part = part * jnp.where(g < ng, 2.0, -2.0)
                gl[m, rows_of(g, LANES), :] = part
            return carry

        lax.fori_loop(0, ng, body, 0)

    def stats_start(i, first, second):
        for n, value in enumerate((first, second)):
            for j in range(fl):
                row = n * fl + j
                st_own[i, row : row + 1, :] = value[:, j * LANES : (j + 1) * LANES]
        copy = remote(st_own.at[i], st_sib.at[i], stc_s.at[i], stc_r.at[i], sibling)
        send(copy)
        copy.wait_recv()
        both = st_own[i] + st_sib[i]
        st_src[i] = both
        st_buf[i, chip] = both
        over_chips(
            lambda q, dev: remote(
                st_src.at[i], st_buf.at[i, chip], stx_s.at[i, q], stx_r.at[i, chip], dev
            ).start()
        )

    def stats_end(i):
        over_chips(
            lambda q, dev: remote(
                st_src.at[i], st_buf.at[i, q], stx_s.at[i, q], stx_r.at[i, q], dev
            ).wait()
        )
        st_tot[i] = jnp.sum(st_buf[i], axis=0)
        return [
            jnp.concatenate(
                [st_tot[i, n * fl + j : n * fl + j + 1, :] for j in range(fl)], axis=1
            )
            for n in range(2)
        ]

    def to_row(value):
        return jnp.sum(value, axis=0, keepdims=True)

    def eights(value):
        return jnp.sum(value.reshape(value.shape[0] // SUBS, SUBS, feats), axis=0)

    def grad_core(m):
        send(
            remote(gl.at[m, core_rows(1 - core), :], gsib.at[m], gc_s.at[m], gc_r.at[m], sibling)
        )

    def grad_blk(m):
        remote(gsib.at[m], gsib.at[m], gc_s.at[m], gc_r.at[m], sibling).wait_recv()

        def body(i, carry):
            rows = rows_of(i, 32)
            own = pl.ds(pl.multiple_of(core * states + i * 32, 32), 32)
            gsib[m, rows, :] += gl[m, own, :]
            return carry

        lax.fori_loop(0, states // 32, body, 0)
        for p in blk_peers:
            piece = gsib.at[m, pl.ds(pl.multiple_of(p * sb, 8), sb), :]
            send(remote(piece, gblk.at[m, b], gb_s.at[m, p], gb_r.at[m, b], blk_dev(p)))

    pr = psum.shape[1] // nz

    def grad_z(m):
        for p in blk_peers:
            piece = gblk.at[m, p]
            remote(piece, piece, gb_s.at[m, p], gb_r.at[m, p], blk_dev(p)).wait_recv()
        own = pl.ds(pl.multiple_of(b * sb, 8), sb)
        for j in range(fl):
            cols = slice(j * LANES, (j + 1) * LANES)
            value = gsib[m, own, cols]
            for p in blk_peers:
                value += gblk[m, p, :, cols]
            psum[m, j * sb : (j + 1) * sb, :] = value
        over_z(
            lambda p: remote(
                psum.at[m, rows_of(p, pr), :], gz.at[m, z], gz_s.at[m, p], gz_r.at[m, z], z_dev(p)
            ).start()
        )

    def grad_gather(m):
        over_z(
            lambda p: remote(
                psum.at[m, rows_of(p, pr), :], gz.at[m, p], gz_s.at[m, p], gz_r.at[m, p], z_dev(p)
            ).wait()
        )
        mine = rows_of(z, pr)
        gz[m, z] = psum[m, mine, :]
        value = gz[m, 0]
        for p in range(1, nz):
            value += gz[m, p]
        fin[m, core, mine, :] = value
        piece = fin.at[m, core, mine, :]
        over_z(
            lambda p: remote(piece, piece, ga_s.at[m, p], ga_r.at[m, z], z_dev(p)).start()
        )

    def grad_share(m):
        def arrive(p):
            piece = fin.at[m, core, rows_of(p, pr), :]
            remote(piece, piece, ga_s.at[m, p], ga_r.at[m, p], z_dev(p)).wait()

        over_z(arrive)
        piece = fin.at[m, core]
        send(remote(piece, piece, g2_s.at[m], g2_r.at[m], sibling))

    stores = []

    def grad_store(m):
        piece = fin.at[m, 1 - core]
        remote(piece, piece, g2_s.at[m], g2_r.at[m], sibling).wait_recv()
        layer, kind = MATRICES[m]
        dst = gin_hbm if kind == "in" else gout_hbm
        for part in range(2):
            for j in range(fl):
                copy = pltpu.make_async_copy(
                    fin.at[m, part, j * sb : (j + 1) * sb, :],
                    dst.at[layer, part, :, j * LANES : (j + 1) * LANES],
                    loc_s.at[9 + (m * 2 + part) * fl + j],
                )
                copy.start()
                stores.append(copy)

    for p in blk_peers:
        remote(s0_b.at[p], s0_b.at[p], s0b_s.at[p], s0b_r.at[p], blk_dev(p)).wait_recv()
    sums = [
        jnp.concatenate([s0_b[p][n : n + 1, :] for p in range(nb)], axis=1) for n in range(2)
    ]
    forward_matrix(0)
    split_matrix(0)
    locals_["h"].wait()
    wait_in(0, hid.at[0])

    scales = []
    small_rows = 32

    for layer in range(2):
        way, reverse = layer, layer == 1
        mean = sums[0] / token_count
        rstd = lax.rsqrt(sums[1] / token_count - mean * mean + EPSILON)
        gain, bias, feed = (feature_row(row + layer) for row in (8, 10, 6))
        scales.append((rstd, gain, bias, feed))

        def normalize(i, carry, layer=layer, mean=mean, rstd=rstd, gain=gain, bias=bias):
            rows = rows_of(i, small_rows)
            unit = (hid[layer, rows, :] - mean) * rstd
            zn[layer, rows, :] = unit
            zh[layer, rows, :], zl[layer, rows, :] = halves(gain * unit + bias)
            return carry

        lax.fori_loop(0, tc // small_rows, normalize, 0)
        to_groups((zh.at[layer], zl.at[layer]), 2 * layer, raw.at[layer])
        lam = [[wide(layer, part, g) for g in range(ng)] for part in range(2)]
        power = [[wide(layer, 4 + part, g) for g in range(ng)] for part in range(2)]
        last = scan_local(raw.at[layer], lam, way, reverse)
        pre = prefix(last, power, way, reverse)
        send_carry(layer, pre, reverse)
        if layer == 0:
            send_matrix(2)
        forward_matrix(2 * layer + 1)
        split_matrix(2 * layer + 1)
        carry = take_carry(layer, pre, layer, way, reverse, 1.0)
        forward_states(layer, carry, way, reverse, lam)
        from_groups(xs.at[layer], 2 * layer + 1, ybuf)

        def activate(i, carry, layer=layer, gain=gain, bias=bias, feed=feed):
            rows = rows_of(i, small_rows)
            mixed = ybuf[rows, :] + feed * (gain * zn[layer, rows, :] + bias)
            below = 0.5 * (1.0 + lax.erf(mixed * 0.7071067811865476))
            density = 0.3989422804014327 * jnp.exp(-0.5 * mixed * mixed)
            gate = 1.0 / (1.0 + jnp.exp(-mixed))
            gelu = mixed * below
            value = hid[layer, rows, :] + gelu * gate
            hid[layer + 1, rows, :] = value
            actp[layer, rows, :] = (below + mixed * density) * gate + gelu * gate * (1.0 - gate)
            return carry[0] + eights(value), carry[1] + eights(value * value)

        zero = jnp.zeros((SUBS, feats), F32)
        parts = lax.fori_loop(0, tc // small_rows, activate, (zero, zero))
        if layer == 0:
            stats_start(0, to_row(parts[0]), to_row(parts[1]))
            send_matrix(3)
            send_in(1, cot_hbm, cotb)
            forward_matrix(2)
            split_matrix(2)
            sums = stats_end(0)

    own_out = send_out(2, hid.at[2], out_hbm)
    locals_["c"].wait()
    wait_in(1, cotb)
    totals = {}
    for layer in (1, 0):
        way, reverse = 1 - layer, layer == 0
        rstd, gain, bias, feed = scales[layer]
        upper = cotb if layer == 1 else dh.at[0]

        def mixed_grad(i, carry, layer=layer, gain=gain, bias=bias, upper=upper):
            rows = rows_of(i, small_rows)
            value = upper[rows, :] * actp[layer, rows, :]
            dyf[rows, :] = value
            dyh[rows, :], dyl[rows, :] = halves(value)
            return carry + eights(value * (gain * zn[layer, rows, :] + bias))

        zero = jnp.zeros((SUBS, feats), F32)
        feed_grad = to_row(lax.fori_loop(0, tc // small_rows, mixed_grad, zero))
        to_groups((dyh, dyl), 2 * layer + 1, seed)
        lam = [
            [wide(layer, 0, g) for g in range(ng)],
            [-wide(layer, 1, g) for g in range(ng)],
        ]
        power = [
            [wide(layer, 4, g) for g in range(ng)],
            [-wide(layer, 5, g) for g in range(ng)],
        ]
        last = scan_local(seed, lam, way, reverse)
        pre = prefix(last, power, way, reverse)
        send_carry(2 + layer, pre, reverse)
        weight_grad(xs.at[layer], (dyh, dyl), 2 * layer + 1, True)
        grad_core(2 * layer + 1)
        carry = take_carry(2 + layer, pre, layer, way, reverse, -1.0)
        state_sums = adjoint_states(layer, carry, way, reverse, lam)
        grad_blk(2 * layer + 1)
        from_groups(gadj, 2 * layer, dz)

        def dz_sums(i, carry, layer=layer, feed=feed):
            rows = rows_of(i, small_rows)
            value = dz[rows, :] + feed * dyf[rows, :]
            dz[rows, :] = value
            return carry[0] + eights(value), carry[1] + eights(value * zn[layer, rows, :])

        parts = lax.fori_loop(0, tc // small_rows, dz_sums, (zero, zero))
        stats_start(1 + layer, to_row(parts[0]), to_row(parts[1]))
        weight_grad(gadj, (zh.at[layer], zl.at[layer]), 2 * layer, False)
        grad_core(2 * layer)
        for p in range(nb):
            q_own[p, layer : layer + 1, :] = feed_grad[:, p * fb : (p + 1) * fb]
        for n in range(4):
            vector = jnp.concatenate(
                [to_row(state_sums[n * ng + g]) for g in range(ng)], axis=1
            )
            row = 2 + 4 * layer + n
            for p in range(nb):
                q_own[p, row : row + 1, 0:sb] = vector[:, p * sb : (p + 1) * sb]
        grad_blk(2 * layer)
        grad_z(2 * layer + 1)
        bias_grad, gain_grad = stats_end(1 + layer)

        def hidden_grad(i, carry, layer=layer, rstd=rstd, gain=gain, bias_grad=bias_grad, gain_grad=gain_grad, upper=upper):
            rows = rows_of(i, small_rows)
            inner = (
                dz[rows, :]
                - bias_grad / token_count
                - zn[layer, rows, :] * (gain_grad / token_count)
            )
            dh[1 - layer, rows, :] = upper[rows, :] + gain * rstd * inner
            return carry

        lax.fori_loop(0, tc // small_rows, hidden_grad, 0)
        ggain_ref[layer : layer + 1, :] = st_tot[1 + layer, pl.ds(fl + b, 1), :]
        gbias_ref[layer : layer + 1, :] = st_tot[1 + layer, pl.ds(b, 1), :]
        if layer == 1:
            grad_gather(3)
            grad_z(2)

    own_gx = send_out(3, dh.at[1], gx_hbm)

    copy = remote(q_own, q_sib, qc.at[0], qc.at[1], sibling)
    send(copy)
    grad_share(3)
    grad_gather(2)
    copy.wait_recv()
    q_sib[...] += q_own[...]
    for p in blk_peers:
        send(remote(q_sib.at[p], q_blk.at[b], qb_s.at[p], qb_r.at[b], blk_dev(p)))
    grad_store(3)
    grad_gather(1)
    grad_share(2)
    grad_z(0)
    grad_store(2)
    grad_share(1)
    for p in blk_peers:
        remote(q_blk.at[p], q_blk.at[p], qb_s.at[p], qb_r.at[p], blk_dev(p)).wait_recv()
    value = q_sib[b]
    for p in blk_peers:
        value += q_blk[p]
    q_z[z] = value
    over_z(
        lambda p: remote(q_z.at[z], q_z.at[z], qz_s.at[p], qz_r.at[z], z_dev(p)).start()
    )
    grad_gather(0)
    grad_store(1)
    over_z(
        lambda p: remote(q_z.at[p], q_z.at[p], qz_s.at[p], qz_r.at[p], z_dev(p)).wait()
    )
    small = jnp.sum(q_z[...], axis=0)
    gfeed_ref[...] = small[0:2, :]
    for layer in range(2):
        real = poles_ref[layer, 0:1, :]
        imag = poles_ref[layer, 1:2, :]
        step, lr, li, fr, fi, modulus = discretize(real, imag, step_ref[layer : layer + 1, :])
        lgr, lgi, fgr, fgi = (
            small[2 + 4 * layer + n : 3 + 4 * layer + n, 0:sb] for n in range(4)
        )
        qr = (real * fgr - imag * fgi) / modulus
        qi = (real * fgi + imag * fgr) / modulus
        tr, ti = lgr + qr, lgi + qi
        wr = lr * tr + li * ti
        wi = lr * ti - li * tr
        gpoles_ref[layer, 0:1, :] = step * wr - (fr * qr + fi * qi)
        gpoles_ref[layer, 1:2, :] = step * wi - (fr * qi - fi * qr)
        gstep_ref[layer : layer + 1, :] = step * (real * wr + imag * wi)
    grad_share(0)
    grad_store(0)
    wait_out(2, out_hbm)
    wait_out(3, gx_hbm)
    own_out.wait()
    own_gx.wait()
    for copy in stores:
        copy.wait()
    for copy in sends:
        copy.wait_send()


def local(mesh, *args):
    inputs, seq_lengths = args[0], args[1]
    nb, nr = mesh.shape["blk"], mesh.shape["row"]
    nz = nr // 2
    tokens, fb = inputs.shape
    sb = args[2].shape[2]
    states, feats = sb * nb, fb * nb
    assert seq_lengths.shape[0] == 1 and nr % 2 == 0
    assert fb % LANES == 0 and states % LANES == 0 and 2 * feats == SUBS * LANES
    assert tokens % (nb * SUBS * SUBS) == 0
    tc = tokens // nb
    steps = tc // SUBS
    assert steps & (steps - 1) == 0
    nch = nb * nz
    fl = feats // LANES
    ng2 = 2 * states // LANES
    piece = -(-fl * sb // (nz * SUBS)) * SUBS
    sizes = (nb, nz, seq_lengths.shape[1], tokens, feats, states, tokens * nr)
    vmem = lambda *shape: pltpu.VMEM(shape, F32)
    half = lambda *shape: pltpu.VMEM(shape, BF16)
    dma = lambda *shape: pltpu.SemaphoreType.DMA(shape)
    scratch = [
        vmem(tokens, fb),
        vmem(16, fb),
        vmem(nb, 16, fb),
        vmem(4, 2 * states, feats),
        half(4, 2 * states, feats),
        half(4, 2 * states, feats),
        vmem(2, 8, states),
        vmem(2, steps, SUBS, LANES),
        vmem(3, tc, feats),
        vmem(tc, feats),
        vmem(2, tc, feats),
        half(2, tc, feats),
        half(2, tc, feats),
        vmem(2, ng2, tc, LANES),
        vmem(2, ng2, tc, LANES),
        vmem(tc, feats),
        vmem(2, tc, feats),
        vmem(tc, feats),
        half(tc, feats),
        half(tc, feats),
        vmem(ng2, tc, LANES),
        vmem(ng2, tc, LANES),
        vmem(tc, feats),
        vmem(2, tc, feats),
        vmem(4, 2 * states, feats),
        vmem(4, states, feats),
        vmem(4, nb, sb, feats),
        vmem(4, nz * piece, LANES),
        vmem(4, nz, piece, LANES),
        vmem(4, 2, nz * piece, LANES),
        vmem(8, fb),
        vmem(8, fb),
        vmem(nz, 8, fb),
        vmem(nb, 8, fb),
        vmem(3, 8, LANES),
        vmem(3, 8, LANES),
        vmem(3, 8, LANES),
        vmem(3, nch, 8, LANES),
        vmem(3, 8, LANES),
        vmem(4, 8, states),
        vmem(4, nb, 8, states),
        vmem(nb, 16, fb),
        vmem(nb, 16, fb),
        vmem(nb, 16, fb),
        vmem(nz, 16, fb),
        dma(9 + 8 * fl),
        dma(nb),
        dma(nb),
        dma(4, nb),
        dma(4, nb),
        dma(4, nb),
        dma(4, nb),
        dma(4),
        dma(4),
        dma(2),
        dma(nz),
        dma(nz),
        dma(nb),
        dma(nb),
        dma(3),
        dma(3),
        dma(3, nch),
        dma(3, nch),
        dma(4, nb),
        dma(4, nb),
        dma(4),
        dma(4),
        dma(4, nb),
        dma(4, nb),
        dma(4, nz),
        dma(4, nz),
        dma(4, nz),
        dma(4, nz),
        dma(4),
        dma(4),
        dma(2),
        dma(nb),
        dma(nb),
        dma(nz),
        dma(nz),
    ]
    shaped = lambda like: jax.ShapeDtypeStruct(like.shape, like.dtype)
    anywhere = pl.BlockSpec(memory_space=pl.ANY)
    fast = pl.BlockSpec(memory_space=pltpu.VMEM)
    return pl.pallas_call(
        functools.partial(kernel, sizes),
        name="s5_layers",
        out_shape=tuple(shaped(args[i]) for i in (0, 0, 2, 3, 4, 5, 6, 7, 8)),
        in_specs=[
            anywhere,
            pl.BlockSpec(memory_space=pltpu.SMEM),
            fast,
            fast,
            anywhere,
            anywhere,
            fast,
            fast,
            fast,
            anywhere,
        ],
        out_specs=(anywhere, anywhere, fast, fast, anywhere, anywhere, fast, fast, fast),
        scratch_shapes=scratch,
        compiler_params=pltpu.CompilerParams(
            collective_id=0, has_side_effects=True, vmem_limit_bytes=60 << 20
        ),
    )(*args)


def solution(mesh):
    by_state = (P(None, None, "blk"), P(None, "blk"), P(None, None, "blk", None), P(None, None, "blk", None))
    by_feature = (P(None, "blk"),) * 3
    tokens = P("row", "blk")
    return jax.shard_map(
        functools.partial(local, mesh),
        mesh=mesh,
        in_specs=(tokens, P("row", None), *by_state, *by_feature, tokens),
        out_specs=(tokens, tokens, *by_state, *by_feature),
        check_vma=False,
    )
```

```python
import functools

import jax
import jax.numpy as jnp
from jax import lax
from jax.experimental import pallas as pl
from jax.experimental.pallas import tpu as pltpu
from jax.sharding import PartitionSpec as P


EPSILON = 1e-05
LANES = 128
SUBS = 8
MESH = pl.DeviceIdType.MESH
F32 = jnp.float32
BF16 = jnp.bfloat16
MATRICES = ((0, "in"), (0, "out"), (1, "in"), (1, "out"))
SHARED = (True, False, True, True)
SEMAPHORES = 128
DIMS = {
    "nt": (((1,), (1,)), ((), ())),
    "nn": (((1,), (0,)), ((), ())),
    "tn": (((0,), (0,)), ((), ())),
}


def halves(values):
    high = values.astype(BF16)
    return high, (values - high.astype(F32)).astype(BF16)


def product(left, right, form):
    def one(a, b):
        return lax.dot_general(a, b, DIMS[form], preferred_element_type=F32)

    return one(left[0], right[0]) + (one(left[0], right[1]) + one(left[1], right[0]))


def cmul(ar, ai, br, bi):
    return ar * br - ai * bi, ar * bi + ai * br


def kernel(
    sizes,
    x_hbm,
    seq_ref,
    poles_ref,
    step_ref,
    in_hbm,
    out_mat_hbm,
    feed_ref,
    gain_ref,
    bias_ref,
    cot_hbm,
    out_hbm,
    gx_hbm,
    gin_hbm,
    gout_hbm,
    gsmall_ref,
    xloc,
    small_src,
    small_all,
    wf,
    wh,
    wl,
    par,
    ktab,
    hid,
    cotb,
    zn,
    zh,
    zl,
    raw,
    xs,
    ybuf,
    actp,
    dyf,
    dyh,
    dyl,
    seed,
    gadj,
    dz,
    dh,
    gl,
    gsib,
    gblk,
    psum,
    gz,
    fin,
    s0_own,
    s0_sib,
    s0_z,
    s0_b,
    st_own,
    st_sib,
    st_src,
    st_buf,
    st_tot,
    cy_src,
    cy_buf,
    q_own,
    q_sib,
    q_blk,
    q_z,
    sem,
):
    nb, nz, seqs, tokens, feats, states, token_count = sizes
    nch = nb * nz
    tc, fb, sb = tokens // nb, feats // nb, states // nb
    steps = tc // SUBS
    ng = states // LANES
    fl = feats // LANES
    b = lax.axis_index("blk")
    r = lax.axis_index("row")
    core = r % 2
    z = r // 2
    chip = b * nz + z
    sibling = (b, z * 2 + 1 - core)
    z_pair = (b, (z + 1 - 2 * (z % 2)) * 2 + core)
    blk_peers = [((b + k) % nb) for k in range(1, nb)]

    def several(count, body):
        if count <= 16:
            for k in range(1, count):
                body(k)
        else:

            def step(k, carry):
                body(k)
                return carry

            lax.fori_loop(1, count, step, 0)

    def over_z(body):
        def peer(k):
            q = (z + k) % nz
            body(q, (b, q * 2 + core))

        several(nz, peer)

    def over_chips(body):
        def peer(k):
            q = (chip + k) % nch
            body((q // nz, (q % nz) * 2 + core))

        several(nch, peer)

    barrier = pltpu.get_barrier_semaphore()
    pl.semaphore_signal(barrier, 1, device_id=sibling, device_id_type=MESH)
    over_chips(
        lambda dev: pl.semaphore_signal(barrier, 1, device_id=dev, device_id_type=MESH)
    )

    slots = iter(range(SEMAPHORES))
    sent = []

    def new():
        return next(slots)

    def start(src, dst, pair, dev):
        pltpu.make_async_remote_copy(
            src, dst, sem.at[pair[0]], sem.at[pair[1]], device_id=dev, device_id_type=MESH
        ).start()

    def take(ref, slot):
        pltpu.make_async_copy(ref, ref, sem.at[slot]).wait()

    def near(src, dst, slot):
        pltpu.make_async_copy(src, dst, sem.at[slot]).start()

    def near_done(ref, slot):
        pltpu.make_async_copy(ref, ref, sem.at[slot]).wait()

    def rows_of(i, size):
        return pl.ds(pl.multiple_of(i * size, size), size)

    def rows_at(i, size):
        return pl.ds(pl.multiple_of(i, 8), size)

    def to_sibling(src, dst, total=None):
        pair = (new(), new())
        start(src, dst, pair, sibling)
        sent.append((src, pair[0]))
        return pair

    def to_blk(make, total):
        pair = (new(), new())
        for p in blk_peers:
            start(*make(p), pair, (p, r))
        sent.append((total, pair[0]))
        return pair

    def to_z(make, total):
        pair = (new(), new())
        over_z(lambda p, dev: start(*make(p), pair, dev))
        sent.append((total, pair[0]))
        return pair

    my_cols = rows_of(b, fb)
    mats = [in_hbm if kind == "in" else out_mat_hbm for _, kind in MATRICES]
    x_slot, h_slot, c_slot = new(), new(), new()
    own_slots = [new() for _ in MATRICES]
    near(x_hbm, xloc, x_slot)
    near(x_hbm.at[rows_of(b, tc), :], hid.at[0, :, my_cols], h_slot)
    near(cot_hbm.at[rows_of(b, tc), :], cotb.at[:, my_cols], c_slot)
    for m, (layer, _) in enumerate(MATRICES):
        for part in range(2):
            near(
                mats[m].at[layer, part],
                wf.at[m, rows_at(part * states + b * sb, sb), :],
                own_slots[m],
            )

    small_src[...] = jnp.zeros_like(small_src)
    for layer in range(2):
        small_src[2 * layer : 2 * layer + 2, 0:sb] = poles_ref[layer]
    small_src[4:6, 0:sb] = step_ref[...]
    small_src[6:8, :] = feed_ref[...]
    small_src[8:10, :] = gain_ref[...]
    small_src[10:12, :] = bias_ref[...]
    small_all[b] = small_src[...]
    pl.semaphore_wait(barrier, nch)

    shared = [s and nz % 2 == 0 for s in SHARED]
    piece_rows = [sb // 2 if s else sb for s in shared]
    fetched = [wf.at[m, 0 : (nb - 1) * piece_rows[m], :] for m in range(4)]
    blk_pairs, z_pairs, near_pairs, far_pairs = {}, {}, {}, {}

    def weight_piece(m, p, other=False):
        half = (z % 2) * piece_rows[m] if shared[m] else 0
        if other:
            half = (1 - z % 2) * piece_rows[m]
        return wf.at[m, rows_at(core * states + p * sb + half, piece_rows[m]), :]

    def fetch(m):
        half = (z % 2) * piece_rows[m] if shared[m] else 0
        src = mats[m].at[MATRICES[m][0], core, rows_at(half, piece_rows[m]), :]
        blk_pairs[m] = to_blk(lambda p: (src, weight_piece(m, b)), fetched[m])

    def relay(m):
        take(fetched[m], blk_pairs[m][1])
        near_pairs[m] = (new(), new())
        if shared[m]:
            z_pairs[m] = (new(), new())
            sent.append((fetched[m], z_pairs[m][0]))
        for p in blk_peers:
            piece = weight_piece(m, p)
            if shared[m]:
                start(piece, piece, z_pairs[m], z_pair)
            start(piece, piece, near_pairs[m], sibling)
        sent.append((fetched[m], near_pairs[m][0]))

    def relay_far(m):
        if shared[m]:
            take(fetched[m], z_pairs[m][1])
            far_pairs[m] = (new(), new())
            for p in blk_peers:
                piece = weight_piece(m, p, other=True)
                start(piece, piece, far_pairs[m], sibling)
            sent.append((fetched[m], far_pairs[m][0]))

    def split_matrix(m):
        near_done(wf.at[m, 0 : 2 * sb, :], own_slots[m])
        take(fetched[m], near_pairs[m][1])
        if shared[m]:
            take(fetched[m], far_pairs[m][1])
        scaled = MATRICES[m][1] == "out"

        def body(i, carry):
            rows = rows_of(i, 64)
            values = wf[m, rows, :]
            if scaled:
                values = values * jnp.where(i * 64 < states, 2.0, -2.0)
            wh[m, rows, :], wl[m, rows, :] = halves(values)
            return carry

        lax.fori_loop(0, 2 * states // 64, body, 0)

    def spread_in(src, dst, low, count):
        total = dst.at[low : low + count, 0 : (nb - 1) * fb]
        pair = to_blk(
            lambda p: (
                src.at[rows_at(p * tc + low, count), :],
                dst.at[low : low + count, my_cols],
            ),
            total,
        )
        return total, pair[1]

    def spread_out(src, dst, low, count):
        slot = new()
        mine = dst.at[rows_at(b * tc + low, count), :]
        near(src.at[low : low + count, my_cols], mine, slot)
        total = dst.at[0 : (nb - 1) * count, :]
        pair = to_blk(lambda p: (src.at[low : low + count, rows_of(p, fb)], mine), total)
        return (total, pair[1]), (mine, slot)

    small_total = small_all.at[0 : nb - 1]
    small_pair = to_blk(lambda p: (small_src, small_all.at[b]), small_total)
    fetch(0)
    x_total, x_arrival = spread_in(x_hbm, hid.at[0], 0, tc)
    near_done(xloc, x_slot)

    def add_rows(i, carry):
        total, square = carry
        values = xloc[rows_of(i, 64), :].reshape(8, SUBS, fb)
        return total + jnp.sum(values, axis=0), square + jnp.sum(values * values, axis=0)

    zero_tile = jnp.zeros((SUBS, fb), F32)
    total, square = lax.fori_loop(0, tokens // 64, add_rows, (zero_tile, zero_tile))
    s0_own[...] = jnp.zeros_like(s0_own)
    s0_own[0:1, :] = jnp.sum(total, axis=0, keepdims=True)
    s0_own[1:2, :] = jnp.sum(square, axis=0, keepdims=True)
    s0_pair = to_sibling(s0_own, s0_sib)
    starts = [jnp.int32(0)]
    for i in range(seqs - 1):
        starts.append(starts[-1] + seq_ref[0, i])
    begins = starts
    ends = starts[1:] + [jnp.int32(tokens)]

    def none_in(low, size, marks, shift):
        hit = None
        for mark in marks:
            at = mark - shift - low
            inside = jnp.logical_and(at >= 0, at < size)
            hit = inside if hit is None else jnp.logical_or(hit, inside)
        return jnp.where(hit, 0.0, 1.0).astype(F32)

    sub_index = lax.broadcasted_iota(jnp.int32, (SUBS, LANES), 0)
    base = b * tc
    marks = ((begins, 0), (ends, 1))

    def fill_flags(k, carry):
        for way in range(2):
            ktab[way, k] = none_in(base + sub_index * steps + k, 1, *marks[way])
        return carry

    lax.fori_loop(0, steps, fill_flags, 0)
    whole_sub = [none_in(base + sub_index * steps, steps, *marks[way]) for way in range(2)]
    whole_chunk = [[none_in(p * tc, tc, *marks[way]) for p in range(nb)] for way in range(2)]

    take(s0_sib, s0_pair[1])
    s0_z[z] = s0_own[...] + s0_sib[...]
    s0_total = s0_z.at[0 : nz - 1]
    s0_pair = to_z(lambda p: (s0_z.at[z], s0_z.at[z]), s0_total)

    take(small_total, small_pair[1])
    state_rows = jnp.concatenate([small_all[p][0:8, 0:sb] for p in range(nb)], axis=1)

    def feature_row(row):
        return jnp.concatenate([small_all[p][row : row + 1, :] for p in range(nb)], axis=1)

    def discretize(real, imag, log_step):
        step = jnp.exp(log_step)
        magnitude = jnp.exp(real * step)
        lr = magnitude * jnp.cos(imag * step)
        li = magnitude * jnp.sin(imag * step)
        modulus = real * real + imag * imag
        fr = ((lr - 1.0) * real + li * imag) / modulus
        fi = (li * real - (lr - 1.0) * imag) / modulus
        return step, lr, li, fr, fi, modulus

    for layer in range(2):
        _, lr, li, fr, fi, _ = discretize(
            state_rows[2 * layer : 2 * layer + 1, :],
            state_rows[2 * layer + 1 : 2 * layer + 2, :],
            state_rows[4 + layer : 5 + layer, :],
        )
        power = [(lr, li)]
        size = 1
        while size < tc:
            power.append(cmul(*power[-1], *power[-1]))
            size *= 2
        at_steps = power[steps.bit_length() - 1]
        for row, value in enumerate((lr, li, fr, fi, *at_steps, *power[-1])):
            par[layer, row : row + 1, :] = value

    def wide(layer, row, group):
        part = par[layer, row : row + 1, group * LANES : (group + 1) * LANES]
        return jnp.broadcast_to(part, (SUBS, LANES))

    take(s0_total, s0_pair[1])
    s0_b[b] = jnp.sum(s0_z[...], axis=0)
    s0_total = s0_b.at[0 : nb - 1]
    s0_pair = to_blk(lambda p: (s0_b.at[b], s0_b.at[b]), s0_total)
    fetch(1)
    relay(0)

    def load(ref, g, k):
        return ref[g, pl.ds(k, SUBS, stride=steps), :]

    def recur(carry, keep, lam, pushes):
        gated = [c * keep for c in carry]
        new = []
        for g in range(ng):
            vr, vi = cmul(lam[0][g], lam[1][g], gated[g], gated[ng + g])
            new.append((vr + pushes[g], vi + pushes[ng + g]))
        return gated, [v[0] for v in new] + [v[1] for v in new]

    def scan_local(src, lam, way, reverse):
        def body(i, carry):
            k = steps - 1 - i if reverse else i
            pushes = [load(src, g, k) for g in range(2 * ng)]
            return tuple(recur(carry, ktab[way, k], lam, pushes)[1])

        zero = jnp.zeros((SUBS, LANES), F32)
        return lax.fori_loop(0, steps, body, (zero,) * (2 * ng), unroll=4)

    def prefix(last, power, way, reverse):
        out = []
        for g in range(ng):
            sr, si = last[g], last[ng + g]
            ar, ai = power[0][g] * whole_sub[way], power[1][g] * whole_sub[way]
            for d in (1, 2, 4):
                shift = SUBS - d if reverse else d
                ok = sub_index < SUBS - d if reverse else sub_index >= d
                tr, ti = cmul(ar, ai, pltpu.roll(sr, shift, 0), pltpu.roll(si, shift, 0))
                br, bi = cmul(ar, ai, pltpu.roll(ar, shift, 0), pltpu.roll(ai, shift, 0))
                sr, si = jnp.where(ok, sr + tr, sr), jnp.where(ok, si + ti, si)
                ar, ai = jnp.where(ok, br, ar), jnp.where(ok, bi, ai)
            out.append((sr, si, ar, ai))
        return out

    carry_pairs = {}

    def send_carry(e, pre, reverse):
        row = 0 if reverse else SUBS - 1
        for g in range(ng):
            cols = slice(g * LANES, (g + 1) * LANES)
            for part in range(2):
                cy_src[e, part : part + 1, cols] = pre[g][part][row : row + 1, :]
                cy_buf[e, b, part : part + 1, cols] = pre[g][part][row : row + 1, :]
        carry_pairs[e] = to_blk(
            lambda p: (cy_src.at[e], cy_buf.at[e, b]), cy_buf.at[e, 0 : nb - 1]
        )

    def take_carry(e, pre, layer, way, reverse, sign):
        take(cy_buf.at[e, 0 : nb - 1], carry_pairs[e][1])
        ar, ai = par[layer, 6:7, :], sign * par[layer, 7:8, :]
        zero = jnp.zeros((1, states), F32)
        cr, ci, er, ei = zero, zero, zero, zero
        for p in reversed(range(nb)) if reverse else range(nb):
            er, ei = jnp.where(b == p, cr, er), jnp.where(b == p, ci, ei)
            tr, ti = cmul(ar, ai, cr, ci)
            keep = whole_chunk[way][p]
            cr = cy_buf[e, p, 0:1, :] + keep * tr
            ci = cy_buf[e, p, 1:2, :] + keep * ti
        shift = SUBS - 1 if reverse else 1
        first = sub_index == (SUBS - 1 if reverse else 0)
        carry_r, carry_i = [], []
        for g in range(ng):
            cols = slice(g * LANES, (g + 1) * LANES)
            wr = jnp.broadcast_to(er[:, cols], (SUBS, LANES))
            wi = jnp.broadcast_to(ei[:, cols], (SUBS, LANES))
            sr, si, dr, di = (pltpu.roll(v, shift, 0) for v in pre[g])
            tr, ti = cmul(dr, di, wr, wi)
            carry_r.append(jnp.where(first, wr, sr + tr))
            carry_i.append(jnp.where(first, wi, si + ti))
        return tuple(carry_r + carry_i)

    def forward_states(layer, carry, way, reverse, lam):
        scale = [[wide(layer, 2 + part, g) for g in range(ng)] for part in range(2)]
        src, dst = raw.at[layer], xs.at[layer]

        def body(i, carry):
            k = steps - 1 - i if reverse else i
            pushes = [load(src, g, k) for g in range(2 * ng)]
            _, new = recur(carry, ktab[way, k], lam, pushes)
            for g in range(ng):
                vr, vi = cmul(scale[0][g], scale[1][g], new[g], new[ng + g])
                dst[g, pl.ds(k, SUBS, stride=steps), :] = vr
                dst[ng + g, pl.ds(k, SUBS, stride=steps), :] = vi
            return tuple(new)

        lax.fori_loop(0, steps, body, carry, unroll=4)

    def adjoint_states(layer, carry, way, reverse, lam):
        scale = [[wide(layer, 2 + part, g) for g in range(ng)] for part in range(2)]
        zero = jnp.zeros((SUBS, LANES), F32)

        def body(i, loop):
            carry, sums = loop
            k = steps - 1 - i if reverse else i
            at = pl.ds(k, SUBS, stride=steps)
            pushes = [load(seed, g, k) for g in range(2 * ng)]
            gated, new = recur(carry, ktab[way, k], lam, pushes)
            sums = list(sums)
            for g in range(ng):
                xr, xi = xs[layer, g, at, :], xs[layer, ng + g, at, :]
                ur, ui = raw[layer, g, at, :], raw[layer, ng + g, at, :]
                pr, pi = gated[g], gated[ng + g]
                vr, vi = new[g], new[ng + g]
                sums[g] += pr * xr + pi * xi
                sums[ng + g] += pi * xr - pr * xi
                sums[2 * ng + g] += vr * ur + vi * ui
                sums[3 * ng + g] += vi * ur - vr * ui
                gadj[g, at, :] = scale[0][g] * vr + scale[1][g] * vi
                gadj[ng + g, at, :] = scale[0][g] * vi - scale[1][g] * vr
            return tuple(new), tuple(sums)

        return lax.fori_loop(0, steps, body, (carry, (zero,) * (4 * ng)), unroll=4)[1]

    tile = 256 if tc % 256 == 0 else tc

    def to_groups(left, m, dst):
        def body(i, carry):
            rows = rows_of(i, tile)
            value = product(
                (left[0][rows, :], left[1][rows, :]), (wh[m], wl[m]), "nt"
            )
            for g in range(2 * ng):
                dst[g, rows, :] = value[:, g * LANES : (g + 1) * LANES]
            return carry

        lax.fori_loop(0, tc // tile, body, 0)

    def from_groups(src, m, dst):
        def body(i, carry):
            rows = rows_of(i, tile)
            left = jnp.concatenate([src[g, rows, :] for g in range(2 * ng)], axis=1)
            dst[rows, :] = product(halves(left), (wh[m], wl[m]), "nn")
            return carry

        lax.fori_loop(0, tc // tile, body, 0)

    def weight_grad(src, right, m, scaled):
        def body(pair, carry):
            left = jnp.concatenate([src[2 * pair], src[2 * pair + 1]], axis=1)
            value = product(halves(left), (right[0][...], right[1][...]), "tn")
            for half in range(2):
                g = 2 * pair + half
                part = value[half * LANES : (half + 1) * LANES, :]
                if scaled:
                    part = part * jnp.where(g < ng, 2.0, -2.0)
                gl[m, rows_of(g, LANES), :] = part
            return carry

        lax.fori_loop(0, ng, body, 0)

    stats_pairs = {}

    def stats_start(i, first, second):
        for n, value in enumerate((first, second)):
            for j in range(fl):
                row = n * fl + j
                st_own[i, row : row + 1, :] = value[:, j * LANES : (j + 1) * LANES]
        take(st_sib.at[i], to_sibling(st_own.at[i], st_sib.at[i])[1])
        both = st_own[i] + st_sib[i]
        st_src[i] = both
        st_buf[i, chip] = both
        stats_pairs[i] = (new(), new())
        over_chips(lambda dev: start(st_src.at[i], st_buf.at[i, chip], stats_pairs[i], dev))
        sent.append((st_buf.at[i, 0 : nch - 1], stats_pairs[i][0]))

    def stats_end(i):
        take(st_buf.at[i, 0 : nch - 1], stats_pairs[i][1])
        st_tot[i] = jnp.sum(st_buf[i], axis=0)
        return [
            jnp.concatenate(
                [st_tot[i, n * fl + j : n * fl + j + 1, :] for j in range(fl)], axis=1
            )
            for n in range(2)
        ]

    def to_row(value):
        return jnp.sum(value, axis=0, keepdims=True)

    def eights(value):
        return jnp.sum(value.reshape(value.shape[0] // SUBS, SUBS, feats), axis=0)

    gpair = {}
    pr = psum.shape[1] // nz

    def core_rows(part):
        return rows_at(part * states, states)

    def grad_core(m):
        gpair["core", m] = to_sibling(gl.at[m, core_rows(1 - core), :], gsib.at[m])

    def grad_add(m):
        take(gsib.at[m], gpair["core", m][1])

        def body(i, carry):
            gsib[m, rows_of(i, 32), :] += gl[m, rows_at(core * states + i * 32, 32), :]
            return carry

        lax.fori_loop(0, states // 32, body, 0)

    def grad_blk(m):
        gpair["blk", m] = to_blk(
            lambda p: (gsib.at[m, rows_at(p * sb, sb), :], gblk.at[m, b]),
            gblk.at[m, 0 : nb - 1],
        )

    def grad_z(m):
        take(gblk.at[m, 0 : nb - 1], gpair["blk", m][1])

        def body(i, carry):
            value = gsib[m, rows_at(b * sb + i * 8, 8), :]
            for p in blk_peers:
                value += gblk[m, p, rows_of(i, 8), :]
            for j in range(fl):
                psum[m, rows_at(j * sb + i * 8, 8), :] = value[:, j * LANES : (j + 1) * LANES]
            return carry

        lax.fori_loop(0, sb // 8, body, 0)
        gpair["z", m] = to_z(
            lambda p: (psum.at[m, rows_of(p, pr), :], gz.at[m, z]), gz.at[m, 0 : nz - 1]
        )

    def grad_gather(m):
        take(gz.at[m, 0 : nz - 1], gpair["z", m][1])
        mine = rows_of(z, pr)
        value = psum[m, mine, :]
        for p in range(nz):
            value += jnp.where(z == p, 0.0, gz[m, p])
        fin[m, core, mine, :] = value
        piece = fin.at[m, core, mine, :]
        gpair["all", m] = to_z(lambda p: (piece, piece), fin.at[m, core, 0 : (nz - 1) * pr, :])

    def grad_share(m):
        take(fin.at[m, core, 0 : (nz - 1) * pr, :], gpair["all", m][1])
        gpair["share", m] = to_sibling(fin.at[m, core], fin.at[m, core])

    stores = []

    def grad_store(m):
        take(fin.at[m, 1 - core], gpair["share", m][1])
        layer, kind = MATRICES[m]
        dst = (gin_hbm if kind == "in" else gout_hbm).at[layer]
        slot = new()
        for part in range(2):
            for j in range(fl):
                near(
                    fin.at[m, part, j * sb : (j + 1) * sb, :],
                    dst.at[part, :, j * LANES : (j + 1) * LANES],
                    slot,
                )
        stores.append((dst, slot))

    hc = tc // 2
    relay_far(0)
    split_matrix(0)
    take(s0_total, s0_pair[1])
    sums = [
        jnp.concatenate([s0_b[p][n : n + 1, :] for p in range(nb)], axis=1) for n in range(2)
    ]
    near_done(hid.at[0, :, my_cols], h_slot)
    take(x_total, x_arrival)

    scales = []
    small_rows = 32
    cot_parts = []

    for layer in range(2):
        way, reverse = layer, layer == 1
        mean = sums[0] / token_count
        rstd = lax.rsqrt(sums[1] / token_count - mean * mean + EPSILON)
        gain, bias, feed = (feature_row(row + layer) for row in (8, 10, 6))
        scales.append((rstd, gain, bias, feed))

        def normalize(i, carry, layer=layer, mean=mean, rstd=rstd, gain=gain, bias=bias):
            rows = rows_of(i, small_rows)
            unit = (hid[layer, rows, :] - mean) * rstd
            zn[layer, rows, :] = unit
            zh[layer, rows, :], zl[layer, rows, :] = halves(gain * unit + bias)
            return carry

        lax.fori_loop(0, tc // small_rows, normalize, 0)
        to_groups((zh.at[layer], zl.at[layer]), 2 * layer, raw.at[layer])
        if layer == 1:
            relay(3)
        lam = [[wide(layer, part, g) for g in range(ng)] for part in range(2)]
        power = [[wide(layer, 4 + part, g) for g in range(ng)] for part in range(2)]
        last = scan_local(raw.at[layer], lam, way, reverse)
        pre = prefix(last, power, way, reverse)
        send_carry(layer, pre, reverse)
        if layer == 0:
            fetch(2)
            relay(1)
            relay_far(1)
            split_matrix(1)
        else:
            cot_parts.append(spread_in(cot_hbm, cotb, hc, tc - hc))
            relay_far(3)
            split_matrix(3)
        carry = take_carry(layer, pre, layer, way, reverse, 1.0)
        forward_states(layer, carry, way, reverse, lam)
        if layer == 0:
            relay(2)
        from_groups(xs.at[layer], 2 * layer + 1, ybuf)

        def activate(i, carry, layer=layer, gain=gain, bias=bias, feed=feed):
            rows = rows_of(i, small_rows)
            mixed = ybuf[rows, :] + feed * (gain * zn[layer, rows, :] + bias)
            below = 0.5 * (1.0 + lax.erf(mixed * 0.7071067811865476))
            density = 0.3989422804014327 * jnp.exp(-0.5 * mixed * mixed)
            gate = 1.0 / (1.0 + jnp.exp(-mixed))
            gelu = mixed * below
            value = hid[layer, rows, :] + gelu * gate
            hid[layer + 1, rows, :] = value
            actp[layer, rows, :] = (below + mixed * density) * gate + gelu * gate * (1.0 - gate)
            return carry[0] + eights(value), carry[1] + eights(value * value)

        zero = jnp.zeros((SUBS, feats), F32)
        parts = lax.fori_loop(0, tc // small_rows, activate, (zero, zero))
        if layer == 0:
            stats_start(0, to_row(parts[0]), to_row(parts[1]))
            fetch(3)
            cot_parts.append(spread_in(cot_hbm, cotb, 0, hc))
            relay_far(2)
            split_matrix(2)
            sums = stats_end(0)

    near_done(cotb.at[:, my_cols], c_slot)
    for part in cot_parts:
        take(*part)
    outs = []
    for layer in (1, 0):
        way, reverse = 1 - layer, layer == 0
        rstd, gain, bias, feed = scales[layer]
        upper = cotb if layer == 1 else dh.at[0]

        def mixed_grad(i, carry, layer=layer, gain=gain, bias=bias, upper=upper):
            rows = rows_of(i, small_rows)
            value = upper[rows, :] * actp[layer, rows, :]
            dyf[rows, :] = value
            dyh[rows, :], dyl[rows, :] = halves(value)
            return carry + eights(value * (gain * zn[layer, rows, :] + bias))

        zero = jnp.zeros((SUBS, feats), F32)
        feed_grad = to_row(lax.fori_loop(0, tc // small_rows, mixed_grad, zero))
        to_groups((dyh, dyl), 2 * layer + 1, seed)
        lam = [
            [wide(layer, 0, g) for g in range(ng)],
            [-wide(layer, 1, g) for g in range(ng)],
        ]
        power = [
            [wide(layer, 4, g) for g in range(ng)],
            [-wide(layer, 5, g) for g in range(ng)],
        ]
        last = scan_local(seed, lam, way, reverse)
        pre = prefix(last, power, way, reverse)
        send_carry(2 + layer, pre, reverse)
        low = 0 if layer == 1 else hc
        outs.append(spread_out(hid.at[2], out_hbm, low, hc))
        weight_grad(xs.at[layer], (dyh, dyl), 2 * layer + 1, True)
        grad_core(2 * layer + 1)
        carry = take_carry(2 + layer, pre, layer, way, reverse, -1.0)
        state_sums = adjoint_states(layer, carry, way, reverse, lam)
        if layer == 0:
            grad_add(2)
            grad_z(3)
        grad_add(2 * layer + 1)
        from_groups(gadj, 2 * layer, dz)

        def dz_sums(i, carry, layer=layer, feed=feed):
            rows = rows_of(i, small_rows)
            value = dz[rows, :] + feed * dyf[rows, :]
            dz[rows, :] = value
            return carry[0] + eights(value), carry[1] + eights(value * zn[layer, rows, :])

        parts = lax.fori_loop(0, tc // small_rows, dz_sums, (zero, zero))
        stats_start(1 + layer, to_row(parts[0]), to_row(parts[1]))
        if layer == 1:
            grad_blk(3)
        else:
            grad_blk(2)
            grad_blk(1)
        weight_grad(gadj, (zh.at[layer], zl.at[layer]), 2 * layer, False)
        grad_core(2 * layer)
        for p in range(nb):
            q_own[p, layer : layer + 1, :] = feed_grad[:, p * fb : (p + 1) * fb]
        for n in range(4):
            vector = jnp.concatenate(
                [to_row(state_sums[n * ng + g]) for g in range(ng)], axis=1
            )
            row = 2 + 4 * layer + n
            for p in range(nb):
                q_own[p, row : row + 1, 0:sb] = vector[:, p * sb : (p + 1) * sb]
        if layer == 0:
            q_pair = to_sibling(q_own, q_sib)
            grad_gather(3)
            grad_add(0)
            grad_blk(0)
            take(q_sib, q_pair[1])
            q_sib[...] += q_own[...]
            q_total = q_blk.at[0 : nb - 1]
            q_pair = to_blk(lambda p: (q_sib.at[p], q_blk.at[b]), q_total)
        bias_grad, gain_grad = stats_end(1 + layer)

        def hidden_grad(
            i, carry, layer=layer, rstd=rstd, gain=gain, bias_grad=bias_grad, gain_grad=gain_grad, upper=upper
        ):
            rows = rows_of(i, small_rows)
            inner = (
                dz[rows, :]
                - bias_grad / token_count
                - zn[layer, rows, :] * (gain_grad / token_count)
            )
            dh[1 - layer, rows, :] = upper[rows, :] + gain * rstd * inner
            return carry

        lax.fori_loop(0, tc // small_rows, hidden_grad, 0)
        gsmall_ref[2 + layer : 3 + layer, :] = st_tot[1 + layer, pl.ds(fl + b, 1), :]
        gsmall_ref[4 + layer : 5 + layer, :] = st_tot[1 + layer, pl.ds(b, 1), :]

    outs.append(spread_out(dh.at[1], gx_hbm, 0, tc))
    grad_share(3)
    grad_z(2)
    grad_store(3)
    grad_z(1)
    grad_gather(2)
    grad_share(2)
    grad_gather(1)
    grad_store(2)
    grad_share(1)
    grad_z(0)
    take(q_total, q_pair[1])
    value = q_sib[b]
    for p in blk_peers:
        value += q_blk[p]
    q_z[z] = value
    q_total = q_z.at[0 : nz - 1]
    q_pair = to_z(lambda p: (q_z.at[z], q_z.at[z]), q_total)
    grad_store(1)
    grad_gather(0)
    take(q_total, q_pair[1])
    small = jnp.sum(q_z[...], axis=0)
    gsmall_ref[0:2, :] = small[0:2, :]
    for layer in range(2):
        real = poles_ref[layer, 0:1, :]
        imag = poles_ref[layer, 1:2, :]
        step, lr, li, fr, fi, modulus = discretize(real, imag, step_ref[layer : layer + 1, :])
        lgr, lgi, fgr, fgi = (
            small[2 + 4 * layer + n : 3 + 4 * layer + n, 0:sb] for n in range(4)
        )
        qr = (real * fgr - imag * fgi) / modulus
        qi = (real * fgi + imag * fgr) / modulus
        tr, ti = lgr + qr, lgi + qi
        wr = lr * tr + li * ti
        wi = lr * ti - li * tr
        row = 6 + 2 * layer
        gsmall_ref[row : row + 1, 0:sb] = step * wr - (fr * qr + fi * qi)
        gsmall_ref[row + 1 : row + 2, 0:sb] = step * wi - (fr * qi - fi * qr)
        gsmall_ref[10 + layer : 11 + layer, 0:sb] = step * (real * wr + imag * wi)
    grad_share(0)
    for arrival, mine in outs:
        take(*arrival)
        near_done(*mine)
    grad_store(0)
    for ref, slot in stores:
        near_done(ref, slot)
    for ref, slot in sent:
        take(ref, slot)


def finish(
    out_in, gx_in, gin_in, gout_in, small_in, out, gx, gpoles, gstep, gin, gout, gfeed, ggain, gbias, *scratch
):
    sem = scratch[-1]
    chunks = []
    for n, (src, dst, buf) in enumerate(zip((out_in, gx_in, gin_in, gout_in), (out, gx, gin, gout), scratch)):
        for half in range(2):
            if n < 2:
                rows = src.shape[0] // 2
                at = pl.ds(half * rows, rows)
            else:
                at = half
            chunks.append((src.at[at], buf.at[at], dst.at[at], sem.at[0, 2 * n + half], sem.at[1, 2 * n + half]))
    for src, buf, _, arrived, _ in chunks:
        pltpu.make_async_copy(src, buf, arrived).start()
    sb = gstep.shape[1]
    gfeed[...] = small_in[0:2, :]
    ggain[...] = small_in[2:4, :]
    gbias[...] = small_in[4:6, :]
    for layer in range(2):
        gpoles[layer] = small_in[6 + 2 * layer : 8 + 2 * layer, 0:sb]
    gstep[...] = small_in[10:12, 0:sb]
    for src, buf, dst, arrived, written in chunks:
        pltpu.make_async_copy(src, buf, arrived).wait()
        pltpu.make_async_copy(buf, dst, written).start()
    for _, buf, dst, _, written in chunks:
        pltpu.make_async_copy(buf, dst, written).wait()


def local(mesh, *args):
    inputs, seq_lengths = args[0], args[1]
    nb, nr = mesh.shape["blk"], mesh.shape["row"]
    nz = nr // 2
    tokens, fb = inputs.shape
    sb = args[2].shape[2]
    states, feats = sb * nb, fb * nb
    assert seq_lengths.shape[0] == 1 and nr % 2 == 0
    assert fb % LANES == 0 and states % LANES == 0 and 2 * feats == SUBS * LANES
    assert tokens % (nb * SUBS * SUBS) == 0 and sb % 16 == 0 and states % 64 == 0
    tc = tokens // nb
    steps = tc // SUBS
    assert steps & (steps - 1) == 0
    nch = nb * nz
    fl = feats // LANES
    ng2 = 2 * states // LANES
    piece = -(-fl * sb // (nz * SUBS)) * SUBS
    sizes = (nb, nz, seq_lengths.shape[1], tokens, feats, states, tokens * nr)
    vmem = lambda *shape: pltpu.VMEM(shape, F32)
    half = lambda *shape: pltpu.VMEM(shape, BF16)
    scratch = [
        vmem(tokens, fb),
        vmem(16, fb),
        vmem(nb, 16, fb),
        vmem(4, 2 * states, feats),
        half(4, 2 * states, feats),
        half(4, 2 * states, feats),
        vmem(2, 8, states),
        vmem(2, steps, SUBS, LANES),
        vmem(3, tc, feats),
        vmem(tc, feats),
        vmem(2, tc, feats),
        half(2, tc, feats),
        half(2, tc, feats),
        vmem(2, ng2, tc, LANES),
        vmem(2, ng2, tc, LANES),
        vmem(tc, feats),
        vmem(2, tc, feats),
        vmem(tc, feats),
        half(tc, feats),
        half(tc, feats),
        vmem(ng2, tc, LANES),
        vmem(ng2, tc, LANES),
        vmem(tc, feats),
        vmem(2, tc, feats),
        vmem(4, 2 * states, feats),
        vmem(4, states, feats),
        vmem(4, nb, sb, feats),
        vmem(4, nz * piece, LANES),
        vmem(4, nz, piece, LANES),
        vmem(4, 2, nz * piece, LANES),
        vmem(8, fb),
        vmem(8, fb),
        vmem(nz, 8, fb),
        vmem(nb, 8, fb),
        vmem(3, 8, LANES),
        vmem(3, 8, LANES),
        vmem(3, 8, LANES),
        vmem(3, nch, 8, LANES),
        vmem(3, 8, LANES),
        vmem(4, 8, states),
        vmem(4, nb, 8, states),
        vmem(nb, 16, fb),
        vmem(nb, 16, fb),
        vmem(nb, 16, fb),
        vmem(nz, 16, fb),
        pltpu.SemaphoreType.DMA((SEMAPHORES,)),
    ]
    shaped = lambda like: jax.ShapeDtypeStruct(like.shape, like.dtype)
    anywhere = pl.BlockSpec(memory_space=pl.ANY)
    fast = pl.BlockSpec(memory_space=pltpu.VMEM)
    raw = pl.pallas_call(
        functools.partial(kernel, sizes),
        name="s5_layers",
        out_shape=tuple(shaped(args[i]) for i in (0, 0, 4, 5)) + (jax.ShapeDtypeStruct((16, fb), F32),),
        in_specs=[
            anywhere,
            pl.BlockSpec(memory_space=pltpu.SMEM),
            fast,
            fast,
            anywhere,
            anywhere,
            fast,
            fast,
            fast,
            anywhere,
        ],
        out_specs=(anywhere,) * 4 + (fast,),
        scratch_shapes=scratch,
        compiler_params=pltpu.CompilerParams(
            collective_id=0, has_side_effects=True, vmem_limit_bytes=60 << 20
        ),
    )(*args)
    return pl.pallas_call(
        finish,
        name="results",
        out_shape=tuple(shaped(args[i]) for i in (0, 0, 2, 3, 4, 5, 6, 7, 8)),
        in_specs=[anywhere] * 4 + [fast],
        out_specs=(anywhere, anywhere, fast, fast, anywhere, anywhere, fast, fast, fast),
        scratch_shapes=[pltpu.VMEM(args[i].shape, F32) for i in (0, 0, 4, 5)]
        + [pltpu.SemaphoreType.DMA((2, 8))],
        compiler_params=pltpu.CompilerParams(vmem_limit_bytes=60 << 20),
    )(*raw)


def solution(mesh):
    by_state = (P(None, None, "blk"), P(None, "blk"), P(None, None, "blk", None), P(None, None, "blk", None))
    by_feature = (P(None, "blk"),) * 3
    tokens = P("row", "blk")
    return jax.shard_map(
        functools.partial(local, mesh),
        mesh=mesh,
        in_specs=(tokens, P("row", None), *by_state, *by_feature, tokens),
        out_specs=(tokens, tokens, *by_state, *by_feature),
        check_vma=False,
    )
```

```python
import functools

import jax
import jax.numpy as jnp
from jax import lax
from jax.experimental import pallas as pl
from jax.experimental.pallas import tpu as pltpu
from jax.sharding import PartitionSpec as P


EPSILON = 1e-05
LANES = 128
SUBS = 8
GROUP = 4
MESH = pl.DeviceIdType.MESH
F32 = jnp.float32
BF16 = jnp.bfloat16
MATRICES = ((0, "in"), (0, "out"), (1, "in"), (1, "out"))
SHARED = (True, False, True, True)
SEMAPHORES = 128
DIMS = {
    "nt": (((1,), (1,)), ((), ())),
    "nn": (((1,), (0,)), ((), ())),
    "tn": (((0,), (0,)), ((), ())),
}


def halves(values):
    high = values.astype(BF16)
    return high, (values - high.astype(F32)).astype(BF16)


def product(left, right, form):
    def one(a, b):
        return lax.dot_general(a, b, DIMS[form], preferred_element_type=F32)

    return one(left[0], right[0]) + (one(left[0], right[1]) + one(left[1], right[0]))


def cmul(ar, ai, br, bi):
    return ar * br - ai * bi, ar * bi + ai * br


def kernel(
    sizes,
    x_hbm,
    seq_ref,
    poles_ref,
    step_ref,
    in_hbm,
    out_mat_hbm,
    feed_ref,
    gain_ref,
    bias_ref,
    cot_hbm,
    out_hbm,
    gx_hbm,
    gin_hbm,
    gout_hbm,
    gsmall_ref,
    xloc,
    small_src,
    small_all,
    wf,
    wh,
    wl,
    par,
    ktab,
    xin,
    hid,
    cotb,
    outb,
    gxb,
    zn,
    zh,
    zl,
    raw,
    xs,
    ybuf,
    actp,
    dyf,
    dyh,
    dyl,
    seed,
    gadj,
    dz,
    dh,
    gl,
    gsib,
    gblk,
    psum,
    gz,
    fin,
    s0_own,
    s0_sib,
    s0_z,
    s0_b,
    st_own,
    st_sib,
    st_src,
    st_buf,
    st_tot,
    cy_src,
    cy_buf,
    q_own,
    q_sib,
    q_blk,
    q_z,
    sem,
):
    nb, nz, seqs, tokens, feats, states, token_count = sizes
    nch = nb * nz
    tc, fb, sb = tokens // nb, feats // nb, states // nb
    steps = tc // SUBS
    ng = states // LANES
    fl = feats // LANES
    b = lax.axis_index("blk")
    r = lax.axis_index("row")
    core = r % 2
    z = r // 2
    chip = b * nz + z
    sibling = (b, z * 2 + 1 - core)
    z_pair = (b, (z + 1 - 2 * (z % 2)) * 2 + core)
    blk_peers = [((b + k) % nb) for k in range(1, nb)]

    def several(count, body):
        if count <= 16:
            for k in range(1, count):
                body(k)
        else:

            def step(k, carry):
                body(k)
                return carry

            lax.fori_loop(1, count, step, 0)

    def over_z(body):
        def peer(k):
            q = (z + k) % nz
            body(q, (b, q * 2 + core))

        several(nz, peer)

    def over_chips(body):
        def peer(k):
            q = (chip + k) % nch
            body((q // nz, (q % nz) * 2 + core))

        several(nch, peer)

    barrier = pltpu.get_barrier_semaphore()
    pl.semaphore_signal(barrier, 1, device_id=sibling, device_id_type=MESH)
    over_chips(
        lambda dev: pl.semaphore_signal(barrier, 1, device_id=dev, device_id_type=MESH)
    )

    slots = iter(range(SEMAPHORES))
    sent = []

    def new():
        return next(slots)

    def start(src, dst, pair, dev):
        pltpu.make_async_remote_copy(
            src, dst, sem.at[pair[0]], sem.at[pair[1]], device_id=dev, device_id_type=MESH
        ).start()

    def take(ref, slot):
        pltpu.make_async_copy(ref, ref, sem.at[slot]).wait()

    def near(src, dst, slot):
        pltpu.make_async_copy(src, dst, sem.at[slot]).start()

    def near_done(ref, slot):
        pltpu.make_async_copy(ref, ref, sem.at[slot]).wait()

    def rows_of(i, size):
        return pl.ds(pl.multiple_of(i * size, size), size)

    def rows_at(i, size):
        return pl.ds(pl.multiple_of(i, 8), size)

    def to_sibling(src, dst, total=None):
        pair = (new(), new())
        start(src, dst, pair, sibling)
        sent.append((src, pair[0]))
        return pair

    def to_blk(make, total):
        pair = (new(), new())
        for p in blk_peers:
            start(*make(p), pair, (p, r))
        sent.append((total, pair[0]))
        return pair

    def to_z(make, total):
        pair = (new(), new())
        over_z(lambda p, dev: start(*make(p), pair, dev))
        sent.append((total, pair[0]))
        return pair

    my_cols = rows_of(b, fb)
    mats = [in_hbm if kind == "in" else out_mat_hbm for _, kind in MATRICES]
    x_slot, h_slot, c_slot = new(), new(), new()
    own_slots = [new() for _ in MATRICES]
    near(x_hbm, xloc, x_slot)
    near(x_hbm.at[rows_of(b, tc), :], xin.at[b], h_slot)
    near(cot_hbm.at[rows_of(b, tc), :], cotb.at[b], c_slot)
    for m, (layer, _) in enumerate(MATRICES):
        for part in range(2):
            near(
                mats[m].at[layer, part],
                wf.at[m, rows_at(part * states + b * sb, sb), :],
                own_slots[m],
            )

    small_src[...] = jnp.zeros_like(small_src)
    for layer in range(2):
        small_src[2 * layer : 2 * layer + 2, 0:sb] = poles_ref[layer]
    small_src[4:6, 0:sb] = step_ref[...]
    small_src[6:8, :] = feed_ref[...]
    small_src[8:10, :] = gain_ref[...]
    small_src[10:12, :] = bias_ref[...]
    small_all[b] = small_src[...]
    pl.semaphore_wait(barrier, nch)

    shared = [s and nz % 2 == 0 for s in SHARED]
    piece_rows = [sb // 2 if s else sb for s in shared]
    fetched = [wf.at[m, 0 : (nb - 1) * piece_rows[m], :] for m in range(4)]
    blk_pairs, z_pairs, near_pairs, far_pairs = {}, {}, {}, {}

    def weight_piece(m, p, other=False):
        half = (z % 2) * piece_rows[m] if shared[m] else 0
        if other:
            half = (1 - z % 2) * piece_rows[m]
        return wf.at[m, rows_at(core * states + p * sb + half, piece_rows[m]), :]

    def fetch(m):
        half = (z % 2) * piece_rows[m] if shared[m] else 0
        src = mats[m].at[MATRICES[m][0], core, rows_at(half, piece_rows[m]), :]
        blk_pairs[m] = to_blk(lambda p: (src, weight_piece(m, b)), fetched[m])

    def relay(m):
        take(fetched[m], blk_pairs[m][1])
        near_pairs[m] = (new(), new())
        if shared[m]:
            z_pairs[m] = (new(), new())
            sent.append((fetched[m], z_pairs[m][0]))
        for p in blk_peers:
            piece = weight_piece(m, p)
            if shared[m]:
                start(piece, piece, z_pairs[m], z_pair)
            start(piece, piece, near_pairs[m], sibling)
        sent.append((fetched[m], near_pairs[m][0]))

    def relay_far(m):
        if shared[m]:
            take(fetched[m], z_pairs[m][1])
            far_pairs[m] = (new(), new())
            for p in blk_peers:
                piece = weight_piece(m, p, other=True)
                start(piece, piece, far_pairs[m], sibling)
            sent.append((fetched[m], far_pairs[m][0]))

    def split_matrix(m):
        near_done(wf.at[m, 0 : 2 * sb, :], own_slots[m])
        take(fetched[m], near_pairs[m][1])
        if shared[m]:
            take(fetched[m], far_pairs[m][1])
        scaled = MATRICES[m][1] == "out"

        def body(i, carry):
            rows = rows_of(i, 64)
            values = wf[m, rows, :]
            if scaled:
                values = values * jnp.where(i * 64 < states, 2.0, -2.0)
            wh[m, rows, :], wl[m, rows, :] = halves(values)
            return carry

        lax.fori_loop(0, 2 * states // 64, body, 0)

    def spread_in(src, dst, low, count):
        total = dst.at[0 : nb - 1, low : low + count, :]
        pair = to_blk(
            lambda p: (src.at[rows_at(p * tc + low, count), :], dst.at[b, low : low + count, :]),
            total,
        )
        return total, pair[1]

    def spread_out(src, dst, low, count):
        slot = new()
        mine = dst.at[rows_at(b * tc + low, count), :]
        near(src.at[b, low : low + count, :], mine, slot)
        total = src.at[0 : nb - 1, low : low + count, :]
        pair = to_blk(lambda p: (src.at[p, low : low + count, :], mine), total)
        return (total, pair[1]), (mine, slot)

    small_total = small_all.at[0 : nb - 1]
    small_pair = to_blk(lambda p: (small_src, small_all.at[b]), small_total)
    fetch(0)
    x_total, x_arrival = spread_in(x_hbm, xin, 0, tc)
    near_done(xloc, x_slot)

    def add_rows(i, carry):
        total, square = carry
        values = xloc[rows_of(i, 64), :].reshape(8, SUBS, fb)
        return total + jnp.sum(values, axis=0), square + jnp.sum(values * values, axis=0)

    zero_tile = jnp.zeros((SUBS, fb), F32)
    total, square = lax.fori_loop(0, tokens // 64, add_rows, (zero_tile, zero_tile))
    s0_own[...] = jnp.zeros_like(s0_own)
    s0_own[0:1, :] = jnp.sum(total, axis=0, keepdims=True)
    s0_own[1:2, :] = jnp.sum(square, axis=0, keepdims=True)
    s0_pair = to_sibling(s0_own, s0_sib)
    starts = [jnp.int32(0)]
    for i in range(seqs - 1):
        starts.append(starts[-1] + seq_ref[0, i])
    begins = starts
    ends = starts[1:] + [jnp.int32(tokens)]

    def none_in(low, size, marks, shift):
        hit = None
        for mark in marks:
            at = mark - shift - low
            inside = jnp.logical_and(at >= 0, at < size)
            hit = inside if hit is None else jnp.logical_or(hit, inside)
        return jnp.where(hit, 0.0, 1.0).astype(F32)

    sub_index = lax.broadcasted_iota(jnp.int32, (SUBS, LANES), 0)
    base = b * tc
    marks = ((begins, 0), (ends, 1))

    def fill_flags(k, carry):
        for way in range(2):
            ktab[way, k] = none_in(base + sub_index * steps + k, 1, *marks[way])
        return carry

    lax.fori_loop(0, steps, fill_flags, 0)
    whole_sub = [none_in(base + sub_index * steps, steps, *marks[way]) for way in range(2)]
    whole_chunk = [[none_in(p * tc, tc, *marks[way]) for p in range(nb)] for way in range(2)]

    take(s0_sib, s0_pair[1])
    s0_z[z] = s0_own[...] + s0_sib[...]
    s0_total = s0_z.at[0 : nz - 1]
    s0_pair = to_z(lambda p: (s0_z.at[z], s0_z.at[z]), s0_total)

    take(small_total, small_pair[1])
    state_rows = jnp.concatenate([small_all[p][0:8, 0:sb] for p in range(nb)], axis=1)

    def feature_row(row):
        return jnp.concatenate([small_all[p][row : row + 1, :] for p in range(nb)], axis=1)

    def discretize(real, imag, log_step):
        step = jnp.exp(log_step)
        magnitude = jnp.exp(real * step)
        lr = magnitude * jnp.cos(imag * step)
        li = magnitude * jnp.sin(imag * step)
        modulus = real * real + imag * imag
        fr = ((lr - 1.0) * real + li * imag) / modulus
        fi = (li * real - (lr - 1.0) * imag) / modulus
        return step, lr, li, fr, fi, modulus

    for layer in range(2):
        _, lr, li, fr, fi, _ = discretize(
            state_rows[2 * layer : 2 * layer + 1, :],
            state_rows[2 * layer + 1 : 2 * layer + 2, :],
            state_rows[4 + layer : 5 + layer, :],
        )
        power = [(lr, li)]
        size = 1
        while size < tc:
            power.append(cmul(*power[-1], *power[-1]))
            size *= 2
        at_steps = power[steps.bit_length() - 1]
        for row, value in enumerate((lr, li, fr, fi, *at_steps, *power[-1])):
            par[layer, row : row + 1, :] = value

    def wide(layer, row, group):
        part = par[layer, row : row + 1, group * LANES : (group + 1) * LANES]
        return jnp.broadcast_to(part, (SUBS, LANES))

    take(s0_total, s0_pair[1])
    s0_b[b] = jnp.sum(s0_z[...], axis=0)
    s0_total = s0_b.at[0 : nb - 1]
    s0_pair = to_blk(lambda p: (s0_b.at[b], s0_b.at[b]), s0_total)
    fetch(1)
    relay(0)

    def load(ref, g, k):
        return ref[rows_of(k, SUBS), g * LANES : (g + 1) * LANES]

    def store(ref, g, k, value):
        ref[rows_of(k, SUBS), g * LANES : (g + 1) * LANES] = value

    def unpack(ref, i):
        parts = [
            jnp.concatenate(
                [ref[j, pl.ds(i * GROUP + k, SUBS, stride=steps), :] for j in range(fl)], axis=1
            )
            for k in range(GROUP)
        ]
        return jnp.concatenate(parts, axis=0)

    def pack(ref, i, value):
        for k in range(GROUP):
            for j in range(fl):
                ref[j, pl.ds(i * GROUP + k, SUBS, stride=steps), :] = value[
                    k * SUBS : (k + 1) * SUBS, j * LANES : (j + 1) * LANES
                ]

    def recur(carry, keep, lam, pushes):
        gated = [c * keep for c in carry]
        new = []
        for g in range(ng):
            vr, vi = cmul(lam[0][g], lam[1][g], gated[g], gated[ng + g])
            new.append((vr + pushes[g], vi + pushes[ng + g]))
        return gated, [v[0] for v in new] + [v[1] for v in new]

    def scan_local(src, lam, way, reverse):
        def body(i, carry):
            k = steps - 1 - i if reverse else i
            pushes = [load(src, g, k) for g in range(2 * ng)]
            return tuple(recur(carry, ktab[way, k], lam, pushes)[1])

        zero = jnp.zeros((SUBS, LANES), F32)
        return lax.fori_loop(0, steps, body, (zero,) * (2 * ng), unroll=4)

    def prefix(last, power, way, reverse):
        out = []
        for g in range(ng):
            sr, si = last[g], last[ng + g]
            ar, ai = power[0][g] * whole_sub[way], power[1][g] * whole_sub[way]
            for d in (1, 2, 4):
                shift = SUBS - d if reverse else d
                ok = sub_index < SUBS - d if reverse else sub_index >= d
                tr, ti = cmul(ar, ai, pltpu.roll(sr, shift, 0), pltpu.roll(si, shift, 0))
                br, bi = cmul(ar, ai, pltpu.roll(ar, shift, 0), pltpu.roll(ai, shift, 0))
                sr, si = jnp.where(ok, sr + tr, sr), jnp.where(ok, si + ti, si)
                ar, ai = jnp.where(ok, br, ar), jnp.where(ok, bi, ai)
            out.append((sr, si, ar, ai))
        return out

    carry_pairs = {}

    def send_carry(e, pre, reverse):
        row = 0 if reverse else SUBS - 1
        for g in range(ng):
            cols = slice(g * LANES, (g + 1) * LANES)
            for part in range(2):
                cy_src[e, part : part + 1, cols] = pre[g][part][row : row + 1, :]
                cy_buf[e, b, part : part + 1, cols] = pre[g][part][row : row + 1, :]
        carry_pairs[e] = to_blk(
            lambda p: (cy_src.at[e], cy_buf.at[e, b]), cy_buf.at[e, 0 : nb - 1]
        )

    def take_carry(e, pre, layer, way, reverse, sign):
        take(cy_buf.at[e, 0 : nb - 1], carry_pairs[e][1])
        ar, ai = par[layer, 6:7, :], sign * par[layer, 7:8, :]
        zero = jnp.zeros((1, states), F32)
        cr, ci, er, ei = zero, zero, zero, zero
        for p in reversed(range(nb)) if reverse else range(nb):
            er, ei = jnp.where(b == p, cr, er), jnp.where(b == p, ci, ei)
            tr, ti = cmul(ar, ai, cr, ci)
            keep = whole_chunk[way][p]
            cr = cy_buf[e, p, 0:1, :] + keep * tr
            ci = cy_buf[e, p, 1:2, :] + keep * ti
        shift = SUBS - 1 if reverse else 1
        first = sub_index == (SUBS - 1 if reverse else 0)
        carry_r, carry_i = [], []
        for g in range(ng):
            cols = slice(g * LANES, (g + 1) * LANES)
            wr = jnp.broadcast_to(er[:, cols], (SUBS, LANES))
            wi = jnp.broadcast_to(ei[:, cols], (SUBS, LANES))
            sr, si, dr, di = (pltpu.roll(v, shift, 0) for v in pre[g])
            tr, ti = cmul(dr, di, wr, wi)
            carry_r.append(jnp.where(first, wr, sr + tr))
            carry_i.append(jnp.where(first, wi, si + ti))
        return tuple(carry_r + carry_i)

    def forward_states(layer, carry, way, reverse, lam):
        scale = [[wide(layer, 2 + part, g) for g in range(ng)] for part in range(2)]
        src, dst = raw.at[layer], xs.at[layer]

        def body(i, carry):
            k = steps - 1 - i if reverse else i
            pushes = [load(src, g, k) for g in range(2 * ng)]
            _, new = recur(carry, ktab[way, k], lam, pushes)
            for g in range(ng):
                vr, vi = cmul(scale[0][g], scale[1][g], new[g], new[ng + g])
                store(dst, g, k, vr)
                store(dst, ng + g, k, vi)
            return tuple(new)

        lax.fori_loop(0, steps, body, carry, unroll=4)

    def adjoint_states(layer, carry, way, reverse, lam):
        scale = [[wide(layer, 2 + part, g) for g in range(ng)] for part in range(2)]
        zero = jnp.zeros((SUBS, LANES), F32)

        def body(i, loop):
            carry, sums = loop
            k = steps - 1 - i if reverse else i
            pushes = [load(seed, g, k) for g in range(2 * ng)]
            gated, new = recur(carry, ktab[way, k], lam, pushes)
            sums = list(sums)
            for g in range(ng):
                xr, xi = load(xs.at[layer], g, k), load(xs.at[layer], ng + g, k)
                ur, ui = load(raw.at[layer], g, k), load(raw.at[layer], ng + g, k)
                pr, pi = gated[g], gated[ng + g]
                vr, vi = new[g], new[ng + g]
                sums[g] += pr * xr + pi * xi
                sums[ng + g] += pi * xr - pr * xi
                sums[2 * ng + g] += vr * ur + vi * ui
                sums[3 * ng + g] += vi * ur - vr * ui
                store(gadj, g, k, scale[0][g] * vr + scale[1][g] * vi)
                store(gadj, ng + g, k, scale[0][g] * vi - scale[1][g] * vr)
            return tuple(new), tuple(sums)

        return lax.fori_loop(0, steps, body, (carry, (zero,) * (4 * ng)), unroll=4)[1]

    tile = 256 if tc % 256 == 0 else tc

    def to_groups(left, m, dst):
        def body(i, carry):
            rows = rows_of(i, tile)
            value = product(
                (left[0][rows, :], left[1][rows, :]), (wh[m], wl[m]), "nt"
            )
            dst[rows, :] = value
            return carry

        lax.fori_loop(0, tc // tile, body, 0)

    def from_groups(src, m, dst):
        def body(i, carry):
            rows = rows_of(i, tile)
            dst[rows, :] = product(halves(src[rows, :]), (wh[m], wl[m]), "nn")
            return carry

        lax.fori_loop(0, tc // tile, body, 0)

    def weight_grad(src, right, m, scaled):
        def body(pair, carry):
            left = src[:, pl.ds(pl.multiple_of(pair * 2 * LANES, 2 * LANES), 2 * LANES)]
            value = product(halves(left), (right[0][...], right[1][...]), "tn")
            for half in range(2):
                g = 2 * pair + half
                part = value[half * LANES : (half + 1) * LANES, :]
                if scaled:
                    part = part * jnp.where(g < ng, 2.0, -2.0)
                gl[m, rows_of(g, LANES), :] = part
            return carry

        lax.fori_loop(0, ng, body, 0)

    stats_pairs = {}

    def stats_start(i, first, second):
        for n, value in enumerate((first, second)):
            for j in range(fl):
                row = n * fl + j
                st_own[i, row : row + 1, :] = value[:, j * LANES : (j + 1) * LANES]
        take(st_sib.at[i], to_sibling(st_own.at[i], st_sib.at[i])[1])
        both = st_own[i] + st_sib[i]
        st_src[i] = both
        st_buf[i, chip] = both
        stats_pairs[i] = (new(), new())
        over_chips(lambda dev: start(st_src.at[i], st_buf.at[i, chip], stats_pairs[i], dev))
        sent.append((st_buf.at[i, 0 : nch - 1], stats_pairs[i][0]))

    def stats_end(i):
        take(st_buf.at[i, 0 : nch - 1], stats_pairs[i][1])
        st_tot[i] = jnp.sum(st_buf[i], axis=0)
        return [
            jnp.concatenate(
                [st_tot[i, n * fl + j : n * fl + j + 1, :] for j in range(fl)], axis=1
            )
            for n in range(2)
        ]

    def to_row(value):
        return jnp.sum(value, axis=0, keepdims=True)

    def eights(value):
        return jnp.sum(value.reshape(value.shape[0] // SUBS, SUBS, feats), axis=0)

    gpair = {}
    pr = psum.shape[1] // nz

    def core_rows(part):
        return rows_at(part * states, states)

    def grad_core(m):
        gpair["core", m] = to_sibling(gl.at[m, core_rows(1 - core), :], gsib.at[m])

    def grad_add(m):
        take(gsib.at[m], gpair["core", m][1])

        def body(i, carry):
            gsib[m, rows_of(i, 32), :] += gl[m, rows_at(core * states + i * 32, 32), :]
            return carry

        lax.fori_loop(0, states // 32, body, 0)

    def grad_blk(m):
        gpair["blk", m] = to_blk(
            lambda p: (gsib.at[m, rows_at(p * sb, sb), :], gblk.at[m, b]),
            gblk.at[m, 0 : nb - 1],
        )

    def grad_z(m):
        take(gblk.at[m, 0 : nb - 1], gpair["blk", m][1])

        def body(i, carry):
            value = gsib[m, rows_at(b * sb + i * 8, 8), :]
            for p in blk_peers:
                value += gblk[m, p, rows_of(i, 8), :]
            for j in range(fl):
                psum[m, rows_at(j * sb + i * 8, 8), :] = value[:, j * LANES : (j + 1) * LANES]
            return carry

        lax.fori_loop(0, sb // 8, body, 0)
        gpair["z", m] = to_z(
            lambda p: (psum.at[m, rows_of(p, pr), :], gz.at[m, z]), gz.at[m, 0 : nz - 1]
        )

    def grad_gather(m):
        take(gz.at[m, 0 : nz - 1], gpair["z", m][1])
        mine = rows_of(z, pr)
        value = psum[m, mine, :]
        for p in range(nz):
            value += jnp.where(z == p, 0.0, gz[m, p])
        fin[m, core, mine, :] = value
        piece = fin.at[m, core, mine, :]
        gpair["all", m] = to_z(lambda p: (piece, piece), fin.at[m, core, 0 : (nz - 1) * pr, :])

    def grad_share(m):
        take(fin.at[m, core, 0 : (nz - 1) * pr, :], gpair["all", m][1])
        gpair["share", m] = to_sibling(fin.at[m, core], fin.at[m, core])

    stores = []

    def grad_store(m):
        take(fin.at[m, 1 - core], gpair["share", m][1])
        layer, kind = MATRICES[m]
        dst = (gin_hbm if kind == "in" else gout_hbm).at[layer]
        slot = new()
        for part in range(2):
            for j in range(fl):
                near(
                    fin.at[m, part, j * sb : (j + 1) * sb, :],
                    dst.at[part, :, j * LANES : (j + 1) * LANES],
                    slot,
                )
        stores.append((dst, slot))

    hc = tc // 2
    relay_far(0)
    split_matrix(0)
    take(s0_total, s0_pair[1])
    sums = [
        jnp.concatenate([s0_b[p][n : n + 1, :] for p in range(nb)], axis=1) for n in range(2)
    ]
    near_done(xin.at[b], h_slot)
    take(x_total, x_arrival)

    scales = []
    small_rows = GROUP * SUBS
    cot_parts = []

    for layer in range(2):
        way, reverse = layer, layer == 1
        mean = sums[0] / token_count
        rstd = lax.rsqrt(sums[1] / token_count - mean * mean + EPSILON)
        gain, bias, feed = (feature_row(row + layer) for row in (8, 10, 6))
        scales.append((rstd, gain, bias, feed))

        def normalize(i, carry, layer=layer, mean=mean, rstd=rstd, gain=gain, bias=bias):
            rows = rows_of(i, small_rows)
            if layer == 0:
                value = unpack(xin, i)
                hid[0, rows, :] = value
            else:
                value = hid[1, rows, :]
            unit = (value - mean) * rstd
            zn[layer, rows, :] = unit
            zh[layer, rows, :], zl[layer, rows, :] = halves(gain * unit + bias)
            return carry

        lax.fori_loop(0, tc // small_rows, normalize, 0)
        to_groups((zh.at[layer], zl.at[layer]), 2 * layer, raw.at[layer])
        if layer == 1:
            relay(3)
        lam = [[wide(layer, part, g) for g in range(ng)] for part in range(2)]
        power = [[wide(layer, 4 + part, g) for g in range(ng)] for part in range(2)]
        last = scan_local(raw.at[layer], lam, way, reverse)
        pre = prefix(last, power, way, reverse)
        send_carry(layer, pre, reverse)
        if layer == 0:
            fetch(2)
            relay(1)
            relay_far(1)
            split_matrix(1)
        else:
            cot_parts.append(spread_in(cot_hbm, cotb, hc, tc - hc))
            relay_far(3)
            split_matrix(3)
        carry = take_carry(layer, pre, layer, way, reverse, 1.0)
        forward_states(layer, carry, way, reverse, lam)
        if layer == 0:
            relay(2)
        from_groups(xs.at[layer], 2 * layer + 1, ybuf)

        def activate(i, carry, layer=layer, gain=gain, bias=bias, feed=feed):
            rows = rows_of(i, small_rows)
            mixed = ybuf[rows, :] + feed * (gain * zn[layer, rows, :] + bias)
            below = 0.5 * (1.0 + lax.erf(mixed * 0.7071067811865476))
            density = 0.3989422804014327 * jnp.exp(-0.5 * mixed * mixed)
            gate = 1.0 / (1.0 + jnp.exp(-mixed))
            gelu = mixed * below
            value = hid[layer, rows, :] + gelu * gate
            if layer == 0:
                hid[1, rows, :] = value
            else:
                pack(outb, i, value)
            actp[layer, rows, :] = (below + mixed * density) * gate + gelu * gate * (1.0 - gate)
            return carry[0] + eights(value), carry[1] + eights(value * value)

        zero = jnp.zeros((SUBS, feats), F32)
        parts = lax.fori_loop(0, tc // small_rows, activate, (zero, zero))
        if layer == 0:
            stats_start(0, to_row(parts[0]), to_row(parts[1]))
            fetch(3)
            cot_parts.append(spread_in(cot_hbm, cotb, 0, hc))
            relay_far(2)
            split_matrix(2)
            sums = stats_end(0)

    near_done(cotb.at[b], c_slot)
    for part in cot_parts:
        take(*part)
    outs = []
    for layer in (1, 0):
        way, reverse = 1 - layer, layer == 0
        rstd, gain, bias, feed = scales[layer]
        upper = dh.at[layer]

        def mixed_grad(i, carry, layer=layer, gain=gain, bias=bias, upper=upper):
            rows = rows_of(i, small_rows)
            value = unpack(cotb, i) if layer == 1 else upper[rows, :]
            if layer == 1:
                upper[rows, :] = value
            value = value * actp[layer, rows, :]
            dyf[rows, :] = value
            dyh[rows, :], dyl[rows, :] = halves(value)
            return carry + eights(value * (gain * zn[layer, rows, :] + bias))

        zero = jnp.zeros((SUBS, feats), F32)
        feed_grad = to_row(lax.fori_loop(0, tc // small_rows, mixed_grad, zero))
        to_groups((dyh, dyl), 2 * layer + 1, seed)
        lam = [
            [wide(layer, 0, g) for g in range(ng)],
            [-wide(layer, 1, g) for g in range(ng)],
        ]
        power = [
            [wide(layer, 4, g) for g in range(ng)],
            [-wide(layer, 5, g) for g in range(ng)],
        ]
        last = scan_local(seed, lam, way, reverse)
        pre = prefix(last, power, way, reverse)
        send_carry(2 + layer, pre, reverse)
        low = 0 if layer == 1 else hc
        outs.append(spread_out(outb, out_hbm, low, hc))
        weight_grad(xs.at[layer], (dyh, dyl), 2 * layer + 1, True)
        grad_core(2 * layer + 1)
        carry = take_carry(2 + layer, pre, layer, way, reverse, -1.0)
        state_sums = adjoint_states(layer, carry, way, reverse, lam)
        if layer == 0:
            grad_add(2)
            grad_z(3)
        grad_add(2 * layer + 1)
        from_groups(gadj, 2 * layer, dz)

        def dz_sums(i, carry, layer=layer, feed=feed):
            rows = rows_of(i, small_rows)
            value = dz[rows, :] + feed * dyf[rows, :]
            dz[rows, :] = value
            return carry[0] + eights(value), carry[1] + eights(value * zn[layer, rows, :])

        parts = lax.fori_loop(0, tc // small_rows, dz_sums, (zero, zero))
        stats_start(1 + layer, to_row(parts[0]), to_row(parts[1]))
        if layer == 1:
            grad_blk(3)
        else:
            grad_blk(2)
            grad_blk(1)
        weight_grad(gadj, (zh.at[layer], zl.at[layer]), 2 * layer, False)
        grad_core(2 * layer)
        for p in range(nb):
            q_own[p, layer : layer + 1, :] = feed_grad[:, p * fb : (p + 1) * fb]
        for n in range(4):
            vector = jnp.concatenate(
                [to_row(state_sums[n * ng + g]) for g in range(ng)], axis=1
            )
            row = 2 + 4 * layer + n
            for p in range(nb):
                q_own[p, row : row + 1, 0:sb] = vector[:, p * sb : (p + 1) * sb]
        if layer == 0:
            q_pair = to_sibling(q_own, q_sib)
            grad_gather(3)
            grad_add(0)
            grad_blk(0)
            take(q_sib, q_pair[1])
            q_sib[...] += q_own[...]
            q_total = q_blk.at[0 : nb - 1]
            q_pair = to_blk(lambda p: (q_sib.at[p], q_blk.at[b]), q_total)
        bias_grad, gain_grad = stats_end(1 + layer)

        def hidden_grad(
            i, carry, layer=layer, rstd=rstd, gain=gain, bias_grad=bias_grad, gain_grad=gain_grad, upper=upper
        ):
            rows = rows_of(i, small_rows)
            inner = (
                dz[rows, :]
                - bias_grad / token_count
                - zn[layer, rows, :] * (gain_grad / token_count)
            )
            value = upper[rows, :] + gain * rstd * inner
            if layer == 1:
                dh[0, rows, :] = value
            else:
                pack(gxb, i, value)
            return carry

        lax.fori_loop(0, tc // small_rows, hidden_grad, 0)
        gsmall_ref[2 + layer : 3 + layer, :] = st_tot[1 + layer, pl.ds(fl + b, 1), :]
        gsmall_ref[4 + layer : 5 + layer, :] = st_tot[1 + layer, pl.ds(b, 1), :]

    outs.append(spread_out(gxb, gx_hbm, 0, tc))
    grad_share(3)
    grad_z(2)
    grad_store(3)
    grad_z(1)
    grad_gather(2)
    grad_share(2)
    grad_gather(1)
    grad_store(2)
    grad_share(1)
    grad_z(0)
    take(q_total, q_pair[1])
    value = q_sib[b]
    for p in blk_peers:
        value += q_blk[p]
    q_z[z] = value
    q_total = q_z.at[0 : nz - 1]
    q_pair = to_z(lambda p: (q_z.at[z], q_z.at[z]), q_total)
    grad_store(1)
    grad_gather(0)
    take(q_total, q_pair[1])
    small = jnp.sum(q_z[...], axis=0)
    gsmall_ref[0:2, :] = small[0:2, :]
    for layer in range(2):
        real = poles_ref[layer, 0:1, :]
        imag = poles_ref[layer, 1:2, :]
        step, lr, li, fr, fi, modulus = discretize(real, imag, step_ref[layer : layer + 1, :])
        lgr, lgi, fgr, fgi = (
            small[2 + 4 * layer + n : 3 + 4 * layer + n, 0:sb] for n in range(4)
        )
        qr = (real * fgr - imag * fgi) / modulus
        qi = (real * fgi + imag * fgr) / modulus
        tr, ti = lgr + qr, lgi + qi
        wr = lr * tr + li * ti
        wi = lr * ti - li * tr
        row = 6 + 2 * layer
        gsmall_ref[row : row + 1, 0:sb] = step * wr - (fr * qr + fi * qi)
        gsmall_ref[row + 1 : row + 2, 0:sb] = step * wi - (fr * qi - fi * qr)
        gsmall_ref[10 + layer : 11 + layer, 0:sb] = step * (real * wr + imag * wi)
    grad_share(0)
    for arrival, mine in outs:
        take(*arrival)
        near_done(*mine)
    grad_store(0)
    for ref, slot in stores:
        near_done(ref, slot)
    for ref, slot in sent:
        take(ref, slot)


def finish(
    out_in, gx_in, gin_in, gout_in, small_in, out, gx, gpoles, gstep, gin, gout, gfeed, ggain, gbias, *scratch
):
    sem = scratch[-1]
    chunks = []
    for n, (src, dst, buf) in enumerate(zip((out_in, gx_in, gin_in, gout_in), (out, gx, gin, gout), scratch)):
        for half in range(2):
            if n < 2:
                rows = src.shape[0] // 2
                at = pl.ds(half * rows, rows)
            else:
                at = half
            chunks.append((src.at[at], buf.at[at], dst.at[at], sem.at[0, 2 * n + half], sem.at[1, 2 * n + half]))
    for src, buf, _, arrived, _ in chunks:
        pltpu.make_async_copy(src, buf, arrived).start()
    sb = gstep.shape[1]
    gfeed[...] = small_in[0:2, :]
    ggain[...] = small_in[2:4, :]
    gbias[...] = small_in[4:6, :]
    for layer in range(2):
        gpoles[layer] = small_in[6 + 2 * layer : 8 + 2 * layer, 0:sb]
    gstep[...] = small_in[10:12, 0:sb]
    for src, buf, dst, arrived, written in chunks:
        pltpu.make_async_copy(src, buf, arrived).wait()
        pltpu.make_async_copy(buf, dst, written).start()
    for _, buf, dst, _, written in chunks:
        pltpu.make_async_copy(buf, dst, written).wait()


def local(mesh, *args):
    inputs, seq_lengths = args[0], args[1]
    nb, nr = mesh.shape["blk"], mesh.shape["row"]
    nz = nr // 2
    tokens, fb = inputs.shape
    sb = args[2].shape[2]
    states, feats = sb * nb, fb * nb
    assert seq_lengths.shape[0] == 1 and nr % 2 == 0
    assert fb == LANES and states % LANES == 0 and 2 * feats == SUBS * LANES
    assert tokens % (nb * SUBS * SUBS) == 0 and sb % 16 == 0 and states % 64 == 0
    tc = tokens // nb
    steps = tc // SUBS
    assert steps & (steps - 1) == 0
    nch = nb * nz
    fl = feats // LANES
    piece = -(-fl * sb // (nz * SUBS)) * SUBS
    sizes = (nb, nz, seq_lengths.shape[1], tokens, feats, states, tokens * nr)
    vmem = lambda *shape: pltpu.VMEM(shape, F32)
    half = lambda *shape: pltpu.VMEM(shape, BF16)
    scratch = [
        vmem(tokens, fb),
        vmem(16, fb),
        vmem(nb, 16, fb),
        vmem(4, 2 * states, feats),
        half(4, 2 * states, feats),
        half(4, 2 * states, feats),
        vmem(2, 8, states),
        vmem(2, steps, SUBS, LANES),
        vmem(nb, tc, fb),
        vmem(2, tc, feats),
        vmem(nb, tc, fb),
        vmem(nb, tc, fb),
        vmem(nb, tc, fb),
        vmem(2, tc, feats),
        half(2, tc, feats),
        half(2, tc, feats),
        vmem(2, tc, 2 * states),
        vmem(2, tc, 2 * states),
        vmem(tc, feats),
        vmem(2, tc, feats),
        vmem(tc, feats),
        half(tc, feats),
        half(tc, feats),
        vmem(tc, 2 * states),
        vmem(tc, 2 * states),
        vmem(tc, feats),
        vmem(2, tc, feats),
        vmem(4, 2 * states, feats),
        vmem(4, states, feats),
        vmem(4, nb, sb, feats),
        vmem(4, nz * piece, LANES),
        vmem(4, nz, piece, LANES),
        vmem(4, 2, nz * piece, LANES),
        vmem(8, fb),
        vmem(8, fb),
        vmem(nz, 8, fb),
        vmem(nb, 8, fb),
        vmem(3, 8, LANES),
        vmem(3, 8, LANES),
        vmem(3, 8, LANES),
        vmem(3, nch, 8, LANES),
        vmem(3, 8, LANES),
        vmem(4, 8, states),
        vmem(4, nb, 8, states),
        vmem(nb, 16, fb),
        vmem(nb, 16, fb),
        vmem(nb, 16, fb),
        vmem(nz, 16, fb),
        pltpu.SemaphoreType.DMA((SEMAPHORES,)),
    ]
    shaped = lambda like: jax.ShapeDtypeStruct(like.shape, like.dtype)
    anywhere = pl.BlockSpec(memory_space=pl.ANY)
    fast = pl.BlockSpec(memory_space=pltpu.VMEM)
    raw = pl.pallas_call(
        functools.partial(kernel, sizes),
        name="s5_layers",
        out_shape=tuple(shaped(args[i]) for i in (0, 0, 4, 5)) + (jax.ShapeDtypeStruct((16, fb), F32),),
        in_specs=[
            anywhere,
            pl.BlockSpec(memory_space=pltpu.SMEM),
            fast,
            fast,
            anywhere,
            anywhere,
            fast,
            fast,
            fast,
            anywhere,
        ],
        out_specs=(anywhere,) * 4 + (fast,),
        scratch_shapes=scratch,
        compiler_params=pltpu.CompilerParams(
            collective_id=0, has_side_effects=True, vmem_limit_bytes=60 << 20
        ),
    )(*args)
    return pl.pallas_call(
        finish,
        name="results",
        out_shape=tuple(shaped(args[i]) for i in (0, 0, 2, 3, 4, 5, 6, 7, 8)),
        in_specs=[anywhere] * 4 + [fast],
        out_specs=(anywhere, anywhere, fast, fast, anywhere, anywhere, fast, fast, fast),
        scratch_shapes=[pltpu.VMEM(args[i].shape, F32) for i in (0, 0, 4, 5)]
        + [pltpu.SemaphoreType.DMA((2, 8))],
        compiler_params=pltpu.CompilerParams(vmem_limit_bytes=60 << 20),
    )(*raw)


def solution(mesh):
    by_state = (P(None, None, "blk"), P(None, "blk"), P(None, None, "blk", None), P(None, None, "blk", None))
    by_feature = (P(None, "blk"),) * 3
    tokens = P("row", "blk")
    return jax.shard_map(
        functools.partial(local, mesh),
        mesh=mesh,
        in_specs=(tokens, P("row", None), *by_state, *by_feature, tokens),
        out_specs=(tokens, tokens, *by_state, *by_feature),
        check_vma=False,
    )
```

```python
import functools

import jax
import jax.numpy as jnp
from jax import lax
from jax.experimental import pallas as pl
from jax.experimental.pallas import tpu as pltpu
from jax.sharding import PartitionSpec as P


EPSILON = 1e-05
LANES = 128
SUBS = 8
GROUP = 4
MESH = pl.DeviceIdType.MESH
F32 = jnp.float32
BF16 = jnp.bfloat16
MATRICES = ((0, "in"), (0, "out"), (1, "in"), (1, "out"))
SHARED = (True, False, True, True)
HALVED = (False, True, True, False)
SEMAPHORES = 136
DIMS = {
    "nt": (((1,), (1,)), ((), ())),
    "nn": (((1,), (0,)), ((), ())),
    "tn": (((0,), (0,)), ((), ())),
}


def halves(values):
    high = values.astype(BF16)
    return high, (values - high.astype(F32)).astype(BF16)


def product(left, right, form):
    def one(a, b):
        return lax.dot_general(a, b, DIMS[form], preferred_element_type=F32)

    return one(left[0], right[0]) + (one(left[0], right[1]) + one(left[1], right[0]))


def cmul(ar, ai, br, bi):
    return ar * br - ai * bi, ar * bi + ai * br


def kernel(
    sizes,
    x_hbm,
    seq_ref,
    poles_ref,
    step_ref,
    in_hbm,
    out_mat_hbm,
    feed_ref,
    gain_ref,
    bias_ref,
    cot_hbm,
    out_hbm,
    gx_hbm,
    gin_hbm,
    gout_hbm,
    gsmall_ref,
    xloc,
    small_src,
    small_all,
    wf,
    wh,
    wl,
    par,
    ktab,
    xin,
    hid,
    cotb,
    outb,
    gxb,
    zn,
    zh,
    zl,
    raw,
    xs,
    ybuf,
    actp,
    dyf,
    dyh,
    dyl,
    seed,
    gadj,
    dz,
    dh,
    gsib,
    gpr,
    gblk,
    psum,
    gz,
    fin,
    s0_own,
    s0_sib,
    s0_z,
    s0_b,
    st_own,
    st_sib,
    st_src,
    st_buf,
    st_tot,
    cy_src,
    cy_buf,
    q_own,
    q_sib,
    q_blk,
    q_z,
    sem,
):
    nb, nz, seqs, tokens, feats, states, token_count = sizes
    nch = nb * nz
    tc, fb, sb = tokens // nb, feats // nb, states // nb
    steps = tc // SUBS
    ng = states // LANES
    fl = feats // LANES
    b = lax.axis_index("blk")
    r = lax.axis_index("row")
    core = r % 2
    z = r // 2
    chip = b * nz + z
    sibling = (b, z * 2 + 1 - core)
    z_pair = (b, (z + 1 - 2 * (z % 2)) * 2 + core)
    blk_peers = [((b + k) % nb) for k in range(1, nb)]

    def several(count, body):
        if count <= 16:
            for k in range(1, count):
                body(k)
        else:

            def step(k, carry):
                body(k)
                return carry

            lax.fori_loop(1, count, step, 0)

    def over_z(body):
        def peer(k):
            q = (z + k) % nz
            body(q, (b, q * 2 + core))

        several(nz, peer)

    def over_chips(body):
        def peer(k):
            q = (chip + k) % nch
            body((q // nz, (q % nz) * 2 + core))

        several(nch, peer)

    barrier = pltpu.get_barrier_semaphore()
    pl.semaphore_signal(barrier, 1, device_id=sibling, device_id_type=MESH)
    over_chips(
        lambda dev: pl.semaphore_signal(barrier, 1, device_id=dev, device_id_type=MESH)
    )

    slots = iter(range(SEMAPHORES))
    sent = []

    def new():
        return next(slots)

    def start(src, dst, pair, dev):
        pltpu.make_async_remote_copy(
            src, dst, sem.at[pair[0]], sem.at[pair[1]], device_id=dev, device_id_type=MESH
        ).start()

    def take(ref, slot):
        pltpu.make_async_copy(ref, ref, sem.at[slot]).wait()

    def near(src, dst, slot):
        pltpu.make_async_copy(src, dst, sem.at[slot]).start()

    def near_done(ref, slot):
        pltpu.make_async_copy(ref, ref, sem.at[slot]).wait()

    def rows_of(i, size):
        return pl.ds(pl.multiple_of(i * size, size), size)

    def rows_at(i, size):
        return pl.ds(pl.multiple_of(i, 8), size)

    def to_sibling(src, dst, total=None):
        pair = (new(), new())
        start(src, dst, pair, sibling)
        sent.append((src, pair[0]))
        return pair

    def to_blk(make, total):
        pair = (new(), new())
        for p in blk_peers:
            start(*make(p), pair, (p, r))
        sent.append((total, pair[0]))
        return pair

    def to_z(make, total):
        pair = (new(), new())
        over_z(lambda p, dev: start(*make(p), pair, dev))
        sent.append((total, pair[0]))
        return pair

    my_cols = rows_of(b, fb)
    mats = [in_hbm if kind == "in" else out_mat_hbm for _, kind in MATRICES]
    x_slot, h_slot, c_slot = new(), new(), new()
    own_slots = [new() for _ in MATRICES]
    near(x_hbm, xloc, x_slot)
    near(x_hbm.at[rows_of(b, tc), :], xin.at[b], h_slot)
    near(cot_hbm.at[rows_of(b, tc), :], cotb.at[b], c_slot)
    for m, (layer, _) in enumerate(MATRICES):
        for part in range(2):
            near(
                mats[m].at[layer, part],
                wf.at[m, rows_at(part * states + b * sb, sb), :],
                own_slots[m],
            )

    small_src[...] = jnp.zeros_like(small_src)
    for layer in range(2):
        small_src[2 * layer : 2 * layer + 2, 0:sb] = poles_ref[layer]
    small_src[4:6, 0:sb] = step_ref[...]
    small_src[6:8, :] = feed_ref[...]
    small_src[8:10, :] = gain_ref[...]
    small_src[10:12, :] = bias_ref[...]
    small_all[b] = small_src[...]
    pl.semaphore_wait(barrier, nch)

    shared = [s and nz % 2 == 0 for s in SHARED]
    piece_rows = [sb // 2 if s else sb for s in shared]
    fetched = [wf.at[m, 0 : (nb - 1) * piece_rows[m], :] for m in range(4)]
    blk_pairs, z_pairs, near_pairs, far_pairs = {}, {}, {}, {}

    def weight_piece(m, p, other=False):
        half = (z % 2) * piece_rows[m] if shared[m] else 0
        if other:
            half = (1 - z % 2) * piece_rows[m]
        return wf.at[m, rows_at(core * states + p * sb + half, piece_rows[m]), :]

    def fetch(m):
        half = (z % 2) * piece_rows[m] if shared[m] else 0
        src = mats[m].at[MATRICES[m][0], core, rows_at(half, piece_rows[m]), :]
        blk_pairs[m] = to_blk(lambda p: (src, weight_piece(m, b)), fetched[m])

    def relay(m):
        take(fetched[m], blk_pairs[m][1])
        near_pairs[m] = (new(), new())
        if shared[m]:
            z_pairs[m] = (new(), new())
            sent.append((fetched[m], z_pairs[m][0]))
        for p in blk_peers:
            piece = weight_piece(m, p)
            if shared[m]:
                start(piece, piece, z_pairs[m], z_pair)
            start(piece, piece, near_pairs[m], sibling)
        sent.append((fetched[m], near_pairs[m][0]))

    def relay_far(m):
        if shared[m]:
            take(fetched[m], z_pairs[m][1])
            far_pairs[m] = (new(), new())
            for p in blk_peers:
                piece = weight_piece(m, p, other=True)
                start(piece, piece, far_pairs[m], sibling)
            sent.append((fetched[m], far_pairs[m][0]))

    def split_matrix(m):
        near_done(wf.at[m, 0 : 2 * sb, :], own_slots[m])
        take(fetched[m], near_pairs[m][1])
        if shared[m]:
            take(fetched[m], far_pairs[m][1])
        scaled = MATRICES[m][1] == "out"

        def body(i, carry):
            rows = rows_of(i, 64)
            values = wf[m, rows, :]
            if scaled:
                values = values * jnp.where(i * 64 < states, 2.0, -2.0)
            wh[m, rows, :], wl[m, rows, :] = halves(values)
            return carry

        lax.fori_loop(0, 2 * states // 64, body, 0)

    def spread_in(src, dst, low, count):
        total = dst.at[0 : nb - 1, low : low + count, :]
        pair = to_blk(
            lambda p: (src.at[rows_at(p * tc + low, count), :], dst.at[b, low : low + count, :]),
            total,
        )
        return total, pair[1]

    def spread_out(src, dst, low, count):
        slot = new()
        mine = dst.at[rows_at(b * tc + low, count), :]
        near(src.at[b, low : low + count, :], mine, slot)
        total = src.at[0 : nb - 1, low : low + count, :]
        pair = to_blk(lambda p: (src.at[p, low : low + count, :], mine), total)
        return (total, pair[1]), (mine, slot)

    small_total = small_all.at[0 : nb - 1]
    small_pair = to_blk(lambda p: (small_src, small_all.at[b]), small_total)
    fetch(0)
    x_total, x_arrival = spread_in(x_hbm, xin, 0, tc)
    near_done(xloc, x_slot)

    def add_rows(i, carry):
        total, square = carry
        values = xloc[rows_of(i, 64), :].reshape(8, SUBS, fb)
        return total + jnp.sum(values, axis=0), square + jnp.sum(values * values, axis=0)

    zero_tile = jnp.zeros((SUBS, fb), F32)
    total, square = lax.fori_loop(0, tokens // 64, add_rows, (zero_tile, zero_tile))
    s0_own[...] = jnp.zeros_like(s0_own)
    s0_own[0:1, :] = jnp.sum(total, axis=0, keepdims=True)
    s0_own[1:2, :] = jnp.sum(square, axis=0, keepdims=True)
    s0_pair = to_sibling(s0_own, s0_sib)
    starts = [jnp.int32(0)]
    for i in range(seqs - 1):
        starts.append(starts[-1] + seq_ref[0, i])
    begins = starts
    ends = starts[1:] + [jnp.int32(tokens)]

    def none_in(low, size, marks, shift):
        hit = None
        for mark in marks:
            at = mark - shift - low
            inside = jnp.logical_and(at >= 0, at < size)
            hit = inside if hit is None else jnp.logical_or(hit, inside)
        return jnp.where(hit, 0.0, 1.0).astype(F32)

    sub_index = lax.broadcasted_iota(jnp.int32, (SUBS, LANES), 0)
    base = b * tc
    marks = ((begins, 0), (ends, 1))

    def fill_flags(k, carry):
        for way in range(2):
            ktab[way, k] = none_in(base + sub_index * steps + k, 1, *marks[way])
        return carry

    lax.fori_loop(0, steps, fill_flags, 0)
    whole_sub = [none_in(base + sub_index * steps, steps, *marks[way]) for way in range(2)]
    whole_chunk = [[none_in(p * tc, tc, *marks[way]) for p in range(nb)] for way in range(2)]

    take(s0_sib, s0_pair[1])
    s0_z[z] = s0_own[...] + s0_sib[...]
    s0_total = s0_z.at[0 : nz - 1]
    s0_pair = to_z(lambda p: (s0_z.at[z], s0_z.at[z]), s0_total)

    take(small_total, small_pair[1])
    state_rows = jnp.concatenate([small_all[p][0:8, 0:sb] for p in range(nb)], axis=1)

    def feature_row(row):
        return jnp.concatenate([small_all[p][row : row + 1, :] for p in range(nb)], axis=1)

    def discretize(real, imag, log_step):
        step = jnp.exp(log_step)
        magnitude = jnp.exp(real * step)
        lr = magnitude * jnp.cos(imag * step)
        li = magnitude * jnp.sin(imag * step)
        modulus = real * real + imag * imag
        fr = ((lr - 1.0) * real + li * imag) / modulus
        fi = (li * real - (lr - 1.0) * imag) / modulus
        return step, lr, li, fr, fi, modulus

    for layer in range(2):
        _, lr, li, fr, fi, _ = discretize(
            state_rows[2 * layer : 2 * layer + 1, :],
            state_rows[2 * layer + 1 : 2 * layer + 2, :],
            state_rows[4 + layer : 5 + layer, :],
        )
        power = [(lr, li)]
        size = 1
        while size < tc:
            power.append(cmul(*power[-1], *power[-1]))
            size *= 2
        at_steps = power[steps.bit_length() - 1]
        for row, value in enumerate((lr, li, fr, fi, *at_steps, *power[-1])):
            par[layer, row : row + 1, :] = value

    def wide(layer, row, group):
        part = par[layer, row : row + 1, group * LANES : (group + 1) * LANES]
        return jnp.broadcast_to(part, (SUBS, LANES))

    take(s0_total, s0_pair[1])
    s0_b[b] = jnp.sum(s0_z[...], axis=0)
    s0_total = s0_b.at[0 : nb - 1]
    s0_pair = to_blk(lambda p: (s0_b.at[b], s0_b.at[b]), s0_total)
    fetch(1)
    fetch(2)
    relay(0)

    def load(ref, g, k):
        return ref[rows_of(k, SUBS), g * LANES : (g + 1) * LANES]

    def store(ref, g, k, value):
        ref[rows_of(k, SUBS), g * LANES : (g + 1) * LANES] = value

    def unpack(ref, i):
        parts = [
            jnp.concatenate(
                [ref[j, pl.ds(i * GROUP + k, SUBS, stride=steps), :] for j in range(fl)], axis=1
            )
            for k in range(GROUP)
        ]
        return jnp.concatenate(parts, axis=0)

    def pack(ref, i, value):
        for k in range(GROUP):
            for j in range(fl):
                ref[j, pl.ds(i * GROUP + k, SUBS, stride=steps), :] = value[
                    k * SUBS : (k + 1) * SUBS, j * LANES : (j + 1) * LANES
                ]

    def recur(carry, keep, lam, pushes):
        gated = [c * keep for c in carry]
        new = []
        for g in range(ng):
            vr, vi = cmul(lam[0][g], lam[1][g], gated[g], gated[ng + g])
            new.append((vr + pushes[g], vi + pushes[ng + g]))
        return gated, [v[0] for v in new] + [v[1] for v in new]

    def scan_local(src, lam, way, reverse):
        def body(i, carry):
            k = steps - 1 - i if reverse else i
            pushes = [load(src, g, k) for g in range(2 * ng)]
            return tuple(recur(carry, ktab[way, k], lam, pushes)[1])

        zero = jnp.zeros((SUBS, LANES), F32)
        return lax.fori_loop(0, steps, body, (zero,) * (2 * ng), unroll=4)

    def prefix(last, power, way, reverse):
        out = []
        for g in range(ng):
            sr, si = last[g], last[ng + g]
            ar, ai = power[0][g] * whole_sub[way], power[1][g] * whole_sub[way]
            for d in (1, 2, 4):
                shift = SUBS - d if reverse else d
                ok = sub_index < SUBS - d if reverse else sub_index >= d
                tr, ti = cmul(ar, ai, pltpu.roll(sr, shift, 0), pltpu.roll(si, shift, 0))
                br, bi = cmul(ar, ai, pltpu.roll(ar, shift, 0), pltpu.roll(ai, shift, 0))
                sr, si = jnp.where(ok, sr + tr, sr), jnp.where(ok, si + ti, si)
                ar, ai = jnp.where(ok, br, ar), jnp.where(ok, bi, ai)
            out.append((sr, si, ar, ai))
        return out

    carry_pairs = {}

    def send_carry(e, pre, reverse):
        row = 0 if reverse else SUBS - 1
        for g in range(ng):
            cols = slice(g * LANES, (g + 1) * LANES)
            for part in range(2):
                cy_src[e, part : part + 1, cols] = pre[g][part][row : row + 1, :]
                cy_buf[e, b, part : part + 1, cols] = pre[g][part][row : row + 1, :]
        carry_pairs[e] = to_blk(
            lambda p: (cy_src.at[e], cy_buf.at[e, b]), cy_buf.at[e, 0 : nb - 1]
        )

    def take_carry(e, pre, layer, way, reverse, sign):
        take(cy_buf.at[e, 0 : nb - 1], carry_pairs[e][1])
        ar, ai = par[layer, 6:7, :], sign * par[layer, 7:8, :]
        zero = jnp.zeros((1, states), F32)
        cr, ci, er, ei = zero, zero, zero, zero
        for p in reversed(range(nb)) if reverse else range(nb):
            er, ei = jnp.where(b == p, cr, er), jnp.where(b == p, ci, ei)
            tr, ti = cmul(ar, ai, cr, ci)
            keep = whole_chunk[way][p]
            cr = cy_buf[e, p, 0:1, :] + keep * tr
            ci = cy_buf[e, p, 1:2, :] + keep * ti
        shift = SUBS - 1 if reverse else 1
        first = sub_index == (SUBS - 1 if reverse else 0)
        carry_r, carry_i = [], []
        for g in range(ng):
            cols = slice(g * LANES, (g + 1) * LANES)
            wr = jnp.broadcast_to(er[:, cols], (SUBS, LANES))
            wi = jnp.broadcast_to(ei[:, cols], (SUBS, LANES))
            sr, si, dr, di = (pltpu.roll(v, shift, 0) for v in pre[g])
            tr, ti = cmul(dr, di, wr, wi)
            carry_r.append(jnp.where(first, wr, sr + tr))
            carry_i.append(jnp.where(first, wi, si + ti))
        return tuple(carry_r + carry_i)

    def forward_states(layer, carry, way, reverse, lam):
        scale = [[wide(layer, 2 + part, g) for g in range(ng)] for part in range(2)]
        src, dst = raw.at[layer], xs.at[layer]

        def body(i, carry):
            k = steps - 1 - i if reverse else i
            pushes = [load(src, g, k) for g in range(2 * ng)]
            _, new = recur(carry, ktab[way, k], lam, pushes)
            for g in range(ng):
                vr, vi = cmul(scale[0][g], scale[1][g], new[g], new[ng + g])
                store(dst, g, k, vr)
                store(dst, ng + g, k, vi)
            return tuple(new)

        lax.fori_loop(0, steps, body, carry, unroll=4)

    def adjoint_states(layer, carry, way, reverse, lam):
        scale = [[wide(layer, 2 + part, g) for g in range(ng)] for part in range(2)]
        zero = jnp.zeros((SUBS, LANES), F32)

        def body(i, loop):
            carry, sums = loop
            k = steps - 1 - i if reverse else i
            pushes = [load(seed, g, k) for g in range(2 * ng)]
            gated, new = recur(carry, ktab[way, k], lam, pushes)
            sums = list(sums)
            for g in range(ng):
                xr, xi = load(xs.at[layer], g, k), load(xs.at[layer], ng + g, k)
                ur, ui = load(raw.at[layer], g, k), load(raw.at[layer], ng + g, k)
                pr, pi = gated[g], gated[ng + g]
                vr, vi = new[g], new[ng + g]
                sums[g] += pr * xr + pi * xi
                sums[ng + g] += pi * xr - pr * xi
                sums[2 * ng + g] += vr * ur + vi * ui
                sums[3 * ng + g] += vi * ur - vr * ui
                store(gadj, g, k, scale[0][g] * vr + scale[1][g] * vi)
                store(gadj, ng + g, k, scale[0][g] * vi - scale[1][g] * vr)
            return tuple(new), tuple(sums)

        return lax.fori_loop(0, steps, body, (carry, (zero,) * (4 * ng)), unroll=4)[1]

    tile = 256 if tc % 256 == 0 else tc

    def to_groups(left, m, dst):
        def body(i, carry):
            rows = rows_of(i, tile)
            value = product(
                (left[0][rows, :], left[1][rows, :]), (wh[m], wl[m]), "nt"
            )
            dst[rows, :] = value
            return carry

        lax.fori_loop(0, tc // tile, body, 0)

    def from_groups(src, m, dst):
        def body(i, carry):
            rows = rows_of(i, tile)
            dst[rows, :] = product(halves(src[rows, :]), (wh[m], wl[m]), "nn")
            return carry

        lax.fori_loop(0, tc // tile, body, 0)

    def weight_grad(src, right, m, scaled):
        def body(pair, carry):
            left = src[:, pl.ds(pl.multiple_of(pair * 2 * LANES, 2 * LANES), 2 * LANES)]
            value = product(halves(left), (right[0][...], right[1][...]), "tn")
            for half in range(2):
                g = 2 * pair + half
                part = value[half * LANES : (half + 1) * LANES, :]
                if scaled:
                    part = part * jnp.where(g < ng, 2.0, -2.0)
                gl[m, rows_of(g, LANES), :] = part
            return carry

        lax.fori_loop(0, ng, body, 0)

    stats_pairs = {}

    def stats_start(i, first, second):
        for n, value in enumerate((first, second)):
            for j in range(fl):
                row = n * fl + j
                st_own[i, row : row + 1, :] = value[:, j * LANES : (j + 1) * LANES]
        take(st_sib.at[i], to_sibling(st_own.at[i], st_sib.at[i])[1])
        both = st_own[i] + st_sib[i]
        st_src[i] = both
        st_buf[i, chip] = both
        stats_pairs[i] = (new(), new())
        over_chips(lambda dev: start(st_src.at[i], st_buf.at[i, chip], stats_pairs[i], dev))
        sent.append((st_buf.at[i, 0 : nch - 1], stats_pairs[i][0]))

    def stats_end(i):
        take(st_buf.at[i, 0 : nch - 1], stats_pairs[i][1])
        st_tot[i] = jnp.sum(st_buf[i], axis=0)
        return [
            jnp.concatenate(
                [st_tot[i, n * fl + j : n * fl + j + 1, :] for j in range(fl)], axis=1
            )
            for n in range(2)
        ]

    def to_row(value):
        return jnp.sum(value, axis=0, keepdims=True)

    def eights(value):
        return jnp.sum(value.reshape(value.shape[0] // SUBS, SUBS, feats), axis=0)

    gpair = {}
    pr = psum.shape[1] // nz

    def core_rows(part):
        return rows_at(part * states, states)

    def grad_core(m):
        gpair["core", m] = to_sibling(gl.at[m, core_rows(1 - core), :], gsib.at[m])

    def grad_add(m):
        take(gsib.at[m], gpair["core", m][1])

        def body(i, carry):
            gsib[m, rows_of(i, 32), :] += gl[m, rows_at(core * states + i * 32, 32), :]
            return carry

        lax.fori_loop(0, states // 32, body, 0)

    halved = [h and nz % 2 == 0 for h in HALVED]
    grad_rows = [sb // 2 if h else sb for h in halved]
    sharers = [nz // 2 if h else nz for h in halved]

    def grad_piece(m, p, other=False):
        low = p * sb
        if halved[m]:
            low = low + (1 - z % 2 if other else z % 2) * grad_rows[m]
        return rows_at(low, grad_rows[m])

    def grad_pair(m):
        pair = (new(), new())
        for p in range(nb):
            start(gsib.at[m, grad_piece(m, p, True), :], gpr.at[m, p], pair, z_pair)
        sent.append((gpr.at[m], pair[0]))
        gpair["pair", m] = pair

    def grad_pair_add(m):
        take(gpr.at[m], gpair["pair", m][1])

        def body(i, carry):
            for p in range(nb):
                low = p * sb + (z % 2) * grad_rows[m]
                gsib[m, rows_at(low + i * 8, 8), :] += gpr[m, p, rows_of(i, 8), :]
            return carry

        lax.fori_loop(0, grad_rows[m] // 8, body, 0)

    def grad_blk(m):
        gpair["blk", m] = to_blk(
            lambda p: (gsib.at[m, grad_piece(m, p), :], gblk.at[m, b, 0 : grad_rows[m], :]),
            gblk.at[m, 0 : nb - 1, 0 : grad_rows[m], :],
        )

    def my_sharers(m, body):
        if halved[m]:
            place = z // 2

            def peer(k):
                q = (place + k) % sharers[m]
                body(q, (b, (q * 2 + z % 2) * 2 + core))

            several(sharers[m], peer)
        else:
            over_z(body)

    def grad_z(m):
        take(gblk.at[m, 0 : nb - 1, 0 : grad_rows[m], :], gpair["blk", m][1])

        def body(i, carry):
            low = b * sb + (z % 2) * grad_rows[m] if halved[m] else b * sb
            value = gsib[m, rows_at(low + i * 8, 8), :]
            for p in blk_peers:
                value += gblk[m, p, rows_of(i, 8), :]
            for j in range(fl):
                psum[m, rows_at(j * grad_rows[m] + i * 8, 8), :] = value[
                    :, j * LANES : (j + 1) * LANES
                ]
            return carry

        lax.fori_loop(0, grad_rows[m] // 8, body, 0)
        place = z // 2 if halved[m] else z
        pair = (new(), new())
        my_sharers(
            m, lambda q, dev: start(psum.at[m, rows_of(q, pr), :], gz.at[m, place], pair, dev)
        )
        sent.append((gz.at[m, 0 : sharers[m] - 1], pair[0]))
        gpair["z", m] = pair

    def grad_gather(m):
        take(gz.at[m, 0 : sharers[m] - 1], gpair["z", m][1])
        place = z // 2 if halved[m] else z
        value = psum[m, rows_of(place, pr), :]
        for q in range(sharers[m]):
            value += jnp.where(place == q, 0.0, gz[m, q])
        mine = rows_of((z % 2) * sharers[m] + place if halved[m] else z, pr)
        fin[m, core, mine, :] = value
        piece = fin.at[m, core, mine, :]
        gpair["all", m] = to_z(lambda p: (piece, piece), fin.at[m, core, 0 : (nz - 1) * pr, :])

    def grad_share(m):
        take(fin.at[m, core, 0 : (nz - 1) * pr, :], gpair["all", m][1])
        gpair["share", m] = to_sibling(fin.at[m, core], fin.at[m, core])

    stores = []

    def grad_store(m):
        take(fin.at[m, 1 - core], gpair["share", m][1])
        layer, kind = MATRICES[m]
        dst = (gin_hbm if kind == "in" else gout_hbm).at[layer]
        slot = new()
        count = grad_rows[m]
        for part in range(2):
            for h in range(sb // count):
                for j in range(fl):
                    low = h * sharers[m] * pr + j * count
                    near(
                        fin.at[m, part, low : low + count, :],
                        dst.at[part, h * count : (h + 1) * count, j * LANES : (j + 1) * LANES],
                        slot,
                    )
        stores.append((dst, slot))

    hc = tc // 2
    relay_far(0)
    split_matrix(0)
    take(s0_total, s0_pair[1])
    sums = [
        jnp.concatenate([s0_b[p][n : n + 1, :] for p in range(nb)], axis=1) for n in range(2)
    ]
    near_done(xin.at[b], h_slot)
    take(x_total, x_arrival)

    scales = []
    small_rows = GROUP * SUBS
    cot_parts = []

    for layer in range(2):
        way, reverse = layer, layer == 1
        mean = sums[0] / token_count
        rstd = lax.rsqrt(sums[1] / token_count - mean * mean + EPSILON)
        gain, bias, feed = (feature_row(row + layer) for row in (8, 10, 6))
        scales.append((rstd, gain, bias, feed))

        def normalize(i, carry, layer=layer, mean=mean, rstd=rstd, gain=gain, bias=bias):
            rows = rows_of(i, small_rows)
            if layer == 0:
                value = unpack(xin, i)
                hid[0, rows, :] = value
            else:
                value = hid[1, rows, :]
            unit = (value - mean) * rstd
            zn[layer, rows, :] = unit
            zh[layer, rows, :], zl[layer, rows, :] = halves(gain * unit + bias)
            return carry

        lax.fori_loop(0, tc // small_rows, normalize, 0)
        to_groups((zh.at[layer], zl.at[layer]), 2 * layer, raw.at[layer])
        lam = [[wide(layer, part, g) for g in range(ng)] for part in range(2)]
        power = [[wide(layer, 4 + part, g) for g in range(ng)] for part in range(2)]
        last = scan_local(raw.at[layer], lam, way, reverse)
        pre = prefix(last, power, way, reverse)
        send_carry(layer, pre, reverse)
        if layer == 0:
            fetch(3)
            relay(1)
            relay_far(1)
            split_matrix(1)
        else:
            cot_parts.append(spread_in(cot_hbm, cotb, hc, tc - hc))
            relay_far(3)
            split_matrix(3)
        carry = take_carry(layer, pre, layer, way, reverse, 1.0)
        forward_states(layer, carry, way, reverse, lam)
        if layer == 0:
            relay(2)
        from_groups(xs.at[layer], 2 * layer + 1, ybuf)

        def activate(i, carry, layer=layer, gain=gain, bias=bias, feed=feed):
            rows = rows_of(i, small_rows)
            mixed = ybuf[rows, :] + feed * (gain * zn[layer, rows, :] + bias)
            below = 0.5 * (1.0 + lax.erf(mixed * 0.7071067811865476))
            density = 0.3989422804014327 * jnp.exp(-0.5 * mixed * mixed)
            gate = 1.0 / (1.0 + jnp.exp(-mixed))
            gelu = mixed * below
            value = hid[layer, rows, :] + gelu * gate
            if layer == 0:
                hid[1, rows, :] = value
            else:
                pack(outb, i, value)
            actp[layer, rows, :] = (below + mixed * density) * gate + gelu * gate * (1.0 - gate)
            return carry[0] + eights(value), carry[1] + eights(value * value)

        zero = jnp.zeros((SUBS, feats), F32)
        parts = lax.fori_loop(0, tc // small_rows, activate, (zero, zero))
        if layer == 0:
            stats_start(0, to_row(parts[0]), to_row(parts[1]))
            cot_parts.append(spread_in(cot_hbm, cotb, 0, hc))
            relay(3)
            relay_far(2)
            split_matrix(2)
            sums = stats_end(0)

    for ref, slot in sent:
        take(ref, slot)
    sent.clear()
    gl = wf
    near_done(cotb.at[b], c_slot)
    for part in cot_parts:
        take(*part)
    outs = []
    for layer in (1, 0):
        way, reverse = 1 - layer, layer == 0
        rstd, gain, bias, feed = scales[layer]
        upper = dh.at[layer]

        def mixed_grad(i, carry, layer=layer, gain=gain, bias=bias, upper=upper):
            rows = rows_of(i, small_rows)
            value = unpack(cotb, i) if layer == 1 else upper[rows, :]
            if layer == 1:
                upper[rows, :] = value
            value = value * actp[layer, rows, :]
            dyf[rows, :] = value
            dyh[rows, :], dyl[rows, :] = halves(value)
            return carry + eights(value * (gain * zn[layer, rows, :] + bias))

        zero = jnp.zeros((SUBS, feats), F32)
        feed_grad = to_row(lax.fori_loop(0, tc // small_rows, mixed_grad, zero))
        to_groups((dyh, dyl), 2 * layer + 1, seed)
        lam = [
            [wide(layer, 0, g) for g in range(ng)],
            [-wide(layer, 1, g) for g in range(ng)],
        ]
        power = [
            [wide(layer, 4, g) for g in range(ng)],
            [-wide(layer, 5, g) for g in range(ng)],
        ]
        last = scan_local(seed, lam, way, reverse)
        pre = prefix(last, power, way, reverse)
        send_carry(2 + layer, pre, reverse)
        outs.append(spread_out(outb, out_hbm, 0 if layer == 1 else hc, hc))
        weight_grad(xs.at[layer], (dyh, dyl), 2 * layer + 1, True)
        grad_core(2 * layer + 1)
        carry = take_carry(2 + layer, pre, layer, way, reverse, -1.0)
        if layer == 0:
            grad_z(3)
        state_sums = adjoint_states(layer, carry, way, reverse, lam)
        grad_add(2 * layer + 1)
        from_groups(gadj, 2 * layer, dz)

        def dz_sums(i, carry, layer=layer, feed=feed):
            rows = rows_of(i, small_rows)
            value = dz[rows, :] + feed * dyf[rows, :]
            dz[rows, :] = value
            return carry[0] + eights(value), carry[1] + eights(value * zn[layer, rows, :])

        parts = lax.fori_loop(0, tc // small_rows, dz_sums, (zero, zero))
        stats_start(1 + layer, to_row(parts[0]), to_row(parts[1]))
        if layer == 0:
            grad_pair_add(2)
            grad_blk(2)
        if halved[2 * layer + 1]:
            grad_pair(2 * layer + 1)
        else:
            grad_blk(2 * layer + 1)
        weight_grad(gadj, (zh.at[layer], zl.at[layer]), 2 * layer, False)
        grad_core(2 * layer)
        for p in range(nb):
            q_own[p, layer : layer + 1, :] = feed_grad[:, p * fb : (p + 1) * fb]
        for n in range(4):
            vector = jnp.concatenate(
                [to_row(state_sums[n * ng + g]) for g in range(ng)], axis=1
            )
            row = 2 + 4 * layer + n
            for p in range(nb):
                q_own[p, row : row + 1, 0:sb] = vector[:, p * sb : (p + 1) * sb]
        grad_add(2 * layer)
        if layer == 1:
            grad_pair(2)
        else:
            grad_blk(0)
            q_pair = to_sibling(q_own, q_sib)
            grad_gather(3)
            if halved[1]:
                grad_pair_add(1)
                grad_blk(1)
            take(q_sib, q_pair[1])
            q_sib[...] += q_own[...]
            q_total = q_blk.at[0 : nb - 1]
            q_pair = to_blk(lambda p: (q_sib.at[p], q_blk.at[b]), q_total)
        bias_grad, gain_grad = stats_end(1 + layer)

        def hidden_grad(
            i, carry, layer=layer, rstd=rstd, gain=gain, bias_grad=bias_grad, gain_grad=gain_grad, upper=upper
        ):
            rows = rows_of(i, small_rows)
            inner = (
                dz[rows, :]
                - bias_grad / token_count
                - zn[layer, rows, :] * (gain_grad / token_count)
            )
            value = upper[rows, :] + gain * rstd * inner
            if layer == 1:
                dh[0, rows, :] = value
            else:
                pack(gxb, i, value)
            return carry

        lax.fori_loop(0, tc // small_rows, hidden_grad, 0)
        gsmall_ref[2 + layer : 3 + layer, :] = st_tot[1 + layer, pl.ds(fl + b, 1), :]
        gsmall_ref[4 + layer : 5 + layer, :] = st_tot[1 + layer, pl.ds(b, 1), :]

    outs.append(spread_out(gxb, gx_hbm, 0, tc))
    grad_z(2)
    grad_share(3)
    first, second = (0, 1) if halved[1] else (1, 0)
    grad_z(first)
    grad_gather(2)
    grad_store(3)
    take(q_total, q_pair[1])
    value = q_sib[b]
    for p in blk_peers:
        value += q_blk[p]
    q_z[z] = value
    q_total = q_z.at[0 : nz - 1]
    q_pair = to_z(lambda p: (q_z.at[z], q_z.at[z]), q_total)
    grad_share(2)
    grad_gather(first)
    grad_z(second)
    grad_store(2)
    grad_share(first)
    grad_gather(second)
    grad_store(first)
    take(q_total, q_pair[1])
    small = jnp.sum(q_z[...], axis=0)
    gsmall_ref[0:2, :] = small[0:2, :]
    for layer in range(2):
        real = poles_ref[layer, 0:1, :]
        imag = poles_ref[layer, 1:2, :]
        step, lr, li, fr, fi, modulus = discretize(real, imag, step_ref[layer : layer + 1, :])
        lgr, lgi, fgr, fgi = (
            small[2 + 4 * layer + n : 3 + 4 * layer + n, 0:sb] for n in range(4)
        )
        qr = (real * fgr - imag * fgi) / modulus
        qi = (real * fgi + imag * fgr) / modulus
        tr, ti = lgr + qr, lgi + qi
        wr = lr * tr + li * ti
        wi = lr * ti - li * tr
        row = 6 + 2 * layer
        gsmall_ref[row : row + 1, 0:sb] = step * wr - (fr * qr + fi * qi)
        gsmall_ref[row + 1 : row + 2, 0:sb] = step * wi - (fr * qi - fi * qr)
        gsmall_ref[10 + layer : 11 + layer, 0:sb] = step * (real * wr + imag * wi)
    for arrival, mine in outs:
        take(*arrival)
        near_done(*mine)
    grad_share(second)
    grad_store(second)
    for ref, slot in stores:
        near_done(ref, slot)
    for ref, slot in sent:
        take(ref, slot)


def finish(out_in, gx_in, gin_in, gout_in, small_in, out, gx, gpoles, gstep, gin, gout, gfeed, ggain, gbias, sem):
    pairs = ((out_in, out), (gx_in, gx), (gin_in, gin), (gout_in, gout))
    for n, (src, dst) in enumerate(pairs):
        pltpu.make_async_copy(src, dst, sem.at[n]).start()
    sb = gstep.shape[1]
    gfeed[...] = small_in[0:2, :]
    ggain[...] = small_in[2:4, :]
    gbias[...] = small_in[4:6, :]
    for layer in range(2):
        gpoles[layer] = small_in[6 + 2 * layer : 8 + 2 * layer, 0:sb]
    gstep[...] = small_in[10:12, 0:sb]
    for n, (src, dst) in enumerate(pairs):
        pltpu.make_async_copy(src, dst, sem.at[n]).wait()


def local(mesh, *args):
    inputs, seq_lengths = args[0], args[1]
    nb, nr = mesh.shape["blk"], mesh.shape["row"]
    nz = nr // 2
    tokens, fb = inputs.shape
    sb = args[2].shape[2]
    states, feats = sb * nb, fb * nb
    assert seq_lengths.shape[0] == 1 and nr % 2 == 0
    assert fb == LANES and states % LANES == 0 and 2 * feats == SUBS * LANES
    assert tokens % (nb * SUBS * SUBS) == 0 and sb % 16 == 0 and states % 64 == 0
    tc = tokens // nb
    steps = tc // SUBS
    assert steps & (steps - 1) == 0
    nch = nb * nz
    fl = feats // LANES
    piece = -(-fl * sb // (nz * SUBS)) * SUBS
    sizes = (nb, nz, seq_lengths.shape[1], tokens, feats, states, tokens * nr)
    vmem = lambda *shape: pltpu.VMEM(shape, F32)
    half = lambda *shape: pltpu.VMEM(shape, BF16)
    scratch = [
        vmem(tokens, fb),
        vmem(16, fb),
        vmem(nb, 16, fb),
        vmem(4, 2 * states, feats),
        half(4, 2 * states, feats),
        half(4, 2 * states, feats),
        vmem(2, 8, states),
        vmem(2, steps, SUBS, LANES),
        vmem(nb, tc, fb),
        vmem(2, tc, feats),
        vmem(nb, tc, fb),
        vmem(nb, tc, fb),
        vmem(nb, tc, fb),
        vmem(2, tc, feats),
        half(2, tc, feats),
        half(2, tc, feats),
        vmem(2, tc, 2 * states),
        vmem(2, tc, 2 * states),
        vmem(tc, feats),
        vmem(2, tc, feats),
        vmem(tc, feats),
        half(tc, feats),
        half(tc, feats),
        vmem(tc, 2 * states),
        vmem(tc, 2 * states),
        vmem(tc, feats),
        vmem(2, tc, feats),
        vmem(4, states, feats),
        vmem(4, nb, sb // 2, feats),
        vmem(4, nb, sb, feats),
        vmem(4, nz * piece, LANES),
        vmem(4, nz, piece, LANES),
        vmem(4, 2, nz * piece, LANES),
        vmem(8, fb),
        vmem(8, fb),
        vmem(nz, 8, fb),
        vmem(nb, 8, fb),
        vmem(3, 8, LANES),
        vmem(3, 8, LANES),
        vmem(3, 8, LANES),
        vmem(3, nch, 8, LANES),
        vmem(3, 8, LANES),
        vmem(4, 8, states),
        vmem(4, nb, 8, states),
        vmem(nb, 16, fb),
        vmem(nb, 16, fb),
        vmem(nb, 16, fb),
        vmem(nz, 16, fb),
        pltpu.SemaphoreType.DMA((SEMAPHORES,)),
    ]
    shaped = lambda like: jax.ShapeDtypeStruct(like.shape, like.dtype)
    anywhere = pl.BlockSpec(memory_space=pl.ANY)
    fast = pl.BlockSpec(memory_space=pltpu.VMEM)
    main = pl.BlockSpec(memory_space=pltpu.HBM)
    raw = pl.pallas_call(
        functools.partial(kernel, sizes),
        name="s5_layers",
        out_shape=tuple(pltpu.VMEM(args[i].shape, F32) for i in (0, 0, 4, 5)) + (pltpu.VMEM((16, fb), F32),),
        in_specs=[
            main,
            pl.BlockSpec(memory_space=pltpu.SMEM),
            fast,
            fast,
            main,
            main,
            fast,
            fast,
            fast,
            main,
        ],
        out_specs=(anywhere,) * 4 + (fast,),
        scratch_shapes=scratch,
        compiler_params=pltpu.CompilerParams(
            collective_id=0, has_side_effects=True, vmem_limit_bytes=57 << 20
        ),
    )(*args)
    return pl.pallas_call(
        finish,
        name="results",
        out_shape=tuple(shaped(args[i]) for i in (0, 0, 2, 3, 4, 5, 6, 7, 8)),
        in_specs=[fast] * 5,
        out_specs=(anywhere, anywhere, fast, fast, anywhere, anywhere, fast, fast, fast),
        scratch_shapes=[pltpu.SemaphoreType.DMA((4,))],
        compiler_params=pltpu.CompilerParams(vmem_limit_bytes=8 << 20),
    )(*raw)


def solution(mesh):
    by_state = (P(None, None, "blk"), P(None, "blk"), P(None, None, "blk", None), P(None, None, "blk", None))
    by_feature = (P(None, "blk"),) * 3
    tokens = P("row", "blk")
    return jax.shard_map(
        functools.partial(local, mesh),
        mesh=mesh,
        in_specs=(tokens, P("row", None), *by_state, *by_feature, tokens),
        out_specs=(tokens, tokens, *by_state, *by_feature),
        check_vma=False,
    )
```

```python
import functools

import jax
import jax.numpy as jnp
from jax import lax
from jax.experimental import pallas as pl
from jax.experimental.pallas import tpu as pltpu
from jax.sharding import PartitionSpec as P


EPSILON = 1e-05
LANES = 128
SUBS = 8
GROUP = 4
MESH = pl.DeviceIdType.MESH
F32 = jnp.float32
BF16 = jnp.bfloat16
MATRICES = ((0, "in"), (0, "out"), (1, "in"), (1, "out"))
SHARED = (True, False, True, True)
HALVED = (False, True, True, False)
SEMAPHORES = 132
DIMS = {
    "nt": (((1,), (1,)), ((), ())),
    "nn": (((1,), (0,)), ((), ())),
    "tn": (((0,), (0,)), ((), ())),
}


def halves(values):
    high = values.astype(BF16)
    return high, (values - high.astype(F32)).astype(BF16)


def product(left, right, form):
    def one(a, b):
        return lax.dot_general(a, b, DIMS[form], preferred_element_type=F32)

    return one(left[0], right[0]) + (one(left[0], right[1]) + one(left[1], right[0]))


def cmul(ar, ai, br, bi):
    return ar * br - ai * bi, ar * bi + ai * br


def kernel(
    sizes,
    x_hbm,
    seq_ref,
    poles_ref,
    step_ref,
    in_hbm,
    out_mat_hbm,
    feed_ref,
    gain_ref,
    bias_ref,
    cot_hbm,
    out_hbm,
    gx_hbm,
    gin_hbm,
    gout_hbm,
    gsmall_ref,
    xloc,
    small_src,
    small_all,
    wf,
    wh,
    wl,
    par,
    ktab,
    xin,
    hid,
    cotb,
    outb,
    gxb,
    zn,
    zh,
    zl,
    raw,
    xs,
    ybuf,
    actp,
    dyf,
    dyh,
    dyl,
    seed,
    gadj,
    dz,
    dh,
    gsib,
    gpr,
    gblk,
    psum,
    gz,
    fin,
    s0_own,
    s0_sib,
    s0_z,
    s0_b,
    st_own,
    st_sib,
    st_src,
    st_buf,
    st_tot,
    cy_src,
    cy_buf,
    q_own,
    q_sib,
    q_blk,
    q_z,
    sem,
):
    nb, nz, seqs, tokens, feats, states, token_count = sizes
    nch = nb * nz
    tc, fb, sb = tokens // nb, feats // nb, states // nb
    steps = tc // SUBS
    ng = states // LANES
    fl = feats // LANES
    b = lax.axis_index("blk")
    r = lax.axis_index("row")
    core = r % 2
    z = r // 2
    chip = b * nz + z
    sibling = (b, z * 2 + 1 - core)
    z_pair = (b, (z + 1 - 2 * (z % 2)) * 2 + core)
    blk_peers = [((b + k) % nb) for k in range(1, nb)]

    def several(count, body):
        if count <= 16:
            for k in range(1, count):
                body(k)
        else:

            def step(k, carry):
                body(k)
                return carry

            lax.fori_loop(1, count, step, 0)

    def over_z(body):
        def peer(k):
            q = (z + k) % nz
            body(q, (b, q * 2 + core))

        several(nz, peer)

    def over_chips(body):
        def peer(k):
            q = (chip + k) % nch
            body((q // nz, (q % nz) * 2 + core))

        several(nch, peer)

    barrier = pltpu.get_barrier_semaphore()
    pl.semaphore_signal(barrier, 1, device_id=sibling, device_id_type=MESH)
    over_chips(
        lambda dev: pl.semaphore_signal(barrier, 1, device_id=dev, device_id_type=MESH)
    )

    slots = iter(range(SEMAPHORES))
    sent = []

    def new():
        return next(slots)

    def start(src, dst, pair, dev):
        pltpu.make_async_remote_copy(
            src, dst, sem.at[pair[0]], sem.at[pair[1]], device_id=dev, device_id_type=MESH
        ).start()

    def take(ref, slot):
        pltpu.make_async_copy(ref, ref, sem.at[slot]).wait()

    def near(src, dst, slot):
        pltpu.make_async_copy(src, dst, sem.at[slot]).start()

    def near_done(ref, slot):
        pltpu.make_async_copy(ref, ref, sem.at[slot]).wait()

    def rows_of(i, size):
        return pl.ds(pl.multiple_of(i * size, size), size)

    def rows_at(i, size):
        return pl.ds(pl.multiple_of(i, 8), size)

    def to_sibling(src, dst, total=None):
        pair = (new(), new())
        start(src, dst, pair, sibling)
        sent.append((src, pair[0]))
        return pair

    def to_blk(make, total):
        pair = (new(), new())
        for p in blk_peers:
            start(*make(p), pair, (p, r))
        sent.append((total, pair[0]))
        return pair

    def to_z(make, total):
        pair = (new(), new())
        over_z(lambda p, dev: start(*make(p), pair, dev))
        sent.append((total, pair[0]))
        return pair

    my_cols = rows_of(b, fb)
    mats = [in_hbm if kind == "in" else out_mat_hbm for _, kind in MATRICES]
    x_slot, h_slot, c_slot = new(), new(), new()
    own_slots = [new() for _ in MATRICES]
    near(x_hbm, xloc, x_slot)
    near(x_hbm.at[rows_of(b, tc), :], xin.at[b], h_slot)
    near(cot_hbm.at[rows_of(b, tc), :], cotb.at[b], c_slot)
    for m, (layer, _) in enumerate(MATRICES):
        for part in range(2):
            near(
                mats[m].at[layer, part],
                wf.at[m, rows_at(part * states + b * sb, sb), :],
                own_slots[m],
            )

    small_src[...] = jnp.zeros_like(small_src)
    for layer in range(2):
        small_src[2 * layer : 2 * layer + 2, 0:sb] = poles_ref[layer]
    small_src[4:6, 0:sb] = step_ref[...]
    small_src[6:8, :] = feed_ref[...]
    small_src[8:10, :] = gain_ref[...]
    small_src[10:12, :] = bias_ref[...]
    small_all[b] = small_src[...]
    pl.semaphore_wait(barrier, nch)

    shared = [s and nz % 2 == 0 for s in SHARED]
    piece_rows = [sb // 2 if s else sb for s in shared]
    fetched = [wf.at[m, 0 : (nb - 1) * piece_rows[m], :] for m in range(4)]
    blk_pairs, z_pairs, near_pairs, far_pairs = {}, {}, {}, {}

    def weight_piece(m, p, other=False):
        half = (z % 2) * piece_rows[m] if shared[m] else 0
        if other:
            half = (1 - z % 2) * piece_rows[m]
        return wf.at[m, rows_at(core * states + p * sb + half, piece_rows[m]), :]

    def fetch(m):
        half = (z % 2) * piece_rows[m] if shared[m] else 0
        src = mats[m].at[MATRICES[m][0], core, rows_at(half, piece_rows[m]), :]
        blk_pairs[m] = to_blk(lambda p: (src, weight_piece(m, b)), fetched[m])

    def relay(m):
        take(fetched[m], blk_pairs[m][1])
        near_pairs[m] = (new(), new())
        if shared[m]:
            z_pairs[m] = (new(), new())
            sent.append((fetched[m], z_pairs[m][0]))
        for p in blk_peers:
            piece = weight_piece(m, p)
            if shared[m]:
                start(piece, piece, z_pairs[m], z_pair)
            start(piece, piece, near_pairs[m], sibling)
        sent.append((fetched[m], near_pairs[m][0]))

    def relay_far(m):
        if shared[m]:
            take(fetched[m], z_pairs[m][1])
            far_pairs[m] = (new(), new())
            for p in blk_peers:
                piece = weight_piece(m, p, other=True)
                start(piece, piece, far_pairs[m], sibling)
            sent.append((fetched[m], far_pairs[m][0]))

    def split_matrix(m):
        near_done(wf.at[m, 0 : 2 * sb, :], own_slots[m])
        take(fetched[m], near_pairs[m][1])
        if shared[m]:
            take(fetched[m], far_pairs[m][1])
        scaled = MATRICES[m][1] == "out"

        def body(i, carry):
            rows = rows_of(i, 64)
            values = wf[m, rows, :]
            if scaled:
                values = values * jnp.where(i * 64 < states, 2.0, -2.0)
            wh[m, rows, :], wl[m, rows, :] = halves(values)
            return carry

        lax.fori_loop(0, 2 * states // 64, body, 0)

    def spread_in(src, dst, low, count):
        total = dst.at[0 : nb - 1, low : low + count, :]
        pair = to_blk(
            lambda p: (src.at[rows_at(p * tc + low, count), :], dst.at[b, low : low + count, :]),
            total,
        )
        return total, pair[1]

    def spread_out(src, dst, low, count):
        slot = new()
        mine = dst.at[rows_at(b * tc + low, count), :]
        near(src.at[b, low : low + count, :], mine, slot)
        total = src.at[0 : nb - 1, low : low + count, :]
        pair = to_blk(lambda p: (src.at[p, low : low + count, :], mine), total)
        return (total, pair[1]), (mine, slot)

    small_total = small_all.at[0 : nb - 1]
    small_pair = to_blk(lambda p: (small_src, small_all.at[b]), small_total)
    fetch(0)
    x_total, x_arrival = spread_in(x_hbm, xin, 0, tc)
    near_done(xloc, x_slot)

    def add_rows(i, carry):
        total, square = carry
        values = xloc[rows_of(i, 64), :].reshape(8, SUBS, fb)
        return total + jnp.sum(values, axis=0), square + jnp.sum(values * values, axis=0)

    zero_tile = jnp.zeros((SUBS, fb), F32)
    total, square = lax.fori_loop(0, tokens // 64, add_rows, (zero_tile, zero_tile))
    s0_own[...] = jnp.zeros_like(s0_own)
    s0_own[0:1, :] = jnp.sum(total, axis=0, keepdims=True)
    s0_own[1:2, :] = jnp.sum(square, axis=0, keepdims=True)
    s0_pair = to_sibling(s0_own, s0_sib)
    starts = [jnp.int32(0)]
    for i in range(seqs - 1):
        starts.append(starts[-1] + seq_ref[0, i])
    begins = starts
    ends = starts[1:] + [jnp.int32(tokens)]

    def none_in(low, size, marks, shift):
        hit = None
        for mark in marks:
            at = mark - shift - low
            inside = jnp.logical_and(at >= 0, at < size)
            hit = inside if hit is None else jnp.logical_or(hit, inside)
        return jnp.where(hit, 0.0, 1.0).astype(F32)

    sub_index = lax.broadcasted_iota(jnp.int32, (SUBS, LANES), 0)
    base = b * tc
    marks = ((begins, 0), (ends, 1))

    def fill_flags(k, carry):
        for way in range(2):
            ktab[way, k] = none_in(base + sub_index * steps + k, 1, *marks[way])
        return carry

    lax.fori_loop(0, steps, fill_flags, 0)
    whole_sub = [none_in(base + sub_index * steps, steps, *marks[way]) for way in range(2)]
    whole_chunk = [[none_in(p * tc, tc, *marks[way]) for p in range(nb)] for way in range(2)]

    take(s0_sib, s0_pair[1])
    s0_z[z] = s0_own[...] + s0_sib[...]
    s0_total = s0_z.at[0 : nz - 1]
    s0_pair = to_z(lambda p: (s0_z.at[z], s0_z.at[z]), s0_total)

    take(small_total, small_pair[1])
    state_rows = jnp.concatenate([small_all[p][0:8, 0:sb] for p in range(nb)], axis=1)

    def feature_row(row):
        return jnp.concatenate([small_all[p][row : row + 1, :] for p in range(nb)], axis=1)

    def discretize(real, imag, log_step):
        step = jnp.exp(log_step)
        magnitude = jnp.exp(real * step)
        lr = magnitude * jnp.cos(imag * step)
        li = magnitude * jnp.sin(imag * step)
        modulus = real * real + imag * imag
        fr = ((lr - 1.0) * real + li * imag) / modulus
        fi = (li * real - (lr - 1.0) * imag) / modulus
        return step, lr, li, fr, fi, modulus

    for layer in range(2):
        _, lr, li, fr, fi, _ = discretize(
            state_rows[2 * layer : 2 * layer + 1, :],
            state_rows[2 * layer + 1 : 2 * layer + 2, :],
            state_rows[4 + layer : 5 + layer, :],
        )
        power = [(lr, li)]
        size = 1
        while size < tc:
            power.append(cmul(*power[-1], *power[-1]))
            size *= 2
        at_steps = power[steps.bit_length() - 1]
        for row, value in enumerate((lr, li, fr, fi, *at_steps, *power[-1])):
            par[layer, row : row + 1, :] = value

    def wide(layer, row, group):
        part = par[layer, row : row + 1, group * LANES : (group + 1) * LANES]
        return jnp.broadcast_to(part, (SUBS, LANES))

    take(s0_total, s0_pair[1])
    s0_b[b] = jnp.sum(s0_z[...], axis=0)
    s0_total = s0_b.at[0 : nb - 1]
    s0_pair = to_blk(lambda p: (s0_b.at[b], s0_b.at[b]), s0_total)
    fetch(1)
    fetch(2)
    relay(0)

    def load(ref, g, k):
        return ref[rows_of(k, SUBS), g * LANES : (g + 1) * LANES]

    def store(ref, g, k, value):
        ref[rows_of(k, SUBS), g * LANES : (g + 1) * LANES] = value

    def unpack(ref, i):
        parts = [
            jnp.concatenate(
                [ref[j, pl.ds(i * GROUP + k, SUBS, stride=steps), :] for j in range(fl)], axis=1
            )
            for k in range(GROUP)
        ]
        return jnp.concatenate(parts, axis=0)

    def pack(ref, i, value):
        for k in range(GROUP):
            for j in range(fl):
                ref[j, pl.ds(i * GROUP + k, SUBS, stride=steps), :] = value[
                    k * SUBS : (k + 1) * SUBS, j * LANES : (j + 1) * LANES
                ]

    def recur(carry, keep, lam, pushes):
        gated = [c * keep for c in carry]
        new = []
        for g in range(ng):
            vr, vi = cmul(lam[0][g], lam[1][g], gated[g], gated[ng + g])
            new.append((vr + pushes[g], vi + pushes[ng + g]))
        return gated, [v[0] for v in new] + [v[1] for v in new]

    def scan_local(src, lam, way, reverse):
        def body(i, carry):
            k = steps - 1 - i if reverse else i
            pushes = [load(src, g, k) for g in range(2 * ng)]
            return tuple(recur(carry, ktab[way, k], lam, pushes)[1])

        zero = jnp.zeros((SUBS, LANES), F32)
        return lax.fori_loop(0, steps, body, (zero,) * (2 * ng), unroll=4)

    def prefix(last, power, way, reverse):
        out = []
        for g in range(ng):
            sr, si = last[g], last[ng + g]
            ar, ai = power[0][g] * whole_sub[way], power[1][g] * whole_sub[way]
            for d in (1, 2, 4):
                shift = SUBS - d if reverse else d
                ok = sub_index < SUBS - d if reverse else sub_index >= d
                tr, ti = cmul(ar, ai, pltpu.roll(sr, shift, 0), pltpu.roll(si, shift, 0))
                br, bi = cmul(ar, ai, pltpu.roll(ar, shift, 0), pltpu.roll(ai, shift, 0))
                sr, si = jnp.where(ok, sr + tr, sr), jnp.where(ok, si + ti, si)
                ar, ai = jnp.where(ok, br, ar), jnp.where(ok, bi, ai)
            out.append((sr, si, ar, ai))
        return out

    carry_pairs = {}
    cy_src[...] = jnp.zeros_like(cy_src)

    def send_carry(e, pre, reverse):
        row = 0 if reverse else SUBS - 1
        for g in range(ng):
            for part in range(2):
                at = part * ng + g
                cy_src[e, at : at + 1, :] = pre[g][part][row : row + 1, :]
        cy_buf[e, b] = cy_src[e]
        carry_pairs[e] = to_blk(
            lambda p: (cy_src.at[e], cy_buf.at[e, b]), cy_buf.at[e, 0 : nb - 1]
        )

    def carry_row(e, p, part):
        rows = range(part * ng, (part + 1) * ng)
        return jnp.concatenate([cy_buf[e, p, at : at + 1, :] for at in rows], axis=1)

    def take_carry(e, pre, layer, way, reverse, sign):
        take(cy_buf.at[e, 0 : nb - 1], carry_pairs[e][1])
        ar, ai = par[layer, 6:7, :], sign * par[layer, 7:8, :]
        zero = jnp.zeros((1, states), F32)
        cr, ci, er, ei = zero, zero, zero, zero
        for p in reversed(range(nb)) if reverse else range(nb):
            er, ei = jnp.where(b == p, cr, er), jnp.where(b == p, ci, ei)
            tr, ti = cmul(ar, ai, cr, ci)
            keep = whole_chunk[way][p]
            cr = carry_row(e, p, 0) + keep * tr
            ci = carry_row(e, p, 1) + keep * ti
        shift = SUBS - 1 if reverse else 1
        first = sub_index == (SUBS - 1 if reverse else 0)
        carry_r, carry_i = [], []
        for g in range(ng):
            cols = slice(g * LANES, (g + 1) * LANES)
            wr = jnp.broadcast_to(er[:, cols], (SUBS, LANES))
            wi = jnp.broadcast_to(ei[:, cols], (SUBS, LANES))
            sr, si, dr, di = (pltpu.roll(v, shift, 0) for v in pre[g])
            tr, ti = cmul(dr, di, wr, wi)
            carry_r.append(jnp.where(first, wr, sr + tr))
            carry_i.append(jnp.where(first, wi, si + ti))
        return tuple(carry_r + carry_i)

    def forward_states(layer, carry, way, reverse, lam):
        scale = [[wide(layer, 2 + part, g) for g in range(ng)] for part in range(2)]
        src, dst = raw.at[layer], xs.at[layer]

        def body(i, carry):
            k = steps - 1 - i if reverse else i
            pushes = [load(src, g, k) for g in range(2 * ng)]
            _, new = recur(carry, ktab[way, k], lam, pushes)
            for g in range(ng):
                vr, vi = cmul(scale[0][g], scale[1][g], new[g], new[ng + g])
                store(dst, g, k, vr)
                store(dst, ng + g, k, vi)
            return tuple(new)

        lax.fori_loop(0, steps, body, carry, unroll=4)

    def adjoint_states(layer, carry, way, reverse, lam):
        scale = [[wide(layer, 2 + part, g) for g in range(ng)] for part in range(2)]
        zero = jnp.zeros((SUBS, LANES), F32)

        def body(i, loop):
            carry, sums = loop
            k = steps - 1 - i if reverse else i
            pushes = [load(seed, g, k) for g in range(2 * ng)]
            gated, new = recur(carry, ktab[way, k], lam, pushes)
            sums = list(sums)
            for g in range(ng):
                xr, xi = load(xs.at[layer], g, k), load(xs.at[layer], ng + g, k)
                ur, ui = load(raw.at[layer], g, k), load(raw.at[layer], ng + g, k)
                pr, pi = gated[g], gated[ng + g]
                vr, vi = new[g], new[ng + g]
                sums[g] += pr * xr + pi * xi
                sums[ng + g] += pi * xr - pr * xi
                sums[2 * ng + g] += vr * ur + vi * ui
                sums[3 * ng + g] += vi * ur - vr * ui
                store(gadj, g, k, scale[0][g] * vr + scale[1][g] * vi)
                store(gadj, ng + g, k, scale[0][g] * vi - scale[1][g] * vr)
            return tuple(new), tuple(sums)

        return lax.fori_loop(0, steps, body, (carry, (zero,) * (4 * ng)), unroll=4)[1]

    tile = 256 if tc % 256 == 0 else tc

    def to_groups(left, m, dst):
        def body(i, carry):
            rows = rows_of(i, tile)
            value = product(
                (left[0][rows, :], left[1][rows, :]), (wh[m], wl[m]), "nt"
            )
            dst[rows, :] = value
            return carry

        lax.fori_loop(0, tc // tile, body, 0)

    def from_groups(src, m, dst):
        def body(i, carry):
            rows = rows_of(i, tile)
            dst[rows, :] = product(halves(src[rows, :]), (wh[m], wl[m]), "nn")
            return carry

        lax.fori_loop(0, tc // tile, body, 0)

    def weight_grad(src, right, m, scaled):
        def body(pair, carry):
            left = src[:, pl.ds(pl.multiple_of(pair * 2 * LANES, 2 * LANES), 2 * LANES)]
            value = product(halves(left), (right[0][...], right[1][...]), "tn")
            for half in range(2):
                g = 2 * pair + half
                part = value[half * LANES : (half + 1) * LANES, :]
                if scaled:
                    part = part * jnp.where(g < ng, 2.0, -2.0)
                gl[m, rows_of(g, LANES), :] = part
            return carry

        lax.fori_loop(0, ng, body, 0)

    stats_pairs = {}

    def stats_start(i, first, second):
        for n, value in enumerate((first, second)):
            for j in range(fl):
                row = n * fl + j
                st_own[i, row : row + 1, :] = value[:, j * LANES : (j + 1) * LANES]
        take(st_sib.at[i], to_sibling(st_own.at[i], st_sib.at[i])[1])
        both = st_own[i] + st_sib[i]
        st_src[i] = both
        st_buf[i, chip] = both
        stats_pairs[i] = (new(), new())
        over_chips(lambda dev: start(st_src.at[i], st_buf.at[i, chip], stats_pairs[i], dev))
        sent.append((st_buf.at[i, 0 : nch - 1], stats_pairs[i][0]))

    def stats_end(i):
        take(st_buf.at[i, 0 : nch - 1], stats_pairs[i][1])
        st_tot[i] = jnp.sum(st_buf[i], axis=0)
        return [
            jnp.concatenate(
                [st_tot[i, n * fl + j : n * fl + j + 1, :] for j in range(fl)], axis=1
            )
            for n in range(2)
        ]

    def to_row(value):
        return jnp.sum(value, axis=0, keepdims=True)

    def eights(value):
        return jnp.sum(value.reshape(value.shape[0] // SUBS, SUBS, feats), axis=0)

    gpair = {}
    pr = psum.shape[1] // nz

    def core_rows(part):
        return rows_at(part * states, states)

    def grad_core(m):
        gpair["core", m] = to_sibling(gl.at[m, core_rows(1 - core), :], gsib.at[m])

    def grad_add(m):
        take(gsib.at[m], gpair["core", m][1])

        def body(i, carry):
            gsib[m, rows_of(i, 32), :] += gl[m, rows_at(core * states + i * 32, 32), :]
            return carry

        lax.fori_loop(0, states // 32, body, 0)

    halved = [h and nz % 2 == 0 for h in HALVED]
    grad_rows = [sb // 2 if h else sb for h in halved]
    sharers = [nz // 2 if h else nz for h in halved]

    def grad_piece(m, p, other=False):
        low = p * sb
        if halved[m]:
            low = low + (1 - z % 2 if other else z % 2) * grad_rows[m]
        return rows_at(low, grad_rows[m])

    def grad_pair(m):
        pair = (new(), new())
        for p in range(nb):
            start(gsib.at[m, grad_piece(m, p, True), :], gpr.at[m, p], pair, z_pair)
        sent.append((gpr.at[m], pair[0]))
        gpair["pair", m] = pair

    def grad_pair_add(m):
        take(gpr.at[m], gpair["pair", m][1])

        def body(i, carry):
            for p in range(nb):
                low = p * sb + (z % 2) * grad_rows[m]
                gsib[m, rows_at(low + i * 8, 8), :] += gpr[m, p, rows_of(i, 8), :]
            return carry

        lax.fori_loop(0, grad_rows[m] // 8, body, 0)

    def grad_blk(m):
        gpair["blk", m] = to_blk(
            lambda p: (gsib.at[m, grad_piece(m, p), :], gblk.at[m, b, 0 : grad_rows[m], :]),
            gblk.at[m, 0 : nb - 1, 0 : grad_rows[m], :],
        )

    def my_sharers(m, body):
        if halved[m]:
            place = z // 2

            def peer(k):
                q = (place + k) % sharers[m]
                body(q, (b, (q * 2 + z % 2) * 2 + core))

            several(sharers[m], peer)
        else:
            over_z(body)

    def grad_z(m):
        take(gblk.at[m, 0 : nb - 1, 0 : grad_rows[m], :], gpair["blk", m][1])

        def body(i, carry):
            low = b * sb + (z % 2) * grad_rows[m] if halved[m] else b * sb
            value = gsib[m, rows_at(low + i * 8, 8), :]
            for p in blk_peers:
                value += gblk[m, p, rows_of(i, 8), :]
            for j in range(fl):
                psum[m, rows_at(j * grad_rows[m] + i * 8, 8), :] = value[
                    :, j * LANES : (j + 1) * LANES
                ]
            return carry

        lax.fori_loop(0, grad_rows[m] // 8, body, 0)
        place = z // 2 if halved[m] else z
        pair = (new(), new())
        my_sharers(
            m, lambda q, dev: start(psum.at[m, rows_of(q, pr), :], gz.at[m, place], pair, dev)
        )
        sent.append((gz.at[m, 0 : sharers[m] - 1], pair[0]))
        gpair["z", m] = pair

    def grad_gather(m):
        take(gz.at[m, 0 : sharers[m] - 1], gpair["z", m][1])
        place = z // 2 if halved[m] else z
        value = psum[m, rows_of(place, pr), :]
        for q in range(sharers[m]):
            value += jnp.where(place == q, 0.0, gz[m, q])
        mine = rows_of((z % 2) * sharers[m] + place if halved[m] else z, pr)
        fin[m, core, mine, :] = value
        piece = fin.at[m, core, mine, :]
        gpair["all", m] = to_z(lambda p: (piece, piece), fin.at[m, core, 0 : (nz - 1) * pr, :])

    def grad_share(m):
        take(fin.at[m, core, 0 : (nz - 1) * pr, :], gpair["all", m][1])
        gpair["share", m] = to_sibling(fin.at[m, core], fin.at[m, core])

    stores = []

    def grad_store(m):
        take(fin.at[m, 1 - core], gpair["share", m][1])
        layer, kind = MATRICES[m]
        dst = (gin_hbm if kind == "in" else gout_hbm).at[layer]
        slot = new()
        count = grad_rows[m]
        for part in range(2):
            for h in range(sb // count):
                for j in range(fl):
                    low = h * sharers[m] * pr + j * count
                    near(
                        fin.at[m, part, low : low + count, :],
                        dst.at[part, h * count : (h + 1) * count, j * LANES : (j + 1) * LANES],
                        slot,
                    )
        stores.append((dst, slot))

    hc = tc // 2
    relay_far(0)
    split_matrix(0)
    take(s0_total, s0_pair[1])
    sums = [
        jnp.concatenate([s0_b[p][n : n + 1, :] for p in range(nb)], axis=1) for n in range(2)
    ]
    near_done(xin.at[b], h_slot)
    take(x_total, x_arrival)

    scales = []
    small_rows = GROUP * SUBS
    cot_parts = []

    for layer in range(2):
        way, reverse = layer, layer == 1
        mean = sums[0] / token_count
        rstd = lax.rsqrt(sums[1] / token_count - mean * mean + EPSILON)
        gain, bias, feed = (feature_row(row + layer) for row in (8, 10, 6))
        scales.append((rstd, gain, bias, feed))

        def normalize(i, carry, layer=layer, mean=mean, rstd=rstd, gain=gain, bias=bias):
            rows = rows_of(i, small_rows)
            if layer == 0:
                value = unpack(xin, i)
                hid[0, rows, :] = value
            else:
                value = hid[1, rows, :]
            unit = (value - mean) * rstd
            zn[layer, rows, :] = unit
            zh[layer, rows, :], zl[layer, rows, :] = halves(gain * unit + bias)
            return carry

        lax.fori_loop(0, tc // small_rows, normalize, 0)
        to_groups((zh.at[layer], zl.at[layer]), 2 * layer, raw.at[layer])
        lam = [[wide(layer, part, g) for g in range(ng)] for part in range(2)]
        power = [[wide(layer, 4 + part, g) for g in range(ng)] for part in range(2)]
        last = scan_local(raw.at[layer], lam, way, reverse)
        pre = prefix(last, power, way, reverse)
        send_carry(layer, pre, reverse)
        if layer == 0:
            fetch(3)
            relay(1)
            relay_far(1)
            split_matrix(1)
        else:
            cot_parts.append(spread_in(cot_hbm, cotb, hc, tc - hc))
            relay_far(3)
            split_matrix(3)
        carry = take_carry(layer, pre, layer, way, reverse, 1.0)
        forward_states(layer, carry, way, reverse, lam)
        if layer == 0:
            relay(2)
        from_groups(xs.at[layer], 2 * layer + 1, ybuf)

        def activate(i, carry, layer=layer, gain=gain, bias=bias, feed=feed):
            rows = rows_of(i, small_rows)
            mixed = ybuf[rows, :] + feed * (gain * zn[layer, rows, :] + bias)
            below = 0.5 * (1.0 + lax.erf(mixed * 0.7071067811865476))
            density = 0.3989422804014327 * jnp.exp(-0.5 * mixed * mixed)
            gate = 1.0 / (1.0 + jnp.exp(-mixed))
            gelu = mixed * below
            value = hid[layer, rows, :] + gelu * gate
            if layer == 0:
                hid[1, rows, :] = value
            else:
                pack(outb, i, value)
            actp[layer, rows, :] = (below + mixed * density) * gate + gelu * gate * (1.0 - gate)
            return carry[0] + eights(value), carry[1] + eights(value * value)

        zero = jnp.zeros((SUBS, feats), F32)
        parts = lax.fori_loop(0, tc // small_rows, activate, (zero, zero))
        if layer == 0:
            stats_start(0, to_row(parts[0]), to_row(parts[1]))
            cot_parts.append(spread_in(cot_hbm, cotb, 0, hc))
            relay(3)
            relay_far(2)
            split_matrix(2)
            sums = stats_end(0)

    for ref, slot in sent:
        take(ref, slot)
    sent.clear()
    gl = wf
    near_done(cotb.at[b], c_slot)
    for part in cot_parts:
        take(*part)
    outs = []
    for layer in (1, 0):
        way, reverse = 1 - layer, layer == 0
        rstd, gain, bias, feed = scales[layer]
        upper = dh.at[layer]

        def mixed_grad(i, carry, layer=layer, gain=gain, bias=bias, upper=upper):
            rows = rows_of(i, small_rows)
            value = unpack(cotb, i) if layer == 1 else upper[rows, :]
            if layer == 1:
                upper[rows, :] = value
            value = value * actp[layer, rows, :]
            dyf[rows, :] = value
            dyh[rows, :], dyl[rows, :] = halves(value)
            return carry + eights(value * (gain * zn[layer, rows, :] + bias))

        zero = jnp.zeros((SUBS, feats), F32)
        feed_grad = to_row(lax.fori_loop(0, tc // small_rows, mixed_grad, zero))
        to_groups((dyh, dyl), 2 * layer + 1, seed)
        lam = [
            [wide(layer, 0, g) for g in range(ng)],
            [-wide(layer, 1, g) for g in range(ng)],
        ]
        power = [
            [wide(layer, 4, g) for g in range(ng)],
            [-wide(layer, 5, g) for g in range(ng)],
        ]
        last = scan_local(seed, lam, way, reverse)
        pre = prefix(last, power, way, reverse)
        send_carry(2 + layer, pre, reverse)
        outs.append(spread_out(outb, out_hbm, 0 if layer == 1 else hc, hc))
        weight_grad(xs.at[layer], (dyh, dyl), 2 * layer + 1, True)
        grad_core(2 * layer + 1)
        carry = take_carry(2 + layer, pre, layer, way, reverse, -1.0)
        if layer == 0:
            grad_z(3)
        state_sums = adjoint_states(layer, carry, way, reverse, lam)
        grad_add(2 * layer + 1)
        from_groups(gadj, 2 * layer, dz)

        def dz_sums(i, carry, layer=layer, feed=feed):
            rows = rows_of(i, small_rows)
            value = dz[rows, :] + feed * dyf[rows, :]
            dz[rows, :] = value
            return carry[0] + eights(value), carry[1] + eights(value * zn[layer, rows, :])

        parts = lax.fori_loop(0, tc // small_rows, dz_sums, (zero, zero))
        stats_start(1 + layer, to_row(parts[0]), to_row(parts[1]))
        if halved[2 * layer + 1]:
            grad_pair(2 * layer + 1)
        if layer == 0:
            grad_pair_add(2)
            grad_blk(2)
        if not halved[2 * layer + 1]:
            grad_blk(2 * layer + 1)
        weight_grad(gadj, (zh.at[layer], zl.at[layer]), 2 * layer, False)
        grad_core(2 * layer)
        for p in range(nb):
            q_own[p, layer : layer + 1, :] = feed_grad[:, p * fb : (p + 1) * fb]
        for n in range(4):
            vector = jnp.concatenate(
                [to_row(state_sums[n * ng + g]) for g in range(ng)], axis=1
            )
            row = 2 + 4 * layer + n
            for p in range(nb):
                q_own[p, row : row + 1, 0:sb] = vector[:, p * sb : (p + 1) * sb]
        grad_add(2 * layer)
        if layer == 1:
            grad_pair(2)
        else:
            grad_blk(0)
            q_pair = to_sibling(q_own, q_sib)
            grad_gather(3)
            take(q_sib, q_pair[1])
            q_sib[...] += q_own[...]
            q_total = q_blk.at[0 : nb - 1]
            q_pair = to_blk(lambda p: (q_sib.at[p], q_blk.at[b]), q_total)
        bias_grad, gain_grad = stats_end(1 + layer)
        if layer == 0:
            grad_z(2)

        def hidden_grad(
            i, carry, layer=layer, rstd=rstd, gain=gain, bias_grad=bias_grad, gain_grad=gain_grad, upper=upper
        ):
            rows = rows_of(i, small_rows)
            inner = (
                dz[rows, :]
                - bias_grad / token_count
                - zn[layer, rows, :] * (gain_grad / token_count)
            )
            value = upper[rows, :] + gain * rstd * inner
            if layer == 1:
                dh[0, rows, :] = value
            else:
                pack(gxb, i, value)
            return carry

        lax.fori_loop(0, tc // small_rows, hidden_grad, 0)
        gsmall_ref[2 + layer : 3 + layer, :] = st_tot[1 + layer, pl.ds(fl + b, 1), :]
        gsmall_ref[4 + layer : 5 + layer, :] = st_tot[1 + layer, pl.ds(b, 1), :]

    if halved[1]:
        grad_pair_add(1)
        grad_blk(1)
    outs.append(spread_out(gxb, gx_hbm, 0, tc))
    grad_share(3)
    grad_gather(2)
    first, second = (0, 1) if halved[1] else (1, 0)
    grad_z(first)
    grad_store(3)
    take(q_total, q_pair[1])
    value = q_sib[b]
    for p in blk_peers:
        value += q_blk[p]
    q_z[z] = value
    q_total = q_z.at[0 : nz - 1]
    q_pair = to_z(lambda p: (q_z.at[z], q_z.at[z]), q_total)
    grad_z(second)
    grad_gather(first)
    grad_share(2)
    grad_gather(second)
    grad_store(2)
    grad_share(first)
    grad_store(first)
    take(q_total, q_pair[1])
    small = jnp.sum(q_z[...], axis=0)
    gsmall_ref[0:2, :] = small[0:2, :]
    for layer in range(2):
        real = poles_ref[layer, 0:1, :]
        imag = poles_ref[layer, 1:2, :]
        step, lr, li, fr, fi, modulus = discretize(real, imag, step_ref[layer : layer + 1, :])
        lgr, lgi, fgr, fgi = (
            small[2 + 4 * layer + n : 3 + 4 * layer + n, 0:sb] for n in range(4)
        )
        qr = (real * fgr - imag * fgi) / modulus
        qi = (real * fgi + imag * fgr) / modulus
        tr, ti = lgr + qr, lgi + qi
        wr = lr * tr + li * ti
        wi = lr * ti - li * tr
        row = 6 + 2 * layer
        gsmall_ref[row : row + 1, 0:sb] = step * wr - (fr * qr + fi * qi)
        gsmall_ref[row + 1 : row + 2, 0:sb] = step * wi - (fr * qi - fi * qr)
        gsmall_ref[10 + layer : 11 + layer, 0:sb] = step * (real * wr + imag * wi)
    for arrival, mine in outs:
        take(*arrival)
        near_done(*mine)
    grad_share(second)
    grad_store(second)
    for ref, slot in stores:
        near_done(ref, slot)
    for ref, slot in sent:
        take(ref, slot)


def finish(out_in, gx_in, gin_in, gout_in, small_in, out, gx, gpoles, gstep, gin, gout, gfeed, ggain, gbias, sem):
    pairs = ((out_in, out), (gx_in, gx), (gin_in, gin), (gout_in, gout))
    for n, (src, dst) in enumerate(pairs):
        pltpu.make_async_copy(src, dst, sem.at[n]).start()
    sb = gstep.shape[1]
    gfeed[...] = small_in[0:2, :]
    ggain[...] = small_in[2:4, :]
    gbias[...] = small_in[4:6, :]
    for layer in range(2):
        gpoles[layer] = small_in[6 + 2 * layer : 8 + 2 * layer, 0:sb]
    gstep[...] = small_in[10:12, 0:sb]
    for n, (src, dst) in enumerate(pairs):
        pltpu.make_async_copy(src, dst, sem.at[n]).wait()


def local(mesh, *args):
    inputs, seq_lengths = args[0], args[1]
    nb, nr = mesh.shape["blk"], mesh.shape["row"]
    nz = nr // 2
    tokens, fb = inputs.shape
    sb = args[2].shape[2]
    states, feats = sb * nb, fb * nb
    assert seq_lengths.shape[0] == 1 and nr % 2 == 0
    assert fb == LANES and states % LANES == 0 and 2 * feats == SUBS * LANES
    assert tokens % (nb * SUBS * SUBS) == 0 and sb % 16 == 0 and states % 64 == 0
    tc = tokens // nb
    steps = tc // SUBS
    assert steps & (steps - 1) == 0 and 2 * states <= SUBS * LANES
    nch = nb * nz
    fl = feats // LANES
    piece = -(-fl * sb // (nz * SUBS)) * SUBS
    sizes = (nb, nz, seq_lengths.shape[1], tokens, feats, states, tokens * nr)
    vmem = lambda *shape: pltpu.VMEM(shape, F32)
    half = lambda *shape: pltpu.VMEM(shape, BF16)
    scratch = [
        vmem(tokens, fb),
        vmem(16, fb),
        vmem(nb, 16, fb),
        vmem(4, 2 * states, feats),
        half(4, 2 * states, feats),
        half(4, 2 * states, feats),
        vmem(2, 8, states),
        vmem(2, steps, SUBS, LANES),
        vmem(nb, tc, fb),
        vmem(2, tc, feats),
        vmem(nb, tc, fb),
        vmem(nb, tc, fb),
        vmem(nb, tc, fb),
        vmem(2, tc, feats),
        half(2, tc, feats),
        half(2, tc, feats),
        vmem(2, tc, 2 * states),
        vmem(2, tc, 2 * states),
        vmem(tc, feats),
        vmem(2, tc, feats),
        vmem(tc, feats),
        half(tc, feats),
        half(tc, feats),
        vmem(tc, 2 * states),
        vmem(tc, 2 * states),
        vmem(tc, feats),
        vmem(2, tc, feats),
        vmem(4, states, feats),
        vmem(4, nb, sb // 2, feats),
        vmem(4, nb, sb, feats),
        vmem(4, nz * piece, LANES),
        vmem(4, nz, piece, LANES),
        vmem(4, 2, nz * piece, LANES),
        vmem(8, fb),
        vmem(8, fb),
        vmem(nz, 8, fb),
        vmem(nb, 8, fb),
        vmem(3, 8, LANES),
        vmem(3, 8, LANES),
        vmem(3, 8, LANES),
        vmem(3, nch, 8, LANES),
        vmem(3, 8, LANES),
        vmem(4, SUBS, LANES),
        vmem(4, nb, SUBS, LANES),
        vmem(nb, 16, fb),
        vmem(nb, 16, fb),
        vmem(nb, 16, fb),
        vmem(nz, 16, fb),
        pltpu.SemaphoreType.DMA((SEMAPHORES,)),
    ]
    shaped = lambda like: jax.ShapeDtypeStruct(like.shape, like.dtype)
    anywhere = pl.BlockSpec(memory_space=pl.ANY)
    fast = pl.BlockSpec(memory_space=pltpu.VMEM)
    main = pl.BlockSpec(memory_space=pltpu.HBM)
    raw = pl.pallas_call(
        functools.partial(kernel, sizes),
        name="s5_layers",
        out_shape=tuple(pltpu.VMEM(args[i].shape, F32) for i in (0, 0, 4, 5)) + (pltpu.VMEM((16, fb), F32),),
        in_specs=[
            main,
            pl.BlockSpec(memory_space=pltpu.SMEM),
            fast,
            fast,
            main,
            main,
            fast,
            fast,
            fast,
            main,
        ],
        out_specs=(anywhere,) * 4 + (fast,),
        scratch_shapes=scratch,
        compiler_params=pltpu.CompilerParams(
            collective_id=0, has_side_effects=True, vmem_limit_bytes=57 << 20
        ),
    )(*args)
    return pl.pallas_call(
        finish,
        name="results",
        out_shape=tuple(shaped(args[i]) for i in (0, 0, 2, 3, 4, 5, 6, 7, 8)),
        in_specs=[fast] * 5,
        out_specs=(anywhere, anywhere, fast, fast, anywhere, anywhere, fast, fast, fast),
        scratch_shapes=[pltpu.SemaphoreType.DMA((4,))],
        compiler_params=pltpu.CompilerParams(vmem_limit_bytes=8 << 20),
    )(*raw)


def solution(mesh):
    by_state = (P(None, None, "blk"), P(None, "blk"), P(None, None, "blk", None), P(None, None, "blk", None))
    by_feature = (P(None, "blk"),) * 3
    tokens = P("row", "blk")
    return jax.shard_map(
        functools.partial(local, mesh),
        mesh=mesh,
        in_specs=(tokens, P("row", None), *by_state, *by_feature, tokens),
        out_specs=(tokens, tokens, *by_state, *by_feature),
        check_vma=False,
    )
```

```python
import functools

import jax
import jax.numpy as jnp
from jax import lax
from jax.experimental import pallas as pl
from jax.experimental.pallas import tpu as pltpu
from jax.sharding import PartitionSpec as P


EPSILON = 1e-05
LANES = 128
SUBS = 8
GROUP = 4
MESH = pl.DeviceIdType.MESH
F32 = jnp.float32
BF16 = jnp.bfloat16
MATRICES = ((0, "in"), (0, "out"), (1, "in"), (1, "out"))
SHARED = (True, False, True, True)
HALVED = (False, True, True, False)
SEMAPHORES = 132
DIMS = {
    "nt": (((1,), (1,)), ((), ())),
    "nn": (((1,), (0,)), ((), ())),
    "tn": (((0,), (0,)), ((), ())),
}


def halves(values):
    high = values.astype(BF16)
    return high, (values - high.astype(F32)).astype(BF16)


def product(left, right, form):
    def one(a, b):
        return lax.dot_general(a, b, DIMS[form], preferred_element_type=F32)

    return one(left[0], right[0]) + (one(left[0], right[1]) + one(left[1], right[0]))


def cmul(ar, ai, br, bi):
    return ar * br - ai * bi, ar * bi + ai * br


def kernel(
    sizes,
    x_hbm,
    seq_ref,
    poles_ref,
    step_ref,
    in_hbm,
    out_mat_hbm,
    feed_ref,
    gain_ref,
    bias_ref,
    cot_hbm,
    out_hbm,
    gx_hbm,
    gin_hbm,
    gout_hbm,
    gsmall_ref,
    xloc,
    small_src,
    small_all,
    wf,
    wh,
    wl,
    par,
    ktab,
    xin,
    hid,
    cotb,
    outb,
    gxb,
    zn,
    zh,
    zl,
    raw,
    xs,
    ybuf,
    actp,
    dyf,
    dyh,
    dyl,
    seed,
    gadj,
    dz,
    dh,
    gsib,
    gpr,
    gblk,
    psum,
    gz,
    fin,
    s0_own,
    s0_sib,
    s0_z,
    s0_b,
    st_own,
    st_sib,
    st_src,
    st_buf,
    st_tot,
    cy_src,
    cy_buf,
    q_own,
    q_sib,
    q_blk,
    q_z,
    sem,
):
    nb, nz, seqs, tokens, feats, states, token_count = sizes
    nch = nb * nz
    tc, fb, sb = tokens // nb, feats // nb, states // nb
    steps = tc // SUBS
    ng = states // LANES
    fl = feats // LANES
    b = lax.axis_index("blk")
    r = lax.axis_index("row")
    core = r % 2
    z = r // 2
    chip = b * nz + z
    sibling = (b, z * 2 + 1 - core)
    z_pair = (b, (z + 1 - 2 * (z % 2)) * 2 + core)
    if nb == 4:
        blk_peers = [b + 1 - 2 * (b % 2), b + 2 - 4 * (b // 2), 3 - b]
    else:
        blk_peers = [(b + k) % nb for k in range(1, nb)]

    def several(count, body):
        if count <= 16:
            for k in range(1, count):
                body(k)
        else:

            def step(k, carry):
                body(k)
                return carry

            lax.fori_loop(1, count, step, 0)

    def over_z(body):
        def peer(k):
            q = (z + k) % nz
            body(q, (b, q * 2 + core))

        several(nz, peer)

    def over_chips(body):
        def peer(up, over):
            body(((b + over) % nb, ((z + up) % nz) * 2 + core))

        if nch <= 16:
            for up in [*range(nz - 1, 0, -1), 0]:
                for over in range(1, nb):
                    peer(up, over)
            for up in range(1, nz):
                peer(up, 0)
        else:

            def step(k, carry):
                peer(k % nz, k // nz)
                return carry

            lax.fori_loop(1, nch, step, 0)

    barrier = pltpu.get_barrier_semaphore()
    pl.semaphore_signal(barrier, 1, device_id=sibling, device_id_type=MESH)
    over_chips(
        lambda dev: pl.semaphore_signal(barrier, 1, device_id=dev, device_id_type=MESH)
    )

    slots = iter(range(SEMAPHORES))
    sent = []

    def new():
        return next(slots)

    def start(src, dst, pair, dev):
        pltpu.make_async_remote_copy(
            src, dst, sem.at[pair[0]], sem.at[pair[1]], device_id=dev, device_id_type=MESH
        ).start()

    def take(ref, slot):
        pltpu.make_async_copy(ref, ref, sem.at[slot]).wait()

    def near(src, dst, slot):
        pltpu.make_async_copy(src, dst, sem.at[slot]).start()

    def near_done(ref, slot):
        pltpu.make_async_copy(ref, ref, sem.at[slot]).wait()

    def rows_of(i, size):
        return pl.ds(pl.multiple_of(i * size, size), size)

    def rows_at(i, size):
        return pl.ds(pl.multiple_of(i, 8), size)

    def to_sibling(src, dst, total=None):
        pair = (new(), new())
        start(src, dst, pair, sibling)
        sent.append((src, pair[0]))
        return pair

    def to_blk(make, total):
        pair = (new(), new())
        for p in blk_peers:
            start(*make(p), pair, (p, r))
        sent.append((total, pair[0]))
        return pair

    def to_z(make, total):
        pair = (new(), new())
        over_z(lambda p, dev: start(*make(p), pair, dev))
        sent.append((total, pair[0]))
        return pair

    my_cols = rows_of(b, fb)
    mats = [in_hbm if kind == "in" else out_mat_hbm for _, kind in MATRICES]
    x_slot, h_slot, c_slot = new(), new(), new()
    own_slots = [new() for _ in MATRICES]
    near(x_hbm, xloc, x_slot)
    near(x_hbm.at[rows_of(b, tc), :], xin.at[b], h_slot)
    near(cot_hbm.at[rows_of(b, tc), :], cotb.at[b], c_slot)
    for m, (layer, _) in enumerate(MATRICES):
        for part in range(2):
            near(
                mats[m].at[layer, part],
                wf.at[m, rows_at(part * states + b * sb, sb), :],
                own_slots[m],
            )

    small_src[...] = jnp.zeros_like(small_src)
    for layer in range(2):
        small_src[2 * layer : 2 * layer + 2, 0:sb] = poles_ref[layer]
    small_src[4:6, 0:sb] = step_ref[...]
    small_src[6:8, :] = feed_ref[...]
    small_src[8:10, :] = gain_ref[...]
    small_src[10:12, :] = bias_ref[...]
    small_all[b] = small_src[...]
    pl.semaphore_wait(barrier, nch)

    shared = [s and nz % 2 == 0 for s in SHARED]
    piece_rows = [sb // 2 if s else sb for s in shared]
    fetched = [wf.at[m, 0 : (nb - 1) * piece_rows[m], :] for m in range(4)]
    blk_pairs, z_pairs, near_pairs, far_pairs = {}, {}, {}, {}

    def weight_piece(m, p, other=False):
        half = (z % 2) * piece_rows[m] if shared[m] else 0
        if other:
            half = (1 - z % 2) * piece_rows[m]
        return wf.at[m, rows_at(core * states + p * sb + half, piece_rows[m]), :]

    def fetch(m):
        half = (z % 2) * piece_rows[m] if shared[m] else 0
        src = mats[m].at[MATRICES[m][0], core, rows_at(half, piece_rows[m]), :]
        blk_pairs[m] = to_blk(lambda p: (src, weight_piece(m, b)), fetched[m])

    def relay(m):
        take(fetched[m], blk_pairs[m][1])
        near_pairs[m] = (new(), new())
        if shared[m]:
            z_pairs[m] = (new(), new())
            sent.append((fetched[m], z_pairs[m][0]))
        for p in blk_peers:
            piece = weight_piece(m, p)
            if shared[m]:
                start(piece, piece, z_pairs[m], z_pair)
            start(piece, piece, near_pairs[m], sibling)
        sent.append((fetched[m], near_pairs[m][0]))

    def relay_far(m):
        if shared[m]:
            take(fetched[m], z_pairs[m][1])
            far_pairs[m] = (new(), new())
            for p in blk_peers:
                piece = weight_piece(m, p, other=True)
                start(piece, piece, far_pairs[m], sibling)
            sent.append((fetched[m], far_pairs[m][0]))

    def split_matrix(m):
        near_done(wf.at[m, 0 : 2 * sb, :], own_slots[m])
        take(fetched[m], near_pairs[m][1])
        if shared[m]:
            take(fetched[m], far_pairs[m][1])
        scaled = MATRICES[m][1] == "out"

        def body(i, carry):
            rows = rows_of(i, 64)
            values = wf[m, rows, :]
            if scaled:
                values = values * jnp.where(i * 64 < states, 2.0, -2.0)
            wh[m, rows, :], wl[m, rows, :] = halves(values)
            return carry

        lax.fori_loop(0, 2 * states // 64, body, 0)

    def spread_in(src, dst, low, count):
        total = dst.at[0 : nb - 1, low : low + count, :]
        pair = to_blk(
            lambda p: (src.at[rows_at(p * tc + low, count), :], dst.at[b, low : low + count, :]),
            total,
        )
        return total, pair[1]

    def spread_out(src, dst, low, count):
        slot = new()
        mine = dst.at[rows_at(b * tc + low, count), :]
        near(src.at[b, low : low + count, :], mine, slot)
        total = src.at[0 : nb - 1, low : low + count, :]
        pair = to_blk(lambda p: (src.at[p, low : low + count, :], mine), total)
        return (total, pair[1]), (mine, slot)

    small_total = small_all.at[0 : nb - 1]
    small_pair = to_blk(lambda p: (small_src, small_all.at[b]), small_total)
    fetch(0)
    x_total, x_arrival = spread_in(x_hbm, xin, 0, tc)
    near_done(xloc, x_slot)

    def add_rows(i, carry):
        total, square = carry
        values = xloc[rows_of(i, 64), :].reshape(8, SUBS, fb)
        return total + jnp.sum(values, axis=0), square + jnp.sum(values * values, axis=0)

    zero_tile = jnp.zeros((SUBS, fb), F32)
    total, square = lax.fori_loop(0, tokens // 64, add_rows, (zero_tile, zero_tile))
    s0_own[...] = jnp.zeros_like(s0_own)
    s0_own[0:1, :] = jnp.sum(total, axis=0, keepdims=True)
    s0_own[1:2, :] = jnp.sum(square, axis=0, keepdims=True)
    s0_pair = to_sibling(s0_own, s0_sib)
    starts = [jnp.int32(0)]
    for i in range(seqs - 1):
        starts.append(starts[-1] + seq_ref[0, i])
    begins = starts
    ends = starts[1:] + [jnp.int32(tokens)]

    def none_in(low, size, marks, shift):
        hit = None
        for mark in marks:
            at = mark - shift - low
            inside = jnp.logical_and(at >= 0, at < size)
            hit = inside if hit is None else jnp.logical_or(hit, inside)
        return jnp.where(hit, 0.0, 1.0).astype(F32)

    sub_index = lax.broadcasted_iota(jnp.int32, (SUBS, LANES), 0)
    base = b * tc
    marks = ((begins, 0), (ends, 1))

    def fill_flags(k, carry):
        for way in range(2):
            ktab[way, k] = none_in(base + sub_index * steps + k, 1, *marks[way])
        return carry

    lax.fori_loop(0, steps, fill_flags, 0)
    whole_sub = [none_in(base + sub_index * steps, steps, *marks[way]) for way in range(2)]
    whole_chunk = [[none_in(p * tc, tc, *marks[way]) for p in range(nb)] for way in range(2)]

    take(s0_sib, s0_pair[1])
    s0_z[z] = s0_own[...] + s0_sib[...]
    s0_total = s0_z.at[0 : nz - 1]
    s0_pair = to_z(lambda p: (s0_z.at[z], s0_z.at[z]), s0_total)

    take(small_total, small_pair[1])
    state_rows = jnp.concatenate([small_all[p][0:8, 0:sb] for p in range(nb)], axis=1)

    def feature_row(row):
        return jnp.concatenate([small_all[p][row : row + 1, :] for p in range(nb)], axis=1)

    def discretize(real, imag, log_step):
        step = jnp.exp(log_step)
        magnitude = jnp.exp(real * step)
        lr = magnitude * jnp.cos(imag * step)
        li = magnitude * jnp.sin(imag * step)
        modulus = real * real + imag * imag
        fr = ((lr - 1.0) * real + li * imag) / modulus
        fi = (li * real - (lr - 1.0) * imag) / modulus
        return step, lr, li, fr, fi, modulus

    for layer in range(2):
        _, lr, li, fr, fi, _ = discretize(
            state_rows[2 * layer : 2 * layer + 1, :],
            state_rows[2 * layer + 1 : 2 * layer + 2, :],
            state_rows[4 + layer : 5 + layer, :],
        )
        power = [(lr, li)]
        size = 1
        while size < tc:
            power.append(cmul(*power[-1], *power[-1]))
            size *= 2
        at_steps = power[steps.bit_length() - 1]
        for row, value in enumerate((lr, li, fr, fi, *at_steps, *power[-1])):
            par[layer, row : row + 1, :] = value

    def wide(layer, row, group):
        part = par[layer, row : row + 1, group * LANES : (group + 1) * LANES]
        return jnp.broadcast_to(part, (SUBS, LANES))

    take(s0_total, s0_pair[1])
    s0_b[b] = jnp.sum(s0_z[...], axis=0)
    s0_total = s0_b.at[0 : nb - 1]
    s0_pair = to_blk(lambda p: (s0_b.at[b], s0_b.at[b]), s0_total)
    fetch(1)
    fetch(2)
    relay(0)

    def load(ref, g, k):
        return ref[rows_of(k, SUBS), g * LANES : (g + 1) * LANES]

    def store(ref, g, k, value):
        ref[rows_of(k, SUBS), g * LANES : (g + 1) * LANES] = value

    def unpack(ref, i):
        parts = [
            jnp.concatenate(
                [ref[j, pl.ds(i * GROUP + k, SUBS, stride=steps), :] for j in range(fl)], axis=1
            )
            for k in range(GROUP)
        ]
        return jnp.concatenate(parts, axis=0)

    def pack(ref, i, value):
        for k in range(GROUP):
            for j in range(fl):
                ref[j, pl.ds(i * GROUP + k, SUBS, stride=steps), :] = value[
                    k * SUBS : (k + 1) * SUBS, j * LANES : (j + 1) * LANES
                ]

    def recur(carry, keep, lam, pushes):
        gated = [c * keep for c in carry]
        new = []
        for g in range(ng):
            vr, vi = cmul(lam[0][g], lam[1][g], gated[g], gated[ng + g])
            new.append((vr + pushes[g], vi + pushes[ng + g]))
        return gated, [v[0] for v in new] + [v[1] for v in new]

    def scan_local(src, lam, way, reverse):
        def body(i, carry):
            k = steps - 1 - i if reverse else i
            pushes = [load(src, g, k) for g in range(2 * ng)]
            return tuple(recur(carry, ktab[way, k], lam, pushes)[1])

        zero = jnp.zeros((SUBS, LANES), F32)
        return lax.fori_loop(0, steps, body, (zero,) * (2 * ng), unroll=4)

    def prefix(last, power, way, reverse):
        out = []
        for g in range(ng):
            sr, si = last[g], last[ng + g]
            ar, ai = power[0][g] * whole_sub[way], power[1][g] * whole_sub[way]
            for d in (1, 2, 4):
                shift = SUBS - d if reverse else d
                ok = sub_index < SUBS - d if reverse else sub_index >= d
                tr, ti = cmul(ar, ai, pltpu.roll(sr, shift, 0), pltpu.roll(si, shift, 0))
                br, bi = cmul(ar, ai, pltpu.roll(ar, shift, 0), pltpu.roll(ai, shift, 0))
                sr, si = jnp.where(ok, sr + tr, sr), jnp.where(ok, si + ti, si)
                ar, ai = jnp.where(ok, br, ar), jnp.where(ok, bi, ai)
            out.append((sr, si, ar, ai))
        return out

    carry_pairs = {}
    cy_src[...] = jnp.zeros_like(cy_src)

    def send_carry(e, pre, reverse):
        row = 0 if reverse else SUBS - 1
        for g in range(ng):
            for part in range(2):
                at = part * ng + g
                cy_src[e, at : at + 1, :] = pre[g][part][row : row + 1, :]
        cy_buf[e, b] = cy_src[e]
        carry_pairs[e] = to_blk(
            lambda p: (cy_src.at[e], cy_buf.at[e, b]), cy_buf.at[e, 0 : nb - 1]
        )

    def carry_row(e, p, part):
        rows = range(part * ng, (part + 1) * ng)
        return jnp.concatenate([cy_buf[e, p, at : at + 1, :] for at in rows], axis=1)

    def take_carry(e, pre, layer, way, reverse, sign):
        take(cy_buf.at[e, 0 : nb - 1], carry_pairs[e][1])
        ar, ai = par[layer, 6:7, :], sign * par[layer, 7:8, :]
        zero = jnp.zeros((1, states), F32)
        cr, ci, er, ei = zero, zero, zero, zero
        for p in reversed(range(nb)) if reverse else range(nb):
            er, ei = jnp.where(b == p, cr, er), jnp.where(b == p, ci, ei)
            tr, ti = cmul(ar, ai, cr, ci)
            keep = whole_chunk[way][p]
            cr = carry_row(e, p, 0) + keep * tr
            ci = carry_row(e, p, 1) + keep * ti
        shift = SUBS - 1 if reverse else 1
        first = sub_index == (SUBS - 1 if reverse else 0)
        carry_r, carry_i = [], []
        for g in range(ng):
            cols = slice(g * LANES, (g + 1) * LANES)
            wr = jnp.broadcast_to(er[:, cols], (SUBS, LANES))
            wi = jnp.broadcast_to(ei[:, cols], (SUBS, LANES))
            sr, si, dr, di = (pltpu.roll(v, shift, 0) for v in pre[g])
            tr, ti = cmul(dr, di, wr, wi)
            carry_r.append(jnp.where(first, wr, sr + tr))
            carry_i.append(jnp.where(first, wi, si + ti))
        return tuple(carry_r + carry_i)

    def forward_states(layer, carry, way, reverse, lam):
        scale = [[wide(layer, 2 + part, g) for g in range(ng)] for part in range(2)]
        src, dst = raw.at[layer], xs.at[layer]

        def body(i, carry):
            k = steps - 1 - i if reverse else i
            pushes = [load(src, g, k) for g in range(2 * ng)]
            _, new = recur(carry, ktab[way, k], lam, pushes)
            for g in range(ng):
                vr, vi = cmul(scale[0][g], scale[1][g], new[g], new[ng + g])
                store(dst, g, k, vr)
                store(dst, ng + g, k, vi)
            return tuple(new)

        lax.fori_loop(0, steps, body, carry, unroll=4)

    def adjoint_states(layer, carry, way, reverse, lam):
        scale = [[wide(layer, 2 + part, g) for g in range(ng)] for part in range(2)]
        zero = jnp.zeros((SUBS, LANES), F32)

        def body(i, loop):
            carry, sums = loop
            k = steps - 1 - i if reverse else i
            pushes = [load(seed, g, k) for g in range(2 * ng)]
            gated, new = recur(carry, ktab[way, k], lam, pushes)
            sums = list(sums)
            for g in range(ng):
                xr, xi = load(xs.at[layer], g, k), load(xs.at[layer], ng + g, k)
                ur, ui = load(raw.at[layer], g, k), load(raw.at[layer], ng + g, k)
                pr, pi = gated[g], gated[ng + g]
                vr, vi = new[g], new[ng + g]
                sums[g] += pr * xr + pi * xi
                sums[ng + g] += pi * xr - pr * xi
                sums[2 * ng + g] += vr * ur + vi * ui
                sums[3 * ng + g] += vi * ur - vr * ui
                store(gadj, g, k, scale[0][g] * vr + scale[1][g] * vi)
                store(gadj, ng + g, k, scale[0][g] * vi - scale[1][g] * vr)
            return tuple(new), tuple(sums)

        return lax.fori_loop(0, steps, body, (carry, (zero,) * (4 * ng)), unroll=4)[1]

    tile = 256 if tc % 256 == 0 else tc

    def to_groups(left, m, dst):
        def body(i, carry):
            rows = rows_of(i, tile)
            value = product(
                (left[0][rows, :], left[1][rows, :]), (wh[m], wl[m]), "nt"
            )
            dst[rows, :] = value
            return carry

        lax.fori_loop(0, tc // tile, body, 0)

    def from_groups(src, m, dst):
        def body(i, carry):
            rows = rows_of(i, tile)
            dst[rows, :] = product(halves(src[rows, :]), (wh[m], wl[m]), "nn")
            return carry

        lax.fori_loop(0, tc // tile, body, 0)

    def weight_grad(src, right, m, scaled):
        def body(pair, carry):
            left = src[:, pl.ds(pl.multiple_of(pair * 2 * LANES, 2 * LANES), 2 * LANES)]
            value = product(halves(left), (right[0][...], right[1][...]), "tn")
            for half in range(2):
                g = 2 * pair + half
                part = value[half * LANES : (half + 1) * LANES, :]
                if scaled:
                    part = part * jnp.where(g < ng, 2.0, -2.0)
                gl[m, rows_of(g, LANES), :] = part
            return carry

        lax.fori_loop(0, ng, body, 0)

    stats_pairs = {}

    def stats_start(i, first, second):
        for n, value in enumerate((first, second)):
            for j in range(fl):
                row = n * fl + j
                st_own[i, row : row + 1, :] = value[:, j * LANES : (j + 1) * LANES]
        take(st_sib.at[i], to_sibling(st_own.at[i], st_sib.at[i])[1])
        both = st_own[i] + st_sib[i]
        st_src[i] = both
        st_buf[i, chip] = both
        stats_pairs[i] = (new(), new())
        over_chips(lambda dev: start(st_src.at[i], st_buf.at[i, chip], stats_pairs[i], dev))
        sent.append((st_buf.at[i, 0 : nch - 1], stats_pairs[i][0]))

    def stats_end(i):
        take(st_buf.at[i, 0 : nch - 1], stats_pairs[i][1])
        st_tot[i] = jnp.sum(st_buf[i], axis=0)
        return [
            jnp.concatenate(
                [st_tot[i, n * fl + j : n * fl + j + 1, :] for j in range(fl)], axis=1
            )
            for n in range(2)
        ]

    def to_row(value):
        return jnp.sum(value, axis=0, keepdims=True)

    def eights(value):
        return jnp.sum(value.reshape(value.shape[0] // SUBS, SUBS, feats), axis=0)

    gpair = {}
    pr = psum.shape[1] // nz

    def core_rows(part):
        return rows_at(part * states, states)

    def grad_core(m):
        gpair["core", m] = to_sibling(gl.at[m, core_rows(1 - core), :], gsib.at[m])

    def grad_add(m):
        take(gsib.at[m], gpair["core", m][1])

        def body(i, carry):
            gsib[m, rows_of(i, 32), :] += gl[m, rows_at(core * states + i * 32, 32), :]
            return carry

        lax.fori_loop(0, states // 32, body, 0)

    halved = [h and nz % 2 == 0 for h in HALVED]
    grad_rows = [sb // 2 if h else sb for h in halved]
    sharers = [nz // 2 if h else nz for h in halved]

    def grad_piece(m, p, other=False):
        low = p * sb
        if halved[m]:
            low = low + (1 - z % 2 if other else z % 2) * grad_rows[m]
        return rows_at(low, grad_rows[m])

    def grad_pair(m):
        pair = (new(), new())
        for p in range(nb):
            start(gsib.at[m, grad_piece(m, p, True), :], gpr.at[m, p], pair, z_pair)
        sent.append((gpr.at[m], pair[0]))
        gpair["pair", m] = pair

    def grad_pair_add(m):
        take(gpr.at[m], gpair["pair", m][1])

        def body(i, carry):
            for p in range(nb):
                low = p * sb + (z % 2) * grad_rows[m]
                gsib[m, rows_at(low + i * 8, 8), :] += gpr[m, p, rows_of(i, 8), :]
            return carry

        lax.fori_loop(0, grad_rows[m] // 8, body, 0)

    def grad_blk(m):
        gpair["blk", m] = to_blk(
            lambda p: (gsib.at[m, grad_piece(m, p), :], gblk.at[m, b, 0 : grad_rows[m], :]),
            gblk.at[m, 0 : nb - 1, 0 : grad_rows[m], :],
        )

    def my_sharers(m, body):
        if halved[m]:
            place = z // 2

            def peer(k):
                q = (place + k) % sharers[m]
                body(q, (b, (q * 2 + z % 2) * 2 + core))

            several(sharers[m], peer)
        else:
            over_z(body)

    def grad_z(m):
        take(gblk.at[m, 0 : nb - 1, 0 : grad_rows[m], :], gpair["blk", m][1])

        def body(i, carry):
            low = b * sb + (z % 2) * grad_rows[m] if halved[m] else b * sb
            value = gsib[m, rows_at(low + i * 8, 8), :]
            for p in blk_peers:
                value += gblk[m, p, rows_of(i, 8), :]
            for j in range(fl):
                psum[m, rows_at(j * grad_rows[m] + i * 8, 8), :] = value[
                    :, j * LANES : (j + 1) * LANES
                ]
            return carry

        lax.fori_loop(0, grad_rows[m] // 8, body, 0)
        place = z // 2 if halved[m] else z
        pair = (new(), new())
        my_sharers(
            m, lambda q, dev: start(psum.at[m, rows_of(q, pr), :], gz.at[m, place], pair, dev)
        )
        sent.append((gz.at[m, 0 : sharers[m] - 1], pair[0]))
        gpair["z", m] = pair

    def grad_gather(m):
        take(gz.at[m, 0 : sharers[m] - 1], gpair["z", m][1])
        place = z // 2 if halved[m] else z
        value = psum[m, rows_of(place, pr), :]
        for q in range(sharers[m]):
            value += jnp.where(place == q, 0.0, gz[m, q])
        mine = rows_of((z % 2) * sharers[m] + place if halved[m] else z, pr)
        fin[m, core, mine, :] = value
        piece = fin.at[m, core, mine, :]
        gpair["all", m] = to_z(lambda p: (piece, piece), fin.at[m, core, 0 : (nz - 1) * pr, :])

    def grad_share(m):
        take(fin.at[m, core, 0 : (nz - 1) * pr, :], gpair["all", m][1])
        gpair["share", m] = to_sibling(fin.at[m, core], fin.at[m, core])

    stores = []

    def grad_store(m):
        take(fin.at[m, 1 - core], gpair["share", m][1])
        layer, kind = MATRICES[m]
        dst = (gin_hbm if kind == "in" else gout_hbm).at[layer]
        slot = new()
        count = grad_rows[m]
        for part in range(2):
            for h in range(sb // count):
                for j in range(fl):
                    low = h * sharers[m] * pr + j * count
                    near(
                        fin.at[m, part, low : low + count, :],
                        dst.at[part, h * count : (h + 1) * count, j * LANES : (j + 1) * LANES],
                        slot,
                    )
        stores.append((dst, slot))

    hc = tc // 2
    relay_far(0)
    split_matrix(0)
    take(s0_total, s0_pair[1])
    sums = [
        jnp.concatenate([s0_b[p][n : n + 1, :] for p in range(nb)], axis=1) for n in range(2)
    ]
    near_done(xin.at[b], h_slot)
    take(x_total, x_arrival)

    scales = []
    small_rows = GROUP * SUBS
    cot_parts = []

    for layer in range(2):
        way, reverse = layer, layer == 1
        mean = sums[0] / token_count
        rstd = lax.rsqrt(sums[1] / token_count - mean * mean + EPSILON)
        gain, bias, feed = (feature_row(row + layer) for row in (8, 10, 6))
        scales.append((rstd, gain, bias, feed))

        def normalize(i, carry, layer=layer, mean=mean, rstd=rstd, gain=gain, bias=bias):
            rows = rows_of(i, small_rows)
            if layer == 0:
                value = unpack(xin, i)
                hid[0, rows, :] = value
            else:
                value = hid[1, rows, :]
            unit = (value - mean) * rstd
            zn[layer, rows, :] = unit
            zh[layer, rows, :], zl[layer, rows, :] = halves(gain * unit + bias)
            return carry

        lax.fori_loop(0, tc // small_rows, normalize, 0)
        to_groups((zh.at[layer], zl.at[layer]), 2 * layer, raw.at[layer])
        lam = [[wide(layer, part, g) for g in range(ng)] for part in range(2)]
        power = [[wide(layer, 4 + part, g) for g in range(ng)] for part in range(2)]
        last = scan_local(raw.at[layer], lam, way, reverse)
        pre = prefix(last, power, way, reverse)
        send_carry(layer, pre, reverse)
        if layer == 0:
            fetch(3)
            relay(1)
            relay_far(1)
            split_matrix(1)
        else:
            cot_parts.append(spread_in(cot_hbm, cotb, hc, tc - hc))
            relay_far(3)
            split_matrix(3)
        carry = take_carry(layer, pre, layer, way, reverse, 1.0)
        forward_states(layer, carry, way, reverse, lam)
        if layer == 0:
            relay(2)
        from_groups(xs.at[layer], 2 * layer + 1, ybuf)

        def activate(i, carry, layer=layer, gain=gain, bias=bias, feed=feed):
            rows = rows_of(i, small_rows)
            mixed = ybuf[rows, :] + feed * (gain * zn[layer, rows, :] + bias)
            below = 0.5 * (1.0 + lax.erf(mixed * 0.7071067811865476))
            density = 0.3989422804014327 * jnp.exp(-0.5 * mixed * mixed)
            gate = 1.0 / (1.0 + jnp.exp(-mixed))
            gelu = mixed * below
            value = hid[layer, rows, :] + gelu * gate
            if layer == 0:
                hid[1, rows, :] = value
            else:
                pack(outb, i, value)
            actp[layer, rows, :] = (below + mixed * density) * gate + gelu * gate * (1.0 - gate)
            return carry[0] + eights(value), carry[1] + eights(value * value)

        zero = jnp.zeros((SUBS, feats), F32)
        parts = lax.fori_loop(0, tc // small_rows, activate, (zero, zero))
        if layer == 0:
            stats_start(0, to_row(parts[0]), to_row(parts[1]))
            cot_parts.append(spread_in(cot_hbm, cotb, 0, hc))
            relay(3)
            relay_far(2)
            split_matrix(2)
            sums = stats_end(0)

    for ref, slot in sent:
        take(ref, slot)
    sent.clear()
    gl = wf
    near_done(cotb.at[b], c_slot)
    for part in cot_parts:
        take(*part)
    outs = []
    for layer in (1, 0):
        way, reverse = 1 - layer, layer == 0
        rstd, gain, bias, feed = scales[layer]
        upper = dh.at[layer]

        def mixed_grad(i, carry, layer=layer, gain=gain, bias=bias, upper=upper):
            rows = rows_of(i, small_rows)
            value = unpack(cotb, i) if layer == 1 else upper[rows, :]
            if layer == 1:
                upper[rows, :] = value
            value = value * actp[layer, rows, :]
            dyf[rows, :] = value
            dyh[rows, :], dyl[rows, :] = halves(value)
            return carry + eights(value * (gain * zn[layer, rows, :] + bias))

        zero = jnp.zeros((SUBS, feats), F32)
        feed_grad = to_row(lax.fori_loop(0, tc // small_rows, mixed_grad, zero))
        to_groups((dyh, dyl), 2 * layer + 1, seed)
        lam = [
            [wide(layer, 0, g) for g in range(ng)],
            [-wide(layer, 1, g) for g in range(ng)],
        ]
        power = [
            [wide(layer, 4, g) for g in range(ng)],
            [-wide(layer, 5, g) for g in range(ng)],
        ]
        last = scan_local(seed, lam, way, reverse)
        pre = prefix(last, power, way, reverse)
        send_carry(2 + layer, pre, reverse)
        outs.append(spread_out(outb, out_hbm, 0 if layer == 1 else hc, hc))
        weight_grad(xs.at[layer], (dyh, dyl), 2 * layer + 1, True)
        grad_core(2 * layer + 1)
        carry = take_carry(2 + layer, pre, layer, way, reverse, -1.0)
        if layer == 0:
            grad_z(3)
        state_sums = adjoint_states(layer, carry, way, reverse, lam)
        grad_add(2 * layer + 1)
        from_groups(gadj, 2 * layer, dz)

        def dz_sums(i, carry, layer=layer, feed=feed):
            rows = rows_of(i, small_rows)
            value = dz[rows, :] + feed * dyf[rows, :]
            dz[rows, :] = value
            return carry[0] + eights(value), carry[1] + eights(value * zn[layer, rows, :])

        parts = lax.fori_loop(0, tc // small_rows, dz_sums, (zero, zero))
        stats_start(1 + layer, to_row(parts[0]), to_row(parts[1]))
        if halved[2 * layer + 1]:
            grad_pair(2 * layer + 1)
        if layer == 0:
            grad_pair_add(2)
            grad_blk(2)
        if not halved[2 * layer + 1]:
            grad_blk(2 * layer + 1)
        weight_grad(gadj, (zh.at[layer], zl.at[layer]), 2 * layer, False)
        grad_core(2 * layer)
        for p in range(nb):
            q_own[p, layer : layer + 1, :] = feed_grad[:, p * fb : (p + 1) * fb]
        for n in range(4):
            vector = jnp.concatenate(
                [to_row(state_sums[n * ng + g]) for g in range(ng)], axis=1
            )
            row = 2 + 4 * layer + n
            for p in range(nb):
                q_own[p, row : row + 1, 0:sb] = vector[:, p * sb : (p + 1) * sb]
        grad_add(2 * layer)
        if layer == 1:
            grad_pair(2)
        else:
            grad_blk(0)
            q_pair = to_sibling(q_own, q_sib)
            grad_gather(3)
            take(q_sib, q_pair[1])
            q_sib[...] += q_own[...]
            q_total = q_blk.at[0 : nb - 1]
            q_pair = to_blk(lambda p: (q_sib.at[p], q_blk.at[b]), q_total)
        bias_grad, gain_grad = stats_end(1 + layer)
        if layer == 0:
            grad_z(2)

        def hidden_grad(
            i, carry, layer=layer, rstd=rstd, gain=gain, bias_grad=bias_grad, gain_grad=gain_grad, upper=upper
        ):
            rows = rows_of(i, small_rows)
            inner = (
                dz[rows, :]
                - bias_grad / token_count
                - zn[layer, rows, :] * (gain_grad / token_count)
            )
            value = upper[rows, :] + gain * rstd * inner
            if layer == 1:
                dh[0, rows, :] = value
            else:
                pack(gxb, i, value)
            return carry

        lax.fori_loop(0, tc // small_rows, hidden_grad, 0)
        gsmall_ref[2 + layer : 3 + layer, :] = st_tot[1 + layer, pl.ds(fl + b, 1), :]
        gsmall_ref[4 + layer : 5 + layer, :] = st_tot[1 + layer, pl.ds(b, 1), :]

    if halved[1]:
        grad_pair_add(1)
        grad_blk(1)
    outs.append(spread_out(gxb, gx_hbm, 0, tc))
    grad_share(3)
    grad_gather(2)
    first, second = (0, 1) if halved[1] else (1, 0)
    grad_z(first)
    grad_store(3)
    take(q_total, q_pair[1])
    value = q_sib[b]
    for p in blk_peers:
        value += q_blk[p]
    q_z[z] = value
    q_total = q_z.at[0 : nz - 1]
    q_pair = to_z(lambda p: (q_z.at[z], q_z.at[z]), q_total)
    grad_z(second)
    grad_gather(first)
    grad_share(2)
    grad_gather(second)
    grad_store(2)
    grad_share(first)
    grad_store(first)
    take(q_total, q_pair[1])
    small = jnp.sum(q_z[...], axis=0)
    gsmall_ref[0:2, :] = small[0:2, :]
    for layer in range(2):
        real = poles_ref[layer, 0:1, :]
        imag = poles_ref[layer, 1:2, :]
        step, lr, li, fr, fi, modulus = discretize(real, imag, step_ref[layer : layer + 1, :])
        lgr, lgi, fgr, fgi = (
            small[2 + 4 * layer + n : 3 + 4 * layer + n, 0:sb] for n in range(4)
        )
        qr = (real * fgr - imag * fgi) / modulus
        qi = (real * fgi + imag * fgr) / modulus
        tr, ti = lgr + qr, lgi + qi
        wr = lr * tr + li * ti
        wi = lr * ti - li * tr
        row = 6 + 2 * layer
        gsmall_ref[row : row + 1, 0:sb] = step * wr - (fr * qr + fi * qi)
        gsmall_ref[row + 1 : row + 2, 0:sb] = step * wi - (fr * qi - fi * qr)
        gsmall_ref[10 + layer : 11 + layer, 0:sb] = step * (real * wr + imag * wi)
    for arrival, mine in outs:
        take(*arrival)
        near_done(*mine)
    grad_share(second)
    grad_store(second)
    for ref, slot in stores:
        near_done(ref, slot)
    for ref, slot in sent:
        take(ref, slot)


def finish(out_in, gx_in, gin_in, gout_in, small_in, out, gx, gpoles, gstep, gin, gout, gfeed, ggain, gbias, sem):
    pairs = ((out_in, out), (gx_in, gx), (gin_in, gin), (gout_in, gout))
    for n, (src, dst) in enumerate(pairs):
        pltpu.make_async_copy(src, dst, sem.at[n]).start()
    sb = gstep.shape[1]
    gfeed[...] = small_in[0:2, :]
    ggain[...] = small_in[2:4, :]
    gbias[...] = small_in[4:6, :]
    for layer in range(2):
        gpoles[layer] = small_in[6 + 2 * layer : 8 + 2 * layer, 0:sb]
    gstep[...] = small_in[10:12, 0:sb]
    for n, (src, dst) in enumerate(pairs):
        pltpu.make_async_copy(src, dst, sem.at[n]).wait()


def local(mesh, *args):
    inputs, seq_lengths = args[0], args[1]
    nb, nr = mesh.shape["blk"], mesh.shape["row"]
    nz = nr // 2
    tokens, fb = inputs.shape
    sb = args[2].shape[2]
    states, feats = sb * nb, fb * nb
    assert seq_lengths.shape[0] == 1 and nr % 2 == 0
    assert fb == LANES and states % LANES == 0 and 2 * feats == SUBS * LANES
    assert tokens % (nb * SUBS * SUBS) == 0 and sb % 16 == 0 and states % 64 == 0
    tc = tokens // nb
    steps = tc // SUBS
    assert steps & (steps - 1) == 0 and 2 * states <= SUBS * LANES
    nch = nb * nz
    fl = feats // LANES
    piece = -(-fl * sb // (nz * SUBS)) * SUBS
    sizes = (nb, nz, seq_lengths.shape[1], tokens, feats, states, tokens * nr)
    vmem = lambda *shape: pltpu.VMEM(shape, F32)
    half = lambda *shape: pltpu.VMEM(shape, BF16)
    scratch = [
        vmem(tokens, fb),
        vmem(16, fb),
        vmem(nb, 16, fb),
        vmem(4, 2 * states, feats),
        half(4, 2 * states, feats),
        half(4, 2 * states, feats),
        vmem(2, 8, states),
        vmem(2, steps, SUBS, LANES),
        vmem(nb, tc, fb),
        vmem(2, tc, feats),
        vmem(nb, tc, fb),
        vmem(nb, tc, fb),
        vmem(nb, tc, fb),
        vmem(2, tc, feats),
        half(2, tc, feats),
        half(2, tc, feats),
        vmem(2, tc, 2 * states),
        vmem(2, tc, 2 * states),
        vmem(tc, feats),
        vmem(2, tc, feats),
        vmem(tc, feats),
        half(tc, feats),
        half(tc, feats),
        vmem(tc, 2 * states),
        vmem(tc, 2 * states),
        vmem(tc, feats),
        vmem(2, tc, feats),
        vmem(4, states, feats),
        vmem(4, nb, sb // 2, feats),
        vmem(4, nb, sb, feats),
        vmem(4, nz * piece, LANES),
        vmem(4, nz, piece, LANES),
        vmem(4, 2, nz * piece, LANES),
        vmem(8, fb),
        vmem(8, fb),
        vmem(nz, 8, fb),
        vmem(nb, 8, fb),
        vmem(3, 8, LANES),
        vmem(3, 8, LANES),
        vmem(3, 8, LANES),
        vmem(3, nch, 8, LANES),
        vmem(3, 8, LANES),
        vmem(4, SUBS, LANES),
        vmem(4, nb, SUBS, LANES),
        vmem(nb, 16, fb),
        vmem(nb, 16, fb),
        vmem(nb, 16, fb),
        vmem(nz, 16, fb),
        pltpu.SemaphoreType.DMA((SEMAPHORES,)),
    ]
    shaped = lambda like: jax.ShapeDtypeStruct(like.shape, like.dtype)
    anywhere = pl.BlockSpec(memory_space=pl.ANY)
    fast = pl.BlockSpec(memory_space=pltpu.VMEM)
    main = pl.BlockSpec(memory_space=pltpu.HBM)
    raw = pl.pallas_call(
        functools.partial(kernel, sizes),
        name="s5_layers",
        out_shape=tuple(pltpu.VMEM(args[i].shape, F32) for i in (0, 0, 4, 5)) + (pltpu.VMEM((16, fb), F32),),
        in_specs=[
            main,
            pl.BlockSpec(memory_space=pltpu.SMEM),
            fast,
            fast,
            main,
            main,
            fast,
            fast,
            fast,
            main,
        ],
        out_specs=(anywhere,) * 4 + (fast,),
        scratch_shapes=scratch,
        compiler_params=pltpu.CompilerParams(
            collective_id=0, has_side_effects=True, vmem_limit_bytes=57 << 20
        ),
    )(*args)
    return pl.pallas_call(
        finish,
        name="results",
        out_shape=tuple(shaped(args[i]) for i in (0, 0, 2, 3, 4, 5, 6, 7, 8)),
        in_specs=[fast] * 5,
        out_specs=(anywhere, anywhere, fast, fast, anywhere, anywhere, fast, fast, fast),
        scratch_shapes=[pltpu.SemaphoreType.DMA((4,))],
        compiler_params=pltpu.CompilerParams(vmem_limit_bytes=8 << 20),
    )(*raw)


def solution(mesh):
    by_state = (P(None, None, "blk"), P(None, "blk"), P(None, None, "blk", None), P(None, None, "blk", None))
    by_feature = (P(None, "blk"),) * 3
    tokens = P("row", "blk")
    return jax.shard_map(
        functools.partial(local, mesh),
        mesh=mesh,
        in_specs=(tokens, P("row", None), *by_state, *by_feature, tokens),
        out_specs=(tokens, tokens, *by_state, *by_feature),
        check_vma=False,
    )
```
